32 devices in a mesh: seq: 8 (over y, x, core), tp: 4 (over z).
Axes of the slice: x: 2, y: 2, z: 4, core: 2. Of those that a mesh axis runs over, the one named last changes fastest.
Arguments:
- conv_values: bfloat16 [2048, 8192], P('seq', 'tp'), may hold values from -6 to 6
- gate_values: bfloat16 [2048, 8192], P('seq', 'tp'), may hold values from -6 to 6
- conv_maps: bfloat16 [2048, 2048], P('seq'), may hold values from -6 to 6
- step_raw: float32 [2048, 128], P('seq', 'tp'), may hold values from -8 to 13
- decay_log: float32 [128], P('tp'), may hold values from -20 to 2
- skip_gain: float32 [128], P('tp'), may hold values from 0.5 to 1.5
- values_kernel: float32 [4, 8192], P(None, 'tp'), may hold values from -3 to 3
- values_offset: float32 [8192], P('tp'), may hold values from -0.5 to 0.5
- maps_kernel: float32 [4, 2048], replicated, may hold values from -3 to 3
- maps_offset: float32 [2048], replicated, may hold values from -0.5 to 0.5
- norm_weight: float32 [8192], P('tp'), may hold values from 0.5 to 1.5
- out_weight: bfloat16 [8192, 8192], P('tp', 'seq'), may hold values from -0.0625 to 0.0625
- residual: bfloat16 [2048, 8192], P(('seq', 'tp')), may hold values from -6 to 6
Outputs:
- mixed: float32 [2048, 8192], P(('seq', 'tp'))
The draws below stay inside these ranges and needn't reach their ends.
All inputs are finite; a program needn't handle non-finite values.
Results may differ from the reference program's by a relative error of at most 0.012.
Values may be sent and summed in bfloat16 or wider, within the bound.
A program may use at most 128 MiB of HBM per device.

```python
import jax
import jax.numpy as jnp
from jax import lax

D = 8192
HEADS = 128
HEAD_DIM = 64
STATE = 128
GROUPS = 8
CONV = 4
LARGE_STEP_COUNT = 3
L_DEV = 256
DI = 8192
TOKEN_COUNT = 2048
N_TP = 4


def head_rates(key):
    random_subkeys = jax.random.split(jax.random.fold_in(key, 11), 2)
    fast_share = 0.5
    chooser = jax.random.uniform(random_subkeys[0], (HEADS,), jnp.float32)
    spread = jax.random.uniform(random_subkeys[1], (HEADS,), jnp.float32, -0.35, 0.35)
    small_step_floor = 0.35 / (TOKEN_COUNT * 0.0078)
    head_rate = jnp.where(chooser < fast_share, 3.2, small_step_floor) * jnp.exp(spread)
    return (head_rate, small_step_floor)


def draw_decay_log(key, part):
    head_rate, small_step_floor = head_rates(key)
    return jnp.log(head_rate).astype(jnp.float32)


def draw_step_raw(key, part):
    head_rate, small_step_floor = head_rates(key)
    random_subkeys = jax.random.split(jax.random.fold_in(key, 23), 2)
    expected_output = jnp.exp(jax.random.uniform(random_subkeys[0], (TOKEN_COUNT, HEADS), jnp.float32, jnp.log(0.002), jnp.log(0.02)))
    large_step_rows = jax.random.randint(random_subkeys[1], (LARGE_STEP_COUNT,), 0, TOKEN_COUNT)
    token_positions = jnp.arange(TOKEN_COUNT, dtype=jnp.int32)
    inside_large_step = jnp.any(token_positions[:, None] == large_step_rows[None, :], axis=1)
    large_step_value = 0.25 / small_step_floor
    expected_output = jnp.where(inside_large_step[:, None], large_step_value, expected_output)
    return (expected_output + jnp.log(-jnp.expm1(-expected_output))).astype(jnp.float32)


def block_levels(stream_key, extent, cuts, smallest, largest):
    def one(dim, shards_of):
        draws = jax.random.uniform(jax.random.fold_in(jax.random.fold_in(stream_key, 6), dim), (shards_of,), jnp.float32, smallest / len(cuts), largest / len(cuts))
        return jnp.repeat(jnp.exp(draws), extent[dim] // shards_of).reshape((-1,) + (1,) * (len(extent) - dim - 1))

    loudness = one(*cuts[0])
    for cut in cuts[1:]:
        loudness = loudness * one(*cut)
    return loudness


def scatter_about(key, extent, deviation, bound, cuts=(), kind=jnp.bfloat16):
    array = jax.random.normal(key, extent, jnp.float32) * deviation
    if len(cuts) > 0:
        array = block_levels(key, extent, cuts, -0.22, 0.18) * array
    return jnp.clip(array, min=-bound, max=bound).astype(kind)


def setup_inputs(seed: int = 0) -> dict:
    keys = jax.random.split(jax.random.key(seed), 14)
    return {
        "conv_values": scatter_about(keys[0], (TOKEN_COUNT, DI), 1.0, 6.0, ((0, 8), (1, 4))),
        "gate_values": scatter_about(keys[1], (TOKEN_COUNT, DI), 1.0, 6.0, ((0, 8), (1, 4))),
        "conv_maps": scatter_about(keys[2], (TOKEN_COUNT, 2 * GROUPS * STATE), 1.0, 6.0, ((0, 8),)),
        "step_raw": draw_step_raw(jax.random.fold_in(keys[13], 71), 0),
        "decay_log": draw_decay_log(jax.random.fold_in(keys[13], 71), 0),
        "skip_gain": jnp.clip(0.5 + 1.0 * jax.random.uniform(keys[5], (HEADS,), jnp.float32) ** block_levels(keys[5], (HEADS,), ((0, 4),), -0.2, 0.2), 0.5, 1.5),
        "values_kernel": scatter_about(keys[6], (CONV, DI), CONV ** -0.5, 3.0, ((1, 4),), jnp.float32),
        "values_offset": jnp.clip(jax.random.uniform(keys[7], (DI,), jnp.float32, -0.5, 0.5) * block_levels(keys[7], (DI,), ((0, 4),), -0.4, 0.0), -0.5, 0.5),
        "maps_kernel": scatter_about(keys[8], (CONV, 2 * GROUPS * STATE), CONV ** -0.5, 3.0, (), jnp.float32),
        "maps_offset": jnp.clip(jax.random.uniform(keys[9], (2 * GROUPS * STATE,), jnp.float32, -0.5, 0.5), -0.5, 0.5),
        "norm_weight": jnp.clip(0.5 + 1.0 * jax.random.uniform(keys[10], (DI,), jnp.float32) ** block_levels(keys[10], (DI,), ((0, 4),), -0.2, 0.2), 0.5, 1.5),
        "out_weight": scatter_about(keys[11], (DI, D), DI ** -0.5, 0.0625, ((0, 4), (1, 8))),
        "residual": scatter_about(keys[12], (TOKEN_COUNT, D), 1.0, 6.0, ((0, 32),)),
    }


def causal_conv(signal, weight, offset):
    length = signal.shape[0]
    padded = jnp.concatenate([jnp.zeros((CONV - 1, signal.shape[1]), jnp.float32), signal.astype(jnp.float32)], axis=0)
    summed = offset[None, :] + weight[0][None, :] * padded[0:length]
    for position in range(1, CONV):
        summed = summed + weight[position][None, :] * padded[position:position + length]
    return jax.nn.silu(summed).astype(jnp.bfloat16)

def reference(conv_values, gate_values, conv_maps, step_raw, decay_log, skip_gain, values_kernel, values_offset, maps_kernel, maps_offset, norm_weight, out_weight, residual):
    highest = lax.Precision.HIGHEST
    values_conv = causal_conv(conv_values, values_kernel, values_offset)
    maps_conv = causal_conv(conv_maps, maps_kernel, maps_offset)
    step_size = jax.nn.softplus(step_raw)
    log_decay = -jnp.exp(decay_log)[None, :] * step_size
    per_group = HEADS // GROUPS
    block_count = TOKEN_COUNT // L_DEV
    value_blocks = values_conv.astype(jnp.float32).reshape(block_count, L_DEV, HEADS, HEAD_DIM)
    input_blocks = maps_conv[:, :GROUPS * STATE].astype(jnp.float32).reshape(block_count, L_DEV, GROUPS, STATE)
    output_blocks = maps_conv[:, GROUPS * STATE:].astype(jnp.float32).reshape(block_count, L_DEV, GROUPS, STATE)
    gate_blocks = gate_values.reshape(block_count, L_DEV, DI)
    step_blocks = step_size.reshape(block_count, L_DEV, HEADS)
    decay_blocks = log_decay.reshape(block_count, L_DEV, HEADS)
    residual_blocks = residual.reshape(block_count, L_DEV, D)
    weight_split = out_weight.astype(jnp.float32).reshape(N_TP, DI // N_TP, D)
    causal = jnp.tril(jnp.ones((L_DEV, L_DEV), dtype=bool))

    def block_step(carry_state, block_items):
        block_values, block_inputs, block_outputs, block_gate, block_step_size, block_decay, block_residual = block_items
        cum_log = jnp.cumsum(block_decay, axis=0)
        input_heads = jnp.repeat(block_inputs, per_group, axis=1)
        output_heads = jnp.repeat(block_outputs, per_group, axis=1)
        group_scores = jnp.einsum('tgn,sgn->gts', block_outputs, block_inputs, precision=highest)
        scores = jnp.repeat(group_scores, per_group, axis=0)
        gap_log = cum_log.T[:, :, None] - cum_log.T[:, None, :]
        kernel = jnp.where(causal[None], jnp.exp(jnp.where(causal[None], gap_log, 0.0)), 0.0)
        mixing = kernel * scores * block_step_size.T[:, None, :]
        within = jnp.einsum('hts,shp->thp', mixing, block_values, precision=highest)
        carried = jnp.einsum('thn,hpn->thp', output_heads, carry_state, precision=highest) * jnp.exp(cum_log)[:, :, None]
        mixer_out = within + carried + skip_gain[None, :, None] * block_values
        end_weight = jnp.exp(cum_log[-1][None, :] - cum_log) * block_step_size
        new_state = jnp.exp(cum_log[-1])[:, None, None] * carry_state + jnp.einsum('shp,shn->hpn', block_values * end_weight[:, :, None], input_heads, precision=highest)
        gated_out = mixer_out * jax.nn.silu(block_gate.astype(jnp.float32)).reshape(L_DEV, HEADS, HEAD_DIM)
        grouped = gated_out.reshape(L_DEV, GROUPS, per_group * HEAD_DIM)
        inv_rms = lax.rsqrt(lax.optimization_barrier(jnp.mean(grouped * grouped, axis=2, keepdims=True)) + 1e-05)
        normed = ((grouped * inv_rms).reshape(L_DEV, DI) * norm_weight[None, :]).astype(jnp.bfloat16)
        parts = jnp.einsum('qkc,kcd->qkd', normed.astype(jnp.float32).reshape(L_DEV, N_TP, DI // N_TP), weight_split)
        rounded = lax.optimization_barrier(parts.astype(jnp.bfloat16))
        mixed_block = block_residual.astype(jnp.float32) + lax.optimization_barrier(jnp.sum(rounded.astype(jnp.float32), axis=1))
        return (new_state, mixed_block)
    start_state = jnp.zeros((HEADS, HEAD_DIM, STATE), jnp.float32)
    final_state, mixed_blocks = lax.scan(block_step, start_state, (value_blocks, input_blocks, output_blocks, gate_blocks, step_blocks, decay_blocks, residual_blocks))
    return mixed_blocks.reshape(TOKEN_COUNT, D)
```

```python
import functools

import jax
import jax.numpy as jnp
from jax import lax
from jax.experimental import pallas as pl
from jax.experimental.pallas import tpu as pltpu
from jax.sharding import PartitionSpec as P

HEADS = 128
HEAD_DIM = 64
STATE = 128
GROUPS = 8
CONV = 4


def ring_place(spot, size):
    if size % 4:
        return spot
    half = size // 2
    past = spot - half
    turned = half + (half - 2 - 2 * lax.div(past, 2)) + lax.rem(past, 2)
    return jnp.where(spot < half, spot, turned)


def mix_kernel(
    n, m, x_ref, w_ref, out_ref, gat, part, up, down,
    own_sem, gat_send, gat_recv, up_send, up_recv, down_send, down_recv, out_send, out_recv,
):
    mesh_ids = pl.DeviceIdType.MESH
    me, z = lax.axis_index("seq"), lax.axis_index("tp")
    spot = ring_place(me, n)
    right = ring_place(lax.rem(spot + 1, n), n)
    left = ring_place(lax.rem(spot + n - 1, n), n)
    half = gat.shape[2]
    depth = gat.shape[3]
    width = w_ref.shape[1]
    rows = part.shape[1] // m
    tile = min(width, 256)

    own = [
        pltpu.make_async_copy(x_ref.at[pl.ds(d * half, half)], gat.at[0, d], own_sem.at[d])
        for d in range(2)
    ]
    for copy in own:
        copy.start()

    barrier = pltpu.get_barrier_semaphore()

    def greet(step, carry):
        pl.semaphore_signal(
            barrier, inc=1, device_id=(lax.rem(me + step, n), z), device_id_type=mesh_ids
        )
        return carry

    lax.fori_loop(1, n, greet, 0)

    @pl.when(z > 0)
    def _():
        pl.semaphore_signal(barrier, inc=1, device_id=(me, z - 1), device_id_type=mesh_ids)

    @pl.when(z < m - 1)
    def _():
        pl.semaphore_signal(barrier, inc=1, device_id=(me, z + 1), device_id_type=mesh_ids)

    beside = (z > 0).astype(jnp.int32) + (z < m - 1).astype(jnp.int32)
    pl.semaphore_wait(barrier, n - 1 + beside)

    for copy in own:
        copy.wait()

    def gather_copy(step, d):
        return pltpu.make_async_remote_copy(
            src_ref=gat.at[step, d],
            dst_ref=gat.at[step + 1, d],
            send_sem=gat_send.at[step, d],
            recv_sem=gat_recv.at[step + 1, d],
            device_id=(right if d == 0 else left, z),
            device_id_type=mesh_ids,
        )

    def gather_arrival(step, d):
        return pltpu.make_async_remote_copy(
            src_ref=gat.at[step, d],
            dst_ref=gat.at[step, d],
            send_sem=gat_send.at[step, d],
            recv_sem=gat_recv.at[step, d],
            device_id=(right if d == 0 else left, z),
            device_id_type=mesh_ids,
        )

    def chain_copy(step, j, buffer, send, recv, to):
        return pltpu.make_async_remote_copy(
            src_ref=part.at[step, pl.ds(j * rows, rows)],
            dst_ref=buffer.at[step, pl.ds(j * rows, rows)],
            send_sem=send.at[step, j],
            recv_sem=recv.at[step, j],
            device_id=(me, to),
            device_id_type=mesh_ids,
        )

    def owner(step):
        there = jnp.where(z < m // 2, spot - step + n, spot + step)
        return ring_place(lax.rem(there, n), n)

    def out_copy(step, sender):
        return pltpu.make_async_remote_copy(
            src_ref=part.at[step, pl.ds(pl.multiple_of(z * rows, rows), rows)],
            dst_ref=out_ref.at[sender],
            send_sem=out_send.at[step],
            recv_sem=out_recv.at[sender],
            device_id=(owner(step), z),
            device_id_type=mesh_ids,
        )

    def added(step, j, buffer):
        span = pl.ds(j * rows, rows)
        part[step, span] = (
            part[step, span].astype(jnp.float32) + buffer[step, span].astype(jnp.float32)
        ).astype(jnp.bfloat16)

    up_lag, down_lag = z, m - 1 - z
    last_lag = jnp.maximum(up_lag, down_lag)

    def turn(tau, carry):
        @pl.when(tau < n)
        def _():
            @pl.when(tau > 0)
            def _():
                for d in range(2):
                    gather_arrival(tau, d).wait_recv()

            @pl.when(tau < n - 1)
            def _():
                for d in range(2):
                    gather_copy(tau, d).start()

            block = gat[tau].reshape(2 * half, depth)
            for c in range(0, width, tile):
                part[tau, :, c : c + tile] = jnp.dot(
                    block, w_ref[:, c : c + tile], preferred_element_type=jnp.float32
                ).astype(jnp.bfloat16)

        t_up = tau - up_lag

        @pl.when((t_up >= 0) & (t_up < n))
        def _():
            for j in range(m - 1, 0, -1):
                @pl.when(z < j)
                def _():
                    copy = chain_copy(t_up, j, up, up_send, up_recv, z + 1)

                    @pl.when(z > 0)
                    def _():
                        copy.wait_recv()
                        added(t_up, j, up)

                    copy.start()

        t_down = tau - down_lag

        @pl.when((t_down >= 0) & (t_down < n))
        def _():
            for j in range(m - 1):
                @pl.when(z > j)
                def _():
                    copy = chain_copy(t_down, j, down, down_send, down_recv, z - 1)

                    @pl.when(z < m - 1)
                    def _():
                        copy.wait_recv()
                        added(t_down, j, down)

                    copy.start()

        t_last = tau - last_lag

        @pl.when((t_last >= 0) & (t_last < n))
        def _():
            for j in range(m):
                @pl.when(z == j)
                def _():
                    span = pl.ds(j * rows, rows)
                    total = part[t_last, span].astype(jnp.float32)
                    if j > 0:
                        chain_copy(t_last, j, up, up_send, up_recv, z).wait_recv()
                        total = total + up[t_last, span].astype(jnp.float32)
                    if j < m - 1:
                        chain_copy(t_last, j, down, down_send, down_recv, z).wait_recv()
                        total = total + down[t_last, span].astype(jnp.float32)
                    part[t_last, span] = total.astype(jnp.bfloat16)

            @pl.when(t_last == 0)
            def _():
                out_ref[me] = part[0, pl.ds(pl.multiple_of(z * rows, rows), rows)]

            @pl.when(t_last > 0)
            def _():
                out_copy(t_last, me).start()

        return carry

    lax.fori_loop(0, n + m - 1, turn, 0)

    def finish(step, carry):
        @pl.when(step < n - 1)
        def _():
            for d in range(2):
                gather_copy(step, d).wait_send()

        for j in range(m):
            @pl.when(z < j)
            def _():
                chain_copy(step, j, up, up_send, up_recv, z).wait_send()

            @pl.when(z > j)
            def _():
                chain_copy(step, j, down, down_send, down_recv, z).wait_send()

        @pl.when(step > 0)
        def _():
            out_copy(step, me).wait_send()
            out_copy(step, lax.rem(me + step, n)).wait_recv()

        return carry

    lax.fori_loop(0, n, finish, 0)


def mix(normed, weight):
    n, m = lax.axis_size("seq"), lax.axis_size("tp")
    length, depth = normed.shape
    width = weight.shape[1]
    rows = length // m
    half = length // 2
    slots = pltpu.VMEM((n, length, width), jnp.bfloat16)
    dma = pltpu.SemaphoreType.DMA
    vmem = pl.BlockSpec(memory_space=pltpu.VMEM)
    return pl.pallas_call(
        functools.partial(mix_kernel, n, m),
        out_shape=jax.ShapeDtypeStruct((n, rows, width), jnp.bfloat16),
        in_specs=[pl.BlockSpec(memory_space=pl.ANY), vmem],
        out_specs=vmem,
        scratch_shapes=[
            pltpu.VMEM((n, 2, half, depth), jnp.bfloat16),
            slots,
            slots,
            slots,
            dma((2,)),
            dma((n, 2)),
            dma((n, 2)),
            dma((n, m)),
            dma((n, m)),
            dma((n, m)),
            dma((n, m)),
            dma((n,)),
            dma((n,)),
        ],
        compiler_params=pltpu.CompilerParams(
            collective_id=0, has_side_effects=True, vmem_limit_bytes=48 << 20
        ),
        cost_estimate=pl.CostEstimate(
            flops=2 * n * length * depth * width,
            bytes_accessed=2 * (depth * width + length * depth),
            transcendentals=0,
        ),
    )(normed, weight)


def front_kernel(
    n, per_group, whole_groups, x_ref, gate_ref, maps_ref, cum_ref, cum_t_ref, step_ref, step_t_ref,
    decay_ref, skip_ref, taps_ref, base_ref, map_taps_ref, map_base_ref, gain_ref, out_ref,
    rim_x, rim_maps, pad, values, y, b_maps, c_maps, scores, local, arrived, leaving,
    rim_send, rim_recv, chain_send, chain_recv,
):
    mesh_ids = pl.DeviceIdType.MESH
    exact = lax.Precision.HIGHEST
    me, z = lax.axis_index("seq"), lax.axis_index("tp")
    length, channels = x_ref.shape
    heads = cum_ref.shape[1]
    groups_here = scores.shape[0]
    first_group = lax.div(z * heads, per_group)
    tile = arrived.shape[2]
    tiles = channels // tile
    group_width = channels // groups_here
    rim = rim_x.shape[0]

    barrier = pltpu.get_barrier_semaphore()
    has_left, has_right = me > 0, me < n - 1

    @pl.when(has_left)
    def _():
        pl.semaphore_signal(barrier, inc=1, device_id=(me - 1, z), device_id_type=mesh_ids)

    @pl.when(has_right)
    def _():
        pl.semaphore_signal(barrier, inc=1, device_id=(me + 1, z), device_id_type=mesh_ids)

    pl.semaphore_wait(barrier, has_left.astype(jnp.int32) + has_right.astype(jnp.int32))

    def rim_copy(which):
        source, target = ((x_ref, rim_x), (maps_ref, rim_maps))[which]
        return pltpu.make_async_remote_copy(
            src_ref=source.at[pl.ds(length - rim, rim)],
            dst_ref=target,
            send_sem=rim_send.at[which],
            recv_sem=rim_recv.at[which],
            device_id=(me + 1, z),
            device_id_type=mesh_ids,
        )

    @pl.when(has_right)
    def _():
        for which in range(2):
            rim_copy(which).start()

    @pl.when(has_left)
    def _():
        for which in range(2):
            rim_copy(which).wait_recv()

    @pl.when(jnp.logical_not(has_left))
    def _():
        rim_x[...] = jnp.zeros_like(rim_x)
        rim_maps[...] = jnp.zeros_like(rim_maps)

    def conv(rows_ref, rim_ref, taps, base, start, size):
        span = pl.ds(start, size)
        pad[0:rim, 0:size] = rim_ref[:, span].astype(jnp.float32)
        pad[rim : rim + length, 0:size] = rows_ref[:, span].astype(jnp.float32)
        total = base[:, span]
        for k in range(CONV):
            at = rim - (CONV - 1) + k
            total = total + taps[k : k + 1, span] * pad[at : at + length, 0:size]
        return jax.nn.silu(total).astype(jnp.bfloat16)

    for g in range(groups_here):
        at = pl.multiple_of((first_group + g) * STATE, STATE)
        b_maps[g] = conv(maps_ref, rim_maps, map_taps_ref, map_base_ref, at, STATE)
        at = pl.multiple_of((GROUPS + first_group + g) * STATE, STATE)
        c_maps[g] = conv(maps_ref, rim_maps, map_taps_ref, map_base_ref, at, STATE)
        scores[g] = lax.dot_general(
            c_maps[g], b_maps[g], (((1,), (1,)), ((), ())), preferred_element_type=jnp.float32
        )

    def spread(per_head, start):
        head = lax.broadcasted_iota(jnp.int32, (heads, tile), 0) * HEAD_DIM
        lane = lax.broadcasted_iota(jnp.int32, (heads, tile), 1) + start
        chosen = ((lane >= head) & (lane < head + HEAD_DIM)).astype(jnp.float32)
        return jnp.dot(
            per_head, chosen, precision=exact, preferred_element_type=jnp.float32
        )

    cum = cum_ref[...]
    end_weight = jnp.exp(cum[length - 1 : length] - cum) * step_ref[...]
    grown = jnp.exp(cum)

    def states(c, carry):
        start = pl.multiple_of(c * tile, tile)
        span = pl.ds(start, tile)
        value = conv(x_ref, rim_x, taps_ref, base_ref, start, tile)
        values[:, span] = value
        weighted = (value.astype(jnp.float32) * spread(end_weight, start)).astype(jnp.bfloat16)
        g = lax.div(start, group_width)
        local[c] = lax.dot_general(
            b_maps[g], weighted, (((0,), (0,)), ((), ())), preferred_element_type=jnp.float32
        )
        return carry

    lax.fori_loop(0, tiles, states, 0)

    def chain_copy(c):
        return pltpu.make_async_remote_copy(
            src_ref=leaving.at[c],
            dst_ref=arrived.at[c],
            send_sem=chain_send.at[c],
            recv_sem=chain_recv.at[c],
            device_id=(me + 1, z),
            device_id_type=mesh_ids,
        )

    def link(c, carry):
        span = pl.ds(pl.multiple_of(c * tile, tile), tile)

        @pl.when(has_left)
        def _():
            chain_copy(c).wait_recv()

        @pl.when(jnp.logical_not(has_left))
        def _():
            arrived[c] = jnp.zeros_like(arrived[c])

        @pl.when(has_right)
        def _():
            leaving[c] = (
                decay_ref[:, span] * arrived[c].astype(jnp.float32) + local[c]
            ).astype(jnp.bfloat16)
            chain_copy(c).start()

        return carry

    pair = 2 * HEAD_DIM
    causal = lax.broadcasted_iota(jnp.int32, (length, length), 0) >= lax.broadcasted_iota(
        jnp.int32, (length, length), 1
    )

    def within(q, carry):
        span = pl.ds(pl.multiple_of(q * pair, pair), pair)
        value = values[:, span]
        g = lax.div(q * pair, group_width)
        sums = []
        for e in range(2):
            h = 2 * q + e
            lane = lax.broadcasted_iota(jnp.int32, (length, heads), 1)
            column = jnp.sum(jnp.where(lane == h, cum_ref[...], 0.0), axis=1, keepdims=True)
            gap = column - cum_t_ref[pl.ds(h, 1), :]
            kernel = jnp.where(causal, jnp.exp(jnp.where(causal, gap, 0.0)), 0.0)
            mixing = kernel * scores[g] * step_t_ref[pl.ds(h, 1), :]
            sums.append(
                jnp.dot(mixing.astype(jnp.bfloat16), value, preferred_element_type=jnp.float32)
            )
        first = lax.broadcasted_iota(jnp.int32, (length, pair), 1) < HEAD_DIM
        y[:, span] = jnp.where(first, sums[0], sums[1])
        return carry

    late = me >= n // 2

    def phase(turn, carry):
        @pl.when((turn == 0) == late)
        def _():
            lax.fori_loop(0, channels // pair, within, 0)

        @pl.when(turn == 0)
        def _():
            lax.fori_loop(0, tiles, link, 0)

        return carry

    lax.fori_loop(0, 2, phase, 0)

    for g in range(groups_here):
        per = group_width // tile

        def gated(c, squares):
            c = c + g * per
            start = pl.multiple_of(c * tile, tile)
            span = pl.ds(start, tile)
            carried = jnp.dot(
                c_maps[g], arrived[c], preferred_element_type=jnp.float32
            ) * spread(grown, start)
            total = y[:, span] + carried + skip_ref[:, span] * values[:, span].astype(jnp.float32)
            total = total * jax.nn.silu(gate_ref[:, span].astype(jnp.float32))
            y[:, span] = total
            return squares + jnp.sum(total * total, axis=1, keepdims=True)

        squares = lax.fori_loop(0, per, gated, jnp.zeros((length, 1), jnp.float32))
        scale = lax.rsqrt(squares / group_width + 1e-05)

        def scaled(c, carry):
            span = pl.ds(pl.multiple_of((c + g * per) * tile, tile), tile)
            if whole_groups:
                out_ref[:, span] = (y[:, span] * scale * gain_ref[:, span]).astype(out_ref.dtype)
            else:
                out_ref[:, span] = y[:, span]
            return carry

        lax.fori_loop(0, per, scaled, 0)

    @pl.when(has_right)
    def _():
        for which in range(2):
            rim_copy(which).wait_send()

        def sent(c, carry):
            chain_copy(c).wait_send()
            return carry

        lax.fori_loop(0, tiles, sent, 0)


def front(x, gate, maps, cum, step, skip, taps, base, map_taps, map_base, gain, whole_groups):
    n = lax.axis_size("seq")
    length, channels = x.shape
    heads = cum.shape[1]
    per_group = HEADS // GROUPS
    groups_here = max(1, heads // per_group)
    tile = max(128, channels // 8)
    tiles = channels // tile
    rim = 16
    bf16, f32 = jnp.bfloat16, jnp.float32
    dma = pltpu.SemaphoreType.DMA
    vmem = pl.BlockSpec(memory_space=pltpu.VMEM)
    decay = jnp.repeat(jnp.exp(cum[-1]), HEAD_DIM)[None]
    skips = jnp.repeat(skip, HEAD_DIM)[None]
    operands = (
        x, gate, maps, cum, cum.T, step, step.T, decay, skips,
        taps, base[None], map_taps, map_base[None], gain[None],
    )
    return pl.pallas_call(
        functools.partial(front_kernel, n, per_group, whole_groups),
        out_shape=jax.ShapeDtypeStruct((length, channels), bf16 if whole_groups else f32),
        in_specs=[vmem] * len(operands),
        out_specs=vmem,
        scratch_shapes=[
            pltpu.VMEM((rim, channels), bf16),
            pltpu.VMEM((rim, maps.shape[1]), bf16),
            pltpu.VMEM((rim + length, max(tile, STATE)), f32),
            pltpu.VMEM((length, channels), bf16),
            pltpu.VMEM((length, channels), f32),
            pltpu.VMEM((groups_here, length, STATE), bf16),
            pltpu.VMEM((groups_here, length, STATE), bf16),
            pltpu.VMEM((groups_here, length, length), f32),
            pltpu.VMEM((tiles, STATE, tile), f32),
            pltpu.VMEM((tiles, STATE, tile), bf16),
            pltpu.VMEM((tiles, STATE, tile), bf16),
            dma((2,)),
            dma((2,)),
            dma((tiles,)),
            dma((tiles,)),
        ],
        compiler_params=pltpu.CompilerParams(
            collective_id=1, has_side_effects=True, vmem_limit_bytes=48 << 20
        ),
    )(*operands)


LOG2E = 1.4426950408889634


def flipped(chip, mask):
    bit = 1
    while bit <= mask:
        if mask & bit:
            chip = chip + bit - 2 * bit * lax.rem(lax.div(chip, bit), 2)
        bit *= 2
    return chip


def three(value):
    high = value.astype(jnp.bfloat16)
    rest = value - high.astype(jnp.float32)
    middle = rest.astype(jnp.bfloat16)
    low = (rest - middle.astype(jnp.float32)).astype(jnp.bfloat16)
    return high, middle, low


def layer_kernel(
    n, m, per_group, x_hbm, gate_hbm, maps_hbm, step_hbm, rate_hbm, skip_hbm, taps_hbm, base_hbm,
    map_taps_hbm, map_base_hbm, gain_hbm, w_hbm, out_ref,
    x_ref, gate_ref, maps_ref, step_ref, rate_ref, skip_ref, taps_ref, base_ref, map_taps_ref,
    map_base_ref, gain_ref, w_ref, in_sem,
    rim_x, rim_maps, pad, values, y, b_maps, c_maps, scores, local, arrived, leaving,
    gap_left, gap_right, ends, growth, channel_rows, gat, part, up, down,
    rim_send, rim_recv, chain_send, chain_recv, gat_send, gat_recv,
    up_send, up_recv, down_send, down_recv, out_send, out_recv,
):
    mesh_ids = pl.DeviceIdType.MESH
    exact = lax.Precision.HIGHEST
    f32, bf16 = jnp.float32, jnp.bfloat16
    me, z = lax.axis_index("seq"), lax.axis_index("tp")
    chips = n // 2
    chip, core = lax.div(me, 2), lax.rem(me, 2)
    partner = me + 1 - 2 * core
    length, channels = x_ref.shape
    heads = step_ref.shape[1]
    groups_here = scores.shape[0]
    first_group = z * groups_here
    span_maps = groups_here * STATE
    tile = arrived.shape[2]
    tiles = channels // tile
    group_width = channels // groups_here
    rim = rim_x.shape[0]
    width = w_ref.shape[1]
    rows = length // m
    half = length // 2

    at_b = pl.ds(pl.multiple_of(first_group * STATE, STATE), span_maps)
    at_c = pl.ds(pl.multiple_of((GROUPS + first_group) * STATE, STATE), span_maps)
    to_b, to_c = pl.ds(0, span_maps), pl.ds(span_maps, span_maps)
    fetches = (
        (step_hbm, step_ref),
        (rate_hbm, rate_ref),
        (skip_hbm, skip_ref),
        (maps_hbm.at[:, at_b], maps_ref.at[:, to_b]),
        (maps_hbm.at[:, at_c], maps_ref.at[:, to_c]),
        (map_taps_hbm.at[:, at_b], map_taps_ref.at[:, to_b]),
        (map_taps_hbm.at[:, at_c], map_taps_ref.at[:, to_c]),
        (map_base_hbm.at[:, at_b], map_base_ref.at[:, to_b]),
        (map_base_hbm.at[:, at_c], map_base_ref.at[:, to_c]),
        (taps_hbm, taps_ref),
        (base_hbm, base_ref),
        (x_hbm, x_ref),
        (gain_hbm, gain_ref),
        (gate_hbm, gate_ref),
        (w_hbm, w_ref),
    )
    loads = [
        pltpu.make_async_copy(source, target, in_sem.at[i])
        for i, (source, target) in enumerate(fetches)
    ]

    barrier = pltpu.get_barrier_semaphore()

    def greet(step, carry):
        pl.semaphore_signal(
            barrier, inc=1, device_id=(lax.rem(me + step, n), z), device_id_type=mesh_ids
        )
        return carry

    lax.fori_loop(1, n, greet, 0)

    @pl.when(z > 0)
    def _():
        pl.semaphore_signal(barrier, inc=1, device_id=(me, z - 1), device_id_type=mesh_ids)

    @pl.when(z < m - 1)
    def _():
        pl.semaphore_signal(barrier, inc=1, device_id=(me, z + 1), device_id_type=mesh_ids)

    for load in loads:
        load.start()

    has_left, has_right = me > 0, me < n - 1

    for load in loads[:3]:
        load.wait()

    step = jax.nn.softplus(step_ref[...])
    log_decay = -jnp.exp(rate_ref[...]) * step
    row = lax.broadcasted_iota(jnp.int32, (length, length), 0)
    column = lax.broadcasted_iota(jnp.int32, (length, length), 1)
    lower = (row >= column).astype(f32)
    cum = jnp.dot(lower, log_decay, precision=exact, preferred_element_type=f32)
    final = cum[length - 1 : length]
    ones = jnp.ones((length, heads), bf16)
    blank = jnp.zeros((length, heads), bf16)
    gap_left[...] = jnp.concatenate(
        [*three(cum * LOG2E), ones, ones, ones, blank, blank], axis=1
    )
    source_log = jnp.log(step) * LOG2E - cum * LOG2E
    same = (row == column).astype(f32)
    source_rows = lax.dot_general(
        source_log, same, (((0,), (0,)), ((), ())), precision=exact, preferred_element_type=f32
    )
    unit = jnp.ones((heads, length), bf16)
    gap_right[...] = jnp.concatenate(
        [unit, unit, unit, *three(source_rows), unit, unit], axis=0
    )
    ends[...] = jnp.concatenate([*three(jnp.exp(final - cum) * step), blank], axis=1)
    growth[...] = jnp.concatenate([*three(jnp.exp(cum)), blank], axis=1)
    first_row = lax.broadcasted_iota(jnp.int32, (16, heads), 0) < 8
    two = jnp.where(first_row, jnp.exp(final), skip_ref[...])
    two = jnp.concatenate([*three(two), jnp.zeros((16, heads), bf16)], axis=1)

    def spread(per_head, start):
        slot = lax.broadcasted_iota(jnp.int32, (4 * heads, tile), 0)
        head = lax.rem(slot, heads) * HEAD_DIM
        lane = lax.broadcasted_iota(jnp.int32, (4 * heads, tile), 1) + start
        chosen = ((lane >= head) & (lane < head + HEAD_DIM)).astype(f32).astype(bf16)
        return jnp.dot(per_head, chosen, preferred_element_type=f32)

    def channel_row(c, carry):
        start = pl.multiple_of(c * tile, tile)
        channel_rows[:, pl.ds(start, tile)] = spread(two, start)
        return carry

    lax.fori_loop(0, tiles, channel_row, 0)

    beside = (z > 0).astype(jnp.int32) + (z < m - 1).astype(jnp.int32)
    pl.semaphore_wait(barrier, n - 1 + beside)

    def rim_copy(which):
        source, target = (
            (x_ref, rim_x),
            (maps_ref, rim_maps),
        )[which]
        return pltpu.make_async_remote_copy(
            src_ref=source.at[pl.ds(length - rim, rim)],
            dst_ref=target,
            send_sem=rim_send.at[which],
            recv_sem=rim_recv.at[which],
            device_id=(me + 1, z),
            device_id_type=mesh_ids,
        )

    for load in loads[3:12]:
        load.wait()

    @pl.when(has_right)
    def _():
        for which in range(2):
            rim_copy(which).start()

    @pl.when(has_left)
    def _():
        for which in range(2):
            rim_copy(which).wait_recv()

    @pl.when(jnp.logical_not(has_left))
    def _():
        rim_x[...] = jnp.zeros_like(rim_x)
        rim_maps[...] = jnp.zeros_like(rim_maps)

    def conv(rows_ref, rim_ref, taps, base, start, size):
        span = pl.ds(start, size)
        pad[0:rim, 0:size] = rim_ref[:, span].astype(f32)
        pad[rim : rim + length, 0:size] = rows_ref[:, span].astype(f32)
        total = base[:, span]
        for k in range(CONV):
            at = rim - (CONV - 1) + k
            total = total + taps[k : k + 1, span] * pad[at : at + length, 0:size]
        return jax.nn.silu(total).astype(bf16)

    for g in range(groups_here):
        b_maps[g] = conv(maps_ref, rim_maps, map_taps_ref, map_base_ref, g * STATE, STATE)
        c_maps[g] = conv(
            maps_ref, rim_maps, map_taps_ref, map_base_ref, span_maps + g * STATE, STATE
        )
        scores[g] = lax.dot_general(
            c_maps[g], b_maps[g], (((1,), (1,)), ((), ())), preferred_element_type=f32
        )

    def states(c, carry):
        start = pl.multiple_of(c * tile, tile)
        span = pl.ds(start, tile)
        value = conv(x_ref, rim_x, taps_ref, base_ref, start, tile)
        values[:, span] = value
        weighted = (value.astype(f32) * spread(ends[...], start)).astype(bf16)
        g = lax.div(start, group_width)
        local[c] = lax.dot_general(
            b_maps[g], weighted, (((0,), (0,)), ((), ())), preferred_element_type=f32
        )
        return carry

    lax.fori_loop(0, tiles, states, 0)

    def chain_copy(c):
        return pltpu.make_async_remote_copy(
            src_ref=leaving.at[c],
            dst_ref=arrived.at[c],
            send_sem=chain_send.at[c],
            recv_sem=chain_recv.at[c],
            device_id=(me + 1, z),
            device_id_type=mesh_ids,
        )

    def link(c, carry):
        span = pl.ds(pl.multiple_of(c * tile, tile), tile)

        @pl.when(has_left)
        def _():
            chain_copy(c).wait_recv()

        @pl.when(jnp.logical_not(has_left))
        def _():
            arrived[c] = jnp.zeros_like(arrived[c])

        @pl.when(has_right)
        def _():
            leaving[c] = (
                channel_rows[0:1, span] * arrived[c].astype(f32) + local[c]
            ).astype(bf16)
            chain_copy(c).start()

        return carry

    pair = 2 * HEAD_DIM
    causal = lax.broadcasted_iota(jnp.int32, (half, half), 0) >= lax.broadcasted_iota(
        jnp.int32, (half, half), 1
    )
    causal_late = lax.broadcasted_iota(jnp.int32, (half, length), 0) + half >= (
        lax.broadcasted_iota(jnp.int32, (half, length), 1)
    )

    def within(q, carry):
        span = pl.ds(pl.multiple_of(q * pair, pair), pair)
        g = lax.div(q * pair, group_width)
        early, late_sums = [], []
        for e in range(2):
            h = 2 * q + e
            slot = lax.broadcasted_iota(jnp.int32, (1, 8 * heads), 1)
            chosen = ((lax.rem(slot, heads) == h) & (slot < 6 * heads)).astype(f32).astype(bf16)
            gap = jnp.dot(
                gap_left[0:half] * chosen, gap_right[:, 0:half], preferred_element_type=f32
            )
            mixing = jnp.where(causal, jnp.exp2(gap), 0.0) * scores[g, 0:half, 0:half]
            early.append(
                jnp.dot(mixing.astype(bf16), values[0:half, span], preferred_element_type=f32)
            )
            gap = jnp.dot(
                gap_left[half:length] * chosen, gap_right[...], preferred_element_type=f32
            )
            mixing = jnp.where(causal_late, jnp.exp2(gap), 0.0) * scores[g, half:length, :]
            late_sums.append(
                jnp.dot(mixing.astype(bf16), values[:, span], preferred_element_type=f32)
            )
        first = lax.broadcasted_iota(jnp.int32, (half, pair), 1) < HEAD_DIM
        y[0:half, span] = jnp.where(first, early[0], early[1])
        y[half:length, span] = jnp.where(first, late_sums[0], late_sums[1])
        return carry

    late = me >= 2

    def phase(turn, carry):
        @pl.when((turn == 0) == late)
        def _():
            lax.fori_loop(0, channels // pair, within, 0)

        @pl.when(turn == 0)
        def _():
            lax.fori_loop(0, tiles, link, 0)

        return carry

    lax.fori_loop(0, 2, phase, 0)

    for load in loads[12:14]:
        load.wait()

    for g in range(groups_here):
        per = group_width // tile

        def gated(c, squares):
            c = c + g * per
            start = pl.multiple_of(c * tile, tile)
            span = pl.ds(start, tile)
            carried = jnp.dot(
                c_maps[g], arrived[c], preferred_element_type=f32
            ) * spread(growth[...], start)
            total = y[:, span] + carried + channel_rows[8:9, span] * values[:, span].astype(f32)
            total = total * jax.nn.silu(gate_ref[:, span].astype(f32))
            y[:, span] = total
            return squares + jnp.sum(total * total, axis=1, keepdims=True)

        squares = lax.fori_loop(0, per, gated, jnp.zeros((length, 1), f32))
        scale = lax.rsqrt(squares / group_width + 1e-05)

        def scaled(c, carry):
            span = pl.ds(pl.multiple_of((c + g * per) * tile, tile), tile)
            gat[0, :, span] = (y[:, span] * scale * gain_ref[:, span]).astype(bf16)
            return carry

        lax.fori_loop(0, per, scaled, 0)

    def partner_copy(slot):
        return pltpu.make_async_remote_copy(
            src_ref=gat.at[slot - 1],
            dst_ref=gat.at[slot],
            send_sem=gat_send.at[slot],
            recv_sem=gat_recv.at[slot],
            device_id=(partner, z),
            device_id_type=mesh_ids,
        )

    def across_copy(i):
        return pltpu.make_async_remote_copy(
            src_ref=gat.at[0],
            dst_ref=gat.at[2 * i],
            send_sem=gat_send.at[2 * i],
            recv_sem=gat_recv.at[2 * i],
            device_id=(2 * flipped(chip, i) + core, z),
            device_id_type=mesh_ids,
        )

    partner_copy(1).start()
    for i in range(1, chips):
        across_copy(i).start()

    def arrival(slot):
        return pltpu.make_async_remote_copy(
            src_ref=gat.at[slot],
            dst_ref=gat.at[slot],
            send_sem=gat_send.at[slot],
            recv_sem=gat_recv.at[slot],
            device_id=(partner, z),
            device_id_type=mesh_ids,
        )

    def chain_z(step, j, buffer, send, recv, to):
        return pltpu.make_async_remote_copy(
            src_ref=part.at[step, pl.ds(j * rows, rows)],
            dst_ref=buffer.at[step, pl.ds(j * rows, rows)],
            send_sem=send.at[step, j],
            recv_sem=recv.at[step, j],
            device_id=(me, to),
            device_id_type=mesh_ids,
        )

    def owner(step):
        i = lax.div(step, 2)
        there, bit = chip, 1
        while bit < chips:
            on = lax.rem(lax.div(i, bit), 2)
            there = there + on * (bit - 2 * bit * lax.rem(lax.div(chip, bit), 2))
            bit *= 2
        odd = lax.rem(step, 2)
        return 2 * there + core + odd * (1 - 2 * core)

    def columns(sender):
        return pl.ds(pl.multiple_of(sender * width, width), width)

    def own_rows():
        return pl.ds(pl.multiple_of(z * rows, rows), rows)

    def out_copy(step, sender):
        return pltpu.make_async_remote_copy(
            src_ref=part.at[step, own_rows()],
            dst_ref=out_ref.at[:, columns(sender)],
            send_sem=out_send.at[step],
            recv_sem=out_recv.at[sender],
            device_id=(owner(step), z),
            device_id_type=mesh_ids,
        )

    def added(step, j, buffer):
        span = pl.ds(j * rows, rows)
        part[step, span] = (
            part[step, span].astype(f32) + buffer[step, span].astype(f32)
        ).astype(bf16)

    up_lag, down_lag = z, m - 1 - z
    last_lag = jnp.maximum(up_lag, down_lag)
    wide = min(width, 256)

    loads[14].wait()

    def turn(tau, carry):
        @pl.when(tau < n)
        def _():
            @pl.when(tau > 0)
            def _():
                arrival(tau).wait_recv()

            @pl.when((tau > 0) & (lax.rem(tau, 2) == 0))
            def _():
                partner_copy(tau + 1).start()

            block = gat[tau]
            for c in range(0, width, wide):
                part[tau, :, c : c + wide] = jnp.dot(
                    block, w_ref[:, c : c + wide], preferred_element_type=f32
                ).astype(bf16)

        t_up = tau - up_lag

        @pl.when((t_up >= 0) & (t_up < n))
        def _():
            for j in range(m - 1, 0, -1):
                @pl.when(z < j)
                def _():
                    copy = chain_z(t_up, j, up, up_send, up_recv, z + 1)

                    @pl.when(z > 0)
                    def _():
                        copy.wait_recv()
                        added(t_up, j, up)

                    copy.start()

        t_down = tau - down_lag

        @pl.when((t_down >= 0) & (t_down < n))
        def _():
            for j in range(m - 1):
                @pl.when(z > j)
                def _():
                    copy = chain_z(t_down, j, down, down_send, down_recv, z - 1)

                    @pl.when(z < m - 1)
                    def _():
                        copy.wait_recv()
                        added(t_down, j, down)

                    copy.start()

        t_last = tau - last_lag

        @pl.when((t_last >= 0) & (t_last < n))
        def _():
            for j in range(m):
                @pl.when(z == j)
                def _():
                    span = pl.ds(j * rows, rows)
                    total = part[t_last, span].astype(f32)
                    if j > 0:
                        chain_z(t_last, j, up, up_send, up_recv, z).wait_recv()
                        total = total + up[t_last, span].astype(f32)
                    if j < m - 1:
                        chain_z(t_last, j, down, down_send, down_recv, z).wait_recv()
                        total = total + down[t_last, span].astype(f32)
                    part[t_last, span] = total.astype(bf16)

            @pl.when(t_last == 0)
            def _():
                out_ref[:, columns(me)] = part[0, own_rows()]

            @pl.when(t_last > 0)
            def _():
                out_copy(t_last, me).start()

        return carry

    lax.fori_loop(0, n + m - 1, turn, 0)

    def finish(step, carry):
        @pl.when(step > 0)
        def _():
            arrival(step).wait_send()

        for j in range(m):
            @pl.when(z < j)
            def _():
                chain_z(step, j, up, up_send, up_recv, z).wait_send()

            @pl.when(z > j)
            def _():
                chain_z(step, j, down, down_send, down_recv, z).wait_send()

        @pl.when(step > 0)
        def _():
            out_copy(step, me).wait_send()
            out_copy(step, lax.rem(me + step, n)).wait_recv()

        return carry

    lax.fori_loop(0, n, finish, 0)

    @pl.when(has_right)
    def _():
        for which in range(2):
            rim_copy(which).wait_send()

        def sent(c, carry):
            chain_copy(c).wait_send()
            return carry

        lax.fori_loop(0, tiles, sent, 0)


def layer(x, gate, maps, step_raw, rate, skip, taps, base, map_taps, map_base, gain, weight):
    n, m = lax.axis_size("seq"), lax.axis_size("tp")
    length, channels = x.shape
    heads = rate.shape[0]
    per_group = HEADS // GROUPS
    groups_here = heads // per_group
    tile = max(128, channels // 8)
    tiles = channels // tile
    width = weight.shape[1]
    span_maps = 2 * groups_here * STATE
    rim = 16
    bf16, f32 = jnp.bfloat16, jnp.float32
    dma = pltpu.SemaphoreType.DMA
    operands = (
        x, gate, maps, step_raw, rate[None], skip[None], taps, base[None],
        map_taps, map_base[None], gain[None], weight,
    )
    blocks = pltpu.VMEM((n, length, width), bf16)
    return pl.pallas_call(
        functools.partial(layer_kernel, n, m, per_group),
        out_shape=jax.ShapeDtypeStruct((length // m, n * width), bf16),
        in_specs=[pl.BlockSpec(memory_space=pl.ANY)] * len(operands),
        out_specs=pl.BlockSpec(memory_space=pltpu.VMEM),
        scratch_shapes=[
            pltpu.VMEM((length, channels), bf16),
            pltpu.VMEM((length, channels), bf16),
            pltpu.VMEM((length, span_maps), bf16),
            pltpu.VMEM((length, heads), f32),
            pltpu.VMEM((1, heads), f32),
            pltpu.VMEM((1, heads), f32),
            pltpu.VMEM((CONV, channels), f32),
            pltpu.VMEM((1, channels), f32),
            pltpu.VMEM((CONV, span_maps), f32),
            pltpu.VMEM((1, span_maps), f32),
            pltpu.VMEM((1, channels), f32),
            pltpu.VMEM(weight.shape, bf16),
            dma((15,)),
            pltpu.VMEM((rim, channels), bf16),
            pltpu.VMEM((rim, span_maps), bf16),
            pltpu.VMEM((rim + length, max(tile, STATE)), f32),
            pltpu.VMEM((length, channels), bf16),
            pltpu.VMEM((length, channels), f32),
            pltpu.VMEM((groups_here, length, STATE), bf16),
            pltpu.VMEM((groups_here, length, STATE), bf16),
            pltpu.VMEM((groups_here, length, length), f32),
            pltpu.VMEM((tiles, STATE, tile), f32),
            pltpu.VMEM((tiles, STATE, tile), bf16),
            pltpu.VMEM((tiles, STATE, tile), bf16),
            pltpu.VMEM((length, 8 * heads), bf16),
            pltpu.VMEM((8 * heads, length), bf16),
            pltpu.VMEM((length, 4 * heads), bf16),
            pltpu.VMEM((length, 4 * heads), bf16),
            pltpu.VMEM((16, channels), f32),
            pltpu.VMEM((n, length, channels), bf16),
            blocks,
            blocks,
            blocks,
            dma((2,)),
            dma((2,)),
            dma((tiles,)),
            dma((tiles,)),
            dma((n,)),
            dma((n,)),
            dma((n, m)),
            dma((n, m)),
            dma((n, m)),
            dma((n, m)),
            dma((n,)),
            dma((n,)),
        ],
        compiler_params=pltpu.CompilerParams(
            collective_id=2, has_side_effects=True, vmem_limit_bytes=52 << 20
        ),
        cost_estimate=pl.CostEstimate(
            flops=2 * n * length * channels * width,
            bytes_accessed=2 * (channels * width + 3 * length * channels),
            transcendentals=0,
        ),
    )(*operands)


def shards(
    conv_values,
    gate_values,
    conv_maps,
    step_raw,
    decay_log,
    skip_gain,
    values_kernel,
    values_offset,
    maps_kernel,
    maps_offset,
    norm_weight,
    out_weight,
    residual,
):
    length = conv_values.shape[0]
    heads_dev = decay_log.shape[0]
    per_group = HEADS // GROUPS
    whole_groups = heads_dev % per_group == 0
    chips = lax.axis_size("seq") // 2
    paired = lax.axis_size("seq") == 2 * chips and chips & (chips - 1) == 0
    if whole_groups and paired and heads_dev % 32 == 0:
        summed = layer(
            conv_values, gate_values, conv_maps, step_raw, decay_log, skip_gain, values_kernel,
            values_offset, maps_kernel, maps_offset, norm_weight, out_weight,
        )
        return residual.astype(jnp.float32) + summed.astype(jnp.float32)
    step_size = jax.nn.softplus(step_raw)
    place = jnp.arange(length, dtype=jnp.int32)
    cum_log = jnp.dot(
        (place[:, None] >= place[None, :]).astype(jnp.float32),
        -jnp.exp(decay_log)[None, :] * step_size,
        precision=lax.Precision.HIGHEST,
    )
    normed = front(
        conv_values, gate_values, conv_maps, cum_log, step_size, skip_gain, values_kernel,
        values_offset, maps_kernel, maps_offset, norm_weight, whole_groups,
    )
    if not whole_groups:
        gated_out = normed.reshape(length, heads_dev, HEAD_DIM)
        head_squares = jnp.sum(gated_out * gated_out, axis=2)
        all_heads = lax.all_gather(head_squares, "tp", axis=1, tiled=True)
        group_totals = jnp.sum(all_heads.reshape(length, GROUPS, per_group), axis=2)
        heads_here = lax.axis_index("tp") * heads_dev + jnp.arange(heads_dev, dtype=jnp.int32)
        inv_rms = lax.rsqrt(
            group_totals[:, heads_here // per_group] / (per_group * HEAD_DIM) + 1e-05
        )
        normed = (
            (gated_out * inv_rms[:, :, None]).reshape(length, heads_dev * HEAD_DIM)
            * norm_weight[None, :]
        ).astype(jnp.bfloat16)
    blocks = mix(normed, out_weight)
    summed = jnp.transpose(blocks, (1, 0, 2)).reshape(residual.shape).astype(jnp.float32)
    return residual.astype(jnp.float32) + summed


def solution(mesh):
    placed = (
        P("seq", "tp"),
        P("seq", "tp"),
        P("seq", None),
        P("seq", "tp"),
        P("tp"),
        P("tp"),
        P(None, "tp"),
        P("tp"),
        P(),
        P(),
        P("tp"),
        P("tp", "seq"),
        P(("seq", "tp"), None),
    )
    return jax.shard_map(
        shards, mesh=mesh, in_specs=placed, out_specs=P(("seq", "tp"), None), check_vma=False
    )
```

```python
import functools

import jax
import jax.numpy as jnp
from jax import lax
from jax.experimental import pallas as pl
from jax.experimental.pallas import tpu as pltpu
from jax.sharding import PartitionSpec as P

HEADS = 128
HEAD_DIM = 64
STATE = 128
GROUPS = 8
CONV = 4


def ring_place(spot, size):
    if size % 4:
        return spot
    half = size // 2
    past = spot - half
    turned = half + (half - 2 - 2 * lax.div(past, 2)) + lax.rem(past, 2)
    return jnp.where(spot < half, spot, turned)


def mix_kernel(
    n, m, x_ref, w_ref, out_ref, gat, part, up, down,
    own_sem, gat_send, gat_recv, up_send, up_recv, down_send, down_recv, out_send, out_recv,
):
    mesh_ids = pl.DeviceIdType.MESH
    me, z = lax.axis_index("seq"), lax.axis_index("tp")
    spot = ring_place(me, n)
    right = ring_place(lax.rem(spot + 1, n), n)
    left = ring_place(lax.rem(spot + n - 1, n), n)
    half = gat.shape[2]
    depth = gat.shape[3]
    width = w_ref.shape[1]
    rows = part.shape[1] // m
    tile = min(width, 256)

    own = [
        pltpu.make_async_copy(x_ref.at[pl.ds(d * half, half)], gat.at[0, d], own_sem.at[d])
        for d in range(2)
    ]
    for copy in own:
        copy.start()

    barrier = pltpu.get_barrier_semaphore()

    def greet(step, carry):
        pl.semaphore_signal(
            barrier, inc=1, device_id=(lax.rem(me + step, n), z), device_id_type=mesh_ids
        )
        return carry

    lax.fori_loop(1, n, greet, 0)

    @pl.when(z > 0)
    def _():
        pl.semaphore_signal(barrier, inc=1, device_id=(me, z - 1), device_id_type=mesh_ids)

    @pl.when(z < m - 1)
    def _():
        pl.semaphore_signal(barrier, inc=1, device_id=(me, z + 1), device_id_type=mesh_ids)

    beside = (z > 0).astype(jnp.int32) + (z < m - 1).astype(jnp.int32)
    pl.semaphore_wait(barrier, n - 1 + beside)

    for copy in own:
        copy.wait()

    def gather_copy(step, d):
        return pltpu.make_async_remote_copy(
            src_ref=gat.at[step, d],
            dst_ref=gat.at[step + 1, d],
            send_sem=gat_send.at[step, d],
            recv_sem=gat_recv.at[step + 1, d],
            device_id=(right if d == 0 else left, z),
            device_id_type=mesh_ids,
        )

    def gather_arrival(step, d):
        return pltpu.make_async_remote_copy(
            src_ref=gat.at[step, d],
            dst_ref=gat.at[step, d],
            send_sem=gat_send.at[step, d],
            recv_sem=gat_recv.at[step, d],
            device_id=(right if d == 0 else left, z),
            device_id_type=mesh_ids,
        )

    def chain_copy(step, j, buffer, send, recv, to):
        return pltpu.make_async_remote_copy(
            src_ref=part.at[step, pl.ds(j * rows, rows)],
            dst_ref=buffer.at[step, pl.ds(j * rows, rows)],
            send_sem=send.at[step, j],
            recv_sem=recv.at[step, j],
            device_id=(me, to),
            device_id_type=mesh_ids,
        )

    def owner(step):
        there = jnp.where(z < m // 2, spot - step + n, spot + step)
        return ring_place(lax.rem(there, n), n)

    def out_copy(step, sender):
        return pltpu.make_async_remote_copy(
            src_ref=part.at[step, pl.ds(pl.multiple_of(z * rows, rows), rows)],
            dst_ref=out_ref.at[sender],
            send_sem=out_send.at[step],
            recv_sem=out_recv.at[sender],
            device_id=(owner(step), z),
            device_id_type=mesh_ids,
        )

    def added(step, j, buffer):
        span = pl.ds(j * rows, rows)
        part[step, span] = (
            part[step, span].astype(jnp.float32) + buffer[step, span].astype(jnp.float32)
        ).astype(jnp.bfloat16)

    up_lag, down_lag = z, m - 1 - z
    last_lag = jnp.maximum(up_lag, down_lag)

    def turn(tau, carry):
        @pl.when(tau < n)
        def _():
            @pl.when(tau > 0)
            def _():
                for d in range(2):
                    gather_arrival(tau, d).wait_recv()

            @pl.when(tau < n - 1)
            def _():
                for d in range(2):
                    gather_copy(tau, d).start()

            block = gat[tau].reshape(2 * half, depth)
            for c in range(0, width, tile):
                part[tau, :, c : c + tile] = jnp.dot(
                    block, w_ref[:, c : c + tile], preferred_element_type=jnp.float32
                ).astype(jnp.bfloat16)

        t_up = tau - up_lag

        @pl.when((t_up >= 0) & (t_up < n))
        def _():
            for j in range(m - 1, 0, -1):
                @pl.when(z < j)
                def _():
                    copy = chain_copy(t_up, j, up, up_send, up_recv, z + 1)

                    @pl.when(z > 0)
                    def _():
                        copy.wait_recv()
                        added(t_up, j, up)

                    copy.start()

        t_down = tau - down_lag

        @pl.when((t_down >= 0) & (t_down < n))
        def _():
            for j in range(m - 1):
                @pl.when(z > j)
                def _():
                    copy = chain_copy(t_down, j, down, down_send, down_recv, z - 1)

                    @pl.when(z < m - 1)
                    def _():
                        copy.wait_recv()
                        added(t_down, j, down)

                    copy.start()

        t_last = tau - last_lag

        @pl.when((t_last >= 0) & (t_last < n))
        def _():
            for j in range(m):
                @pl.when(z == j)
                def _():
                    span = pl.ds(j * rows, rows)
                    total = part[t_last, span].astype(jnp.float32)
                    if j > 0:
                        chain_copy(t_last, j, up, up_send, up_recv, z).wait_recv()
                        total = total + up[t_last, span].astype(jnp.float32)
                    if j < m - 1:
                        chain_copy(t_last, j, down, down_send, down_recv, z).wait_recv()
                        total = total + down[t_last, span].astype(jnp.float32)
                    part[t_last, span] = total.astype(jnp.bfloat16)

            @pl.when(t_last == 0)
            def _():
                out_ref[me] = part[0, pl.ds(pl.multiple_of(z * rows, rows), rows)]

            @pl.when(t_last > 0)
            def _():
                out_copy(t_last, me).start()

        return carry

    lax.fori_loop(0, n + m - 1, turn, 0)

    def finish(step, carry):
        @pl.when(step < n - 1)
        def _():
            for d in range(2):
                gather_copy(step, d).wait_send()

        for j in range(m):
            @pl.when(z < j)
            def _():
                chain_copy(step, j, up, up_send, up_recv, z).wait_send()

            @pl.when(z > j)
            def _():
                chain_copy(step, j, down, down_send, down_recv, z).wait_send()

        @pl.when(step > 0)
        def _():
            out_copy(step, me).wait_send()
            out_copy(step, lax.rem(me + step, n)).wait_recv()

        return carry

    lax.fori_loop(0, n, finish, 0)


def mix(normed, weight):
    n, m = lax.axis_size("seq"), lax.axis_size("tp")
    length, depth = normed.shape
    width = weight.shape[1]
    rows = length // m
    half = length // 2
    slots = pltpu.VMEM((n, length, width), jnp.bfloat16)
    dma = pltpu.SemaphoreType.DMA
    vmem = pl.BlockSpec(memory_space=pltpu.VMEM)
    return pl.pallas_call(
        functools.partial(mix_kernel, n, m),
        out_shape=jax.ShapeDtypeStruct((n, rows, width), jnp.bfloat16),
        in_specs=[pl.BlockSpec(memory_space=pl.ANY), vmem],
        out_specs=vmem,
        scratch_shapes=[
            pltpu.VMEM((n, 2, half, depth), jnp.bfloat16),
            slots,
            slots,
            slots,
            dma((2,)),
            dma((n, 2)),
            dma((n, 2)),
            dma((n, m)),
            dma((n, m)),
            dma((n, m)),
            dma((n, m)),
            dma((n,)),
            dma((n,)),
        ],
        compiler_params=pltpu.CompilerParams(
            collective_id=0, has_side_effects=True, vmem_limit_bytes=48 << 20
        ),
        cost_estimate=pl.CostEstimate(
            flops=2 * n * length * depth * width,
            bytes_accessed=2 * (depth * width + length * depth),
            transcendentals=0,
        ),
    )(normed, weight)


def front_kernel(
    n, per_group, whole_groups, x_ref, gate_ref, maps_ref, cum_ref, cum_t_ref, step_ref, step_t_ref,
    decay_ref, skip_ref, taps_ref, base_ref, map_taps_ref, map_base_ref, gain_ref, out_ref,
    rim_x, rim_maps, pad, values, y, b_maps, c_maps, scores, local, arrived, leaving,
    rim_send, rim_recv, chain_send, chain_recv,
):
    mesh_ids = pl.DeviceIdType.MESH
    exact = lax.Precision.HIGHEST
    me, z = lax.axis_index("seq"), lax.axis_index("tp")
    length, channels = x_ref.shape
    heads = cum_ref.shape[1]
    groups_here = scores.shape[0]
    first_group = lax.div(z * heads, per_group)
    tile = arrived.shape[2]
    tiles = channels // tile
    group_width = channels // groups_here
    rim = rim_x.shape[0]

    barrier = pltpu.get_barrier_semaphore()
    has_left, has_right = me > 0, me < n - 1

    @pl.when(has_left)
    def _():
        pl.semaphore_signal(barrier, inc=1, device_id=(me - 1, z), device_id_type=mesh_ids)

    @pl.when(has_right)
    def _():
        pl.semaphore_signal(barrier, inc=1, device_id=(me + 1, z), device_id_type=mesh_ids)

    pl.semaphore_wait(barrier, has_left.astype(jnp.int32) + has_right.astype(jnp.int32))

    def rim_copy(which):
        source, target = ((x_ref, rim_x), (maps_ref, rim_maps))[which]
        return pltpu.make_async_remote_copy(
            src_ref=source.at[pl.ds(length - rim, rim)],
            dst_ref=target,
            send_sem=rim_send.at[which],
            recv_sem=rim_recv.at[which],
            device_id=(me + 1, z),
            device_id_type=mesh_ids,
        )

    @pl.when(has_right)
    def _():
        for which in range(2):
            rim_copy(which).start()

    @pl.when(has_left)
    def _():
        for which in range(2):
            rim_copy(which).wait_recv()

    @pl.when(jnp.logical_not(has_left))
    def _():
        rim_x[...] = jnp.zeros_like(rim_x)
        rim_maps[...] = jnp.zeros_like(rim_maps)

    def conv(rows_ref, rim_ref, taps, base, start, size):
        span = pl.ds(start, size)
        pad[0:rim, 0:size] = rim_ref[:, span].astype(jnp.float32)
        pad[rim : rim + length, 0:size] = rows_ref[:, span].astype(jnp.float32)
        total = base[:, span]
        for k in range(CONV):
            at = rim - (CONV - 1) + k
            total = total + taps[k : k + 1, span] * pad[at : at + length, 0:size]
        return jax.nn.silu(total).astype(jnp.bfloat16)

    for g in range(groups_here):
        at = pl.multiple_of((first_group + g) * STATE, STATE)
        b_maps[g] = conv(maps_ref, rim_maps, map_taps_ref, map_base_ref, at, STATE)
        at = pl.multiple_of((GROUPS + first_group + g) * STATE, STATE)
        c_maps[g] = conv(maps_ref, rim_maps, map_taps_ref, map_base_ref, at, STATE)
        scores[g] = lax.dot_general(
            c_maps[g], b_maps[g], (((1,), (1,)), ((), ())), preferred_element_type=jnp.float32
        )

    def spread(per_head, start):
        head = lax.broadcasted_iota(jnp.int32, (heads, tile), 0) * HEAD_DIM
        lane = lax.broadcasted_iota(jnp.int32, (heads, tile), 1) + start
        chosen = ((lane >= head) & (lane < head + HEAD_DIM)).astype(jnp.float32)
        return jnp.dot(
            per_head, chosen, precision=exact, preferred_element_type=jnp.float32
        )

    cum = cum_ref[...]
    end_weight = jnp.exp(cum[length - 1 : length] - cum) * step_ref[...]
    grown = jnp.exp(cum)

    def states(c, carry):
        start = pl.multiple_of(c * tile, tile)
        span = pl.ds(start, tile)
        value = conv(x_ref, rim_x, taps_ref, base_ref, start, tile)
        values[:, span] = value
        weighted = (value.astype(jnp.float32) * spread(end_weight, start)).astype(jnp.bfloat16)
        g = lax.div(start, group_width)
        local[c] = lax.dot_general(
            b_maps[g], weighted, (((0,), (0,)), ((), ())), preferred_element_type=jnp.float32
        )
        return carry

    lax.fori_loop(0, tiles, states, 0)

    def chain_copy(c):
        return pltpu.make_async_remote_copy(
            src_ref=leaving.at[c],
            dst_ref=arrived.at[c],
            send_sem=chain_send.at[c],
            recv_sem=chain_recv.at[c],
            device_id=(me + 1, z),
            device_id_type=mesh_ids,
        )

    def link(c, carry):
        span = pl.ds(pl.multiple_of(c * tile, tile), tile)

        @pl.when(has_left)
        def _():
            chain_copy(c).wait_recv()

        @pl.when(jnp.logical_not(has_left))
        def _():
            arrived[c] = jnp.zeros_like(arrived[c])

        @pl.when(has_right)
        def _():
            leaving[c] = (
                decay_ref[:, span] * arrived[c].astype(jnp.float32) + local[c]
            ).astype(jnp.bfloat16)
            chain_copy(c).start()

        return carry

    pair = 2 * HEAD_DIM
    causal = lax.broadcasted_iota(jnp.int32, (length, length), 0) >= lax.broadcasted_iota(
        jnp.int32, (length, length), 1
    )

    def within(q, carry):
        span = pl.ds(pl.multiple_of(q * pair, pair), pair)
        value = values[:, span]
        g = lax.div(q * pair, group_width)
        sums = []
        for e in range(2):
            h = 2 * q + e
            lane = lax.broadcasted_iota(jnp.int32, (length, heads), 1)
            column = jnp.sum(jnp.where(lane == h, cum_ref[...], 0.0), axis=1, keepdims=True)
            gap = column - cum_t_ref[pl.ds(h, 1), :]
            kernel = jnp.where(causal, jnp.exp(jnp.where(causal, gap, 0.0)), 0.0)
            mixing = kernel * scores[g] * step_t_ref[pl.ds(h, 1), :]
            sums.append(
                jnp.dot(mixing.astype(jnp.bfloat16), value, preferred_element_type=jnp.float32)
            )
        first = lax.broadcasted_iota(jnp.int32, (length, pair), 1) < HEAD_DIM
        y[:, span] = jnp.where(first, sums[0], sums[1])
        return carry

    late = me >= n // 2

    def phase(turn, carry):
        @pl.when((turn == 0) == late)
        def _():
            lax.fori_loop(0, channels // pair, within, 0)

        @pl.when(turn == 0)
        def _():
            lax.fori_loop(0, tiles, link, 0)

        return carry

    lax.fori_loop(0, 2, phase, 0)

    for g in range(groups_here):
        per = group_width // tile

        def gated(c, squares):
            c = c + g * per
            start = pl.multiple_of(c * tile, tile)
            span = pl.ds(start, tile)
            carried = jnp.dot(
                c_maps[g], arrived[c], preferred_element_type=jnp.float32
            ) * spread(grown, start)
            total = y[:, span] + carried + skip_ref[:, span] * values[:, span].astype(jnp.float32)
            total = total * jax.nn.silu(gate_ref[:, span].astype(jnp.float32))
            y[:, span] = total
            return squares + jnp.sum(total * total, axis=1, keepdims=True)

        squares = lax.fori_loop(0, per, gated, jnp.zeros((length, 1), jnp.float32))
        scale = lax.rsqrt(squares / group_width + 1e-05)

        def scaled(c, carry):
            span = pl.ds(pl.multiple_of((c + g * per) * tile, tile), tile)
            if whole_groups:
                out_ref[:, span] = (y[:, span] * scale * gain_ref[:, span]).astype(out_ref.dtype)
            else:
                out_ref[:, span] = y[:, span]
            return carry

        lax.fori_loop(0, per, scaled, 0)

    @pl.when(has_right)
    def _():
        for which in range(2):
            rim_copy(which).wait_send()

        def sent(c, carry):
            chain_copy(c).wait_send()
            return carry

        lax.fori_loop(0, tiles, sent, 0)


def front(x, gate, maps, cum, step, skip, taps, base, map_taps, map_base, gain, whole_groups):
    n = lax.axis_size("seq")
    length, channels = x.shape
    heads = cum.shape[1]
    per_group = HEADS // GROUPS
    groups_here = max(1, heads // per_group)
    tile = max(128, channels // 8)
    tiles = channels // tile
    rim = 16
    bf16, f32 = jnp.bfloat16, jnp.float32
    dma = pltpu.SemaphoreType.DMA
    vmem = pl.BlockSpec(memory_space=pltpu.VMEM)
    decay = jnp.repeat(jnp.exp(cum[-1]), HEAD_DIM)[None]
    skips = jnp.repeat(skip, HEAD_DIM)[None]
    operands = (
        x, gate, maps, cum, cum.T, step, step.T, decay, skips,
        taps, base[None], map_taps, map_base[None], gain[None],
    )
    return pl.pallas_call(
        functools.partial(front_kernel, n, per_group, whole_groups),
        out_shape=jax.ShapeDtypeStruct((length, channels), bf16 if whole_groups else f32),
        in_specs=[vmem] * len(operands),
        out_specs=vmem,
        scratch_shapes=[
            pltpu.VMEM((rim, channels), bf16),
            pltpu.VMEM((rim, maps.shape[1]), bf16),
            pltpu.VMEM((rim + length, max(tile, STATE)), f32),
            pltpu.VMEM((length, channels), bf16),
            pltpu.VMEM((length, channels), f32),
            pltpu.VMEM((groups_here, length, STATE), bf16),
            pltpu.VMEM((groups_here, length, STATE), bf16),
            pltpu.VMEM((groups_here, length, length), f32),
            pltpu.VMEM((tiles, STATE, tile), f32),
            pltpu.VMEM((tiles, STATE, tile), bf16),
            pltpu.VMEM((tiles, STATE, tile), bf16),
            dma((2,)),
            dma((2,)),
            dma((tiles,)),
            dma((tiles,)),
        ],
        compiler_params=pltpu.CompilerParams(
            collective_id=1, has_side_effects=True, vmem_limit_bytes=48 << 20
        ),
    )(*operands)


LOG2E = 1.4426950408889634


def three(value):
    high = value.astype(jnp.bfloat16)
    rest = value - high.astype(jnp.float32)
    middle = rest.astype(jnp.bfloat16)
    low = (rest - middle.astype(jnp.float32)).astype(jnp.bfloat16)
    return high, middle, low


def layer_kernel(
    n, m, per_group, x_hbm, gate_hbm, maps_hbm, step_hbm, rate_hbm, skip_hbm, taps_hbm, base_hbm,
    map_taps_hbm, map_base_hbm, gain_hbm, w_hbm, out_ref,
    x_ref, gate_ref, maps_ref, step_ref, rate_ref, skip_ref, taps_ref, base_ref, map_taps_ref,
    map_base_ref, gain_ref, w_ref, in_sem,
    rim_x, rim_maps, pad, values, maps_conv, y, scores, local, state, arrived, leaving,
    gap_left, gap_right, turned_maps, ends, growth, own_end, all_ends, chosen, channel_rows, prefix_rows,
    gat, part, up, down,
    rim_send, rim_recv, end_send, end_recv, chain_send, chain_recv, forward_send,
    gat_send, gat_recv, up_send, up_recv, down_send, down_recv, out_send, out_recv,
):
    mesh_ids = pl.DeviceIdType.MESH
    exact = lax.Precision.HIGHEST
    f32, bf16 = jnp.float32, jnp.bfloat16
    me, z = lax.axis_index("seq"), lax.axis_index("tp")
    chips = n // 2
    chip, core = lax.div(me, 2), lax.rem(me, 2)
    partner = me + 1 - 2 * core
    length, channels = x_ref.shape
    heads = step_ref.shape[0]
    levels = arrived.shape[0]
    groups_here = scores.shape[0]
    first_group = z * groups_here
    span_maps = groups_here * STATE
    tile = arrived.shape[3]
    tiles = channels // tile
    group_width = channels // groups_here
    rim = rim_x.shape[0]
    width = w_ref.shape[1]
    rows = length // m
    half = length // 2

    at_b = pl.ds(pl.multiple_of(first_group * STATE, STATE), span_maps)
    at_c = pl.ds(pl.multiple_of((GROUPS + first_group) * STATE, STATE), span_maps)
    to_b, to_c = pl.ds(0, span_maps), pl.ds(span_maps, span_maps)
    fetches = (
        (step_hbm, step_ref),
        (rate_hbm, rate_ref),
        (skip_hbm, skip_ref),
        (maps_hbm.at[:, at_b], maps_ref.at[:, to_b]),
        (maps_hbm.at[:, at_c], maps_ref.at[:, to_c]),
        (map_taps_hbm.at[:, at_b], map_taps_ref.at[:, to_b]),
        (map_taps_hbm.at[:, at_c], map_taps_ref.at[:, to_c]),
        (map_base_hbm.at[:, at_b], map_base_ref.at[:, to_b]),
        (map_base_hbm.at[:, at_c], map_base_ref.at[:, to_c]),
        (taps_hbm, taps_ref),
        (base_hbm, base_ref),
        (x_hbm, x_ref),
        (gate_hbm, gate_ref),
        (gain_hbm, gain_ref),
        (w_hbm, w_ref),
    )
    loads = [
        pltpu.make_async_copy(source, target, in_sem.at[i])
        for i, (source, target) in enumerate(fetches)
    ]

    barrier = pltpu.get_barrier_semaphore()

    def greet(step, carry):
        pl.semaphore_signal(
            barrier, inc=1, device_id=(lax.rem(me + step, n), z), device_id_type=mesh_ids
        )
        return carry

    lax.fori_loop(1, n, greet, 0)

    @pl.when(z > 0)
    def _():
        pl.semaphore_signal(barrier, inc=1, device_id=(me, z - 1), device_id_type=mesh_ids)

    @pl.when(z < m - 1)
    def _():
        pl.semaphore_signal(barrier, inc=1, device_id=(me, z + 1), device_id_type=mesh_ids)

    for load in loads[:12]:
        load.start()

    has_left, has_right = me > 0, me < n - 1
    odd = core == 1

    for load in loads[:3]:
        load.wait()

    def turned(value):
        size = value.shape[0]
        same = lax.broadcasted_iota(jnp.int32, (size, size), 0) == lax.broadcasted_iota(
            jnp.int32, (size, size), 1
        )
        return lax.dot_general(
            value, same.astype(f32), (((0,), (0,)), ((), ())), precision=exact,
            preferred_element_type=f32,
        )

    step = jax.nn.softplus(turned(step_ref[...]))
    log_decay = -jnp.exp(rate_ref[...]) * step
    row = lax.broadcasted_iota(jnp.int32, (length, length), 0)
    column = lax.broadcasted_iota(jnp.int32, (length, length), 1)
    lower = (row >= column).astype(f32)
    cum = jnp.dot(lower, log_decay, precision=exact, preferred_element_type=f32)
    final = cum[length - 1 : length]
    ones = jnp.ones((length, heads), bf16)
    blank = jnp.zeros((length, heads), bf16)
    gap_left[...] = jnp.concatenate(
        [*three(cum * LOG2E), ones, ones, ones, blank, blank], axis=1
    )
    source_log = jnp.log(step) * LOG2E - cum * LOG2E
    source_rows = turned(source_log)
    unit = jnp.ones((heads, length), bf16)
    gap_right[...] = jnp.concatenate(
        [unit, unit, unit, *three(source_rows), unit, unit], axis=0
    )
    ends[...] = jnp.concatenate([*three(jnp.exp(final - cum) * step), blank], axis=1)
    growth[...] = jnp.concatenate([*three(jnp.exp(cum)), blank], axis=1)
    first_row = lax.broadcasted_iota(jnp.int32, (16, heads), 0) < 8
    two = jnp.where(first_row, jnp.exp(final), skip_ref[...])
    two = jnp.concatenate([*three(two), jnp.zeros((16, heads), bf16)], axis=1)

    def choose(c, carry):
        start = pl.multiple_of(c * tile, tile)
        slot = lax.broadcasted_iota(jnp.int32, (4 * heads, tile), 0)
        head = lax.rem(slot, heads) * HEAD_DIM
        lane = lax.broadcasted_iota(jnp.int32, (4 * heads, tile), 1) + start
        chosen[:, pl.ds(start, tile)] = (
            ((lane >= head) & (lane < head + HEAD_DIM)).astype(f32).astype(bf16)
        )
        return carry

    lax.fori_loop(0, tiles, choose, 0)

    def spread(per_head, span):
        return jnp.dot(per_head, chosen[:, span], preferred_element_type=f32)

    channel_rows[...] = spread(two, slice(None))
    lanes = own_end.shape[1]
    own_end[...] = jnp.zeros_like(own_end)
    own_end[:, 0:heads] = jnp.broadcast_to(final, (8, heads))
    all_ends[me] = jnp.zeros((8, lanes), f32)

    beside = (z > 0).astype(jnp.int32) + (z < m - 1).astype(jnp.int32)
    pl.semaphore_wait(barrier, n - 1 + beside)

    last_rows = pl.ds(length - rim, rim)

    def rim_copy(which):
        source, target = (
            (x_hbm.at[last_rows], rim_x),
            (maps_hbm.at[last_rows, at_b], rim_maps.at[:, to_b]),
            (maps_hbm.at[last_rows, at_c], rim_maps.at[:, to_c]),
        )[which]
        return pltpu.make_async_remote_copy(
            src_ref=source,
            dst_ref=target,
            send_sem=rim_send.at[which],
            recv_sem=rim_recv.at[which],
            device_id=(me + 1, z),
            device_id_type=mesh_ids,
        )

    @pl.when(has_right)
    def _():
        for which in range(3):
            rim_copy(which).start()

    def end_copy(offset, sender):
        return pltpu.make_async_remote_copy(
            src_ref=own_end,
            dst_ref=all_ends.at[sender],
            send_sem=end_send.at[offset],
            recv_sem=end_recv.at[sender],
            device_id=(lax.rem(me + offset, n), z),
            device_id_type=mesh_ids,
        )

    def send_end(offset, carry):
        end_copy(offset, me).start()
        return carry

    lax.fori_loop(1, n, send_end, 0)

    for load in loads[3:12]:
        load.wait()
    for load in loads[12:]:
        load.start()

    def smooth(rows_ref, taps, base, out, start, size):
        span = pl.ds(start, size)
        pad[:, 0:size] = rows_ref[:, span].astype(f32)
        total = base[:, span]
        for k in range(CONV):
            at = rim - (CONV - 1) + k
            total = total + taps[k : k + 1, span] * pad[at : at + length - rim, 0:size]
        out[rim:length, span] = jax.nn.silu(total).astype(bf16)

    def smooth_rim(rows_ref, rim_ref, taps, base, out, start, size):
        span = pl.ds(start, size)
        pad[0:rim, 0:size] = rim_ref[:, span].astype(f32)
        pad[rim : 2 * rim, 0:size] = rows_ref[0:rim, span].astype(f32)
        total = base[:, span]
        for k in range(CONV):
            at = rim - (CONV - 1) + k
            total = total + taps[k : k + 1, span] * pad[at : at + rim, 0:size]
        out[0:rim, span] = jax.nn.silu(total).astype(bf16)

    for c in range(0, 2 * span_maps, tile):
        smooth(maps_ref, map_taps_ref, map_base_ref, maps_conv, c, tile)

    def smooth_tile(c, carry):
        smooth(x_ref, taps_ref, base_ref, values, pl.multiple_of(c * tile, tile), tile)
        return carry

    lax.fori_loop(0, tiles, smooth_tile, 0)

    @pl.when(has_left)
    def _():
        for which in range(3):
            rim_copy(which).wait_recv()

    @pl.when(jnp.logical_not(has_left))
    def _():
        rim_x[...] = jnp.zeros_like(rim_x)
        rim_maps[...] = jnp.zeros_like(rim_maps)

    for c in range(0, 2 * span_maps, tile):
        smooth_rim(maps_ref, rim_maps, map_taps_ref, map_base_ref, maps_conv, c, tile)
    for c in range(0, channels, tile):
        smooth_rim(x_ref, rim_x, taps_ref, base_ref, values, c, tile)

    def chain_send_copy(level, hop, c):
        return pltpu.make_async_remote_copy(
            src_ref=leaving.at[c],
            dst_ref=arrived.at[level, c],
            send_sem=chain_send.at[hop, c],
            recv_sem=chain_recv.at[level, c],
            device_id=(me + 1 if level == 0 else me + 2 * (hop + 1), z),
            device_id_type=mesh_ids,
        )

    def chain_forward(level, c):
        return pltpu.make_async_remote_copy(
            src_ref=arrived.at[level, c],
            dst_ref=arrived.at[level, c],
            send_sem=forward_send.at[level, c],
            recv_sem=chain_recv.at[level, c],
            device_id=(partner, z),
            device_id_type=mesh_ids,
        )

    def hops(level):
        return range(max(1, 2**level // 2))

    def sends(level):
        return lax.rem(me, 2 ** (level + 1)) == 2**level - 1

    def gets(level):
        return lax.rem(lax.div(me, 2**level), 2) == 1

    per = group_width // tile

    for g in range(groups_here):
        turned_maps[g] = turned(
            maps_conv[:, g * STATE : (g + 1) * STATE].astype(f32)
        ).astype(bf16)

    for g in range(groups_here):
        mine = range(g * per, (g + 1) * per)
        spans = [slice(c * tile, (c + 1) * tile) for c in mine]
        weighted = [
            (values[:, span].astype(f32) * spread(ends[...], span)).astype(bf16)
            for span in spans
        ]
        totals = [jnp.dot(turned_maps[g], w, preferred_element_type=f32) for w in weighted]
        for c, total in zip(mine, totals):
            local[c] = total
            state[c] = jnp.zeros_like(total)
            leaving[c] = total.astype(bf16)

        @pl.when(sends(0))
        def _():
            for c in mine:
                chain_send_copy(0, 0, c).start()

    def link(level, c):
        span = pl.ds(pl.multiple_of(c * tile, tile), tile)

        @pl.when(gets(level))
        def _():
            chain_forward(level, c).wait_recv()
            if level == 0:
                state[c] = arrived[level, c].astype(f32)
            else:
                @pl.when(odd)
                def _():
                    chain_forward(level, c).start()

                state[c] = state[c] + prefix_rows[level, 0:1, span] * arrived[level, c].astype(f32)

        if level + 1 < levels:
            @pl.when(sends(level + 1))
            def _():
                leaving[c] = (channel_rows[0:1, span] * state[c] + local[c]).astype(bf16)
                for hop in hops(level + 1):
                    chain_send_copy(level + 1, hop, c).start()

    def link_all(level, first, last):
        def body(c, carry):
            link(level, c)
            return carry

        lax.fori_loop(first, last, body, 0)

    link_all(0, 0, tiles)

    for g in range(groups_here):
        scores[g] = lax.dot_general(
            maps_conv[:, span_maps + g * STATE : span_maps + (g + 1) * STATE],
            maps_conv[:, g * STATE : (g + 1) * STATE],
            (((1,), (1,)), ((), ())),
            preferred_element_type=f32,
        )

    def get_end(offset, carry):
        end_copy(offset, lax.rem(me + offset, n)).wait_recv()
        return carry

    lax.fori_loop(1, n, get_end, 0)

    for level in range(1, levels):
        base = me - lax.rem(me, 2**level)
        total = jnp.zeros((8, lanes), f32)
        for i in range(n):
            total = total + jnp.where((base <= i) & (i < me), all_ends[i], 0.0)
        passed = jnp.exp(total[:, 0:heads])
        passed = jnp.concatenate([passed, passed], axis=0)
        passed = jnp.concatenate([*three(passed), jnp.zeros((16, heads), bf16)], axis=1)

        prefix_rows[level] = spread(passed, slice(None))

    pair = 2 * HEAD_DIM
    lane = lax.broadcasted_iota(jnp.int32, (half, pair), 1)
    batch = 4

    def mask_of(head):
        slot = lax.broadcasted_iota(jnp.int32, (1, 8 * heads), 1)
        return ((lax.rem(slot, heads) == head) & (slot < 6 * heads)).astype(f32).astype(bf16)

    def within(turn, carry):
        g = lax.div(turn * batch * pair, group_width)
        gaps = []
        for e in range(2 * batch):
            left = gap_left[...] * mask_of(2 * batch * turn + e)
            gaps.append((
                jnp.dot(left[0:half], gap_right[:, 0:half], preferred_element_type=f32),
                jnp.dot(left[half:length], gap_right[...], preferred_element_type=f32),
            ))
        causal = lax.broadcasted_iota(jnp.int32, (half, half), 0) >= lax.broadcasted_iota(
            jnp.int32, (half, half), 1
        )
        causal_late = lax.broadcasted_iota(jnp.int32, (half, length), 0) + half >= (
            lax.broadcasted_iota(jnp.int32, (half, length), 1)
        )
        mixing = [
            (
                (jnp.where(causal, jnp.exp2(a), 0.0) * scores[g, 0:half, 0:half]).astype(bf16),
                (jnp.where(causal_late, jnp.exp2(b), 0.0) * scores[g, half:length]).astype(bf16),
            )
            for a, b in gaps
        ]
        for q in range(batch):
            span = pl.ds(pl.multiple_of((turn * batch + q) * pair, pair), pair)
            early, late = [], []
            for a, b in mixing[2 * q : 2 * q + 2]:
                early.append(jnp.dot(a, values[0:half, span], preferred_element_type=f32))
                late.append(jnp.dot(b, values[:, span], preferred_element_type=f32))
            y[0:half, span] = jnp.where(lane < HEAD_DIM, early[0], early[1])
            y[half:length, span] = jnp.where(lane < HEAD_DIM, late[0], late[1])
        return carry

    lax.fori_loop(0, channels // (pair * batch), within, 0)

    for level in range(1, levels - 1):
        link_all(level, 0, tiles)

    for load in loads[12:14]:
        load.wait()

    def partner_copy(slot, g):
        return pltpu.make_async_remote_copy(
            src_ref=gat.at[slot - 1, g],
            dst_ref=gat.at[slot, g],
            send_sem=gat_send.at[slot, g],
            recv_sem=gat_recv.at[slot, g],
            device_id=(partner, z),
            device_id_type=mesh_ids,
        )

    def source_mask(i, who):
        swap = (who == 1) & (chips >= 4)
        return i + jnp.where(swap & (i == 1), 1, 0) - jnp.where(swap & (i == 2), 1, 0)

    def chip_at(mask):
        there, bit = chip, 1
        while bit < chips:
            on = lax.rem(lax.div(mask, bit), 2)
            there = there + on * (bit - 2 * bit * lax.rem(lax.div(chip, bit), 2))
            bit *= 2
        return there

    def across_copy(i, g):
        return pltpu.make_async_remote_copy(
            src_ref=gat.at[0, g],
            dst_ref=gat.at[2 * i, g],
            send_sem=gat_send.at[2 * i, g],
            recv_sem=gat_recv.at[2 * i, g],
            device_id=(2 * chip_at(source_mask(i, core)) + core, z),
            device_id_type=mesh_ids,
        )

    def arrival(slot, g):
        return pltpu.make_async_remote_copy(
            src_ref=gat.at[slot, g],
            dst_ref=gat.at[slot, g],
            send_sem=gat_send.at[slot, g],
            recv_sem=gat_recv.at[slot, g],
            device_id=(partner, z),
            device_id_type=mesh_ids,
        )

    for g in range(groups_here):
        link_all(levels - 1, g * per, (g + 1) * per)
        mine = range(g * per, (g + 1) * per)
        spans = [slice(c * tile, (c + 1) * tile) for c in mine]
        output_map = maps_conv[:, span_maps + g * STATE : span_maps + (g + 1) * STATE]
        carried = [
            jnp.dot(output_map, state[c].astype(bf16), preferred_element_type=f32)
            for c in mine
        ]
        grown = [spread(growth[...], span) for span in spans]
        squares = jnp.zeros((length, 128), f32)
        for span, more, scale in zip(spans, carried, grown):
            total = y[:, span] + more * scale
            total = total + channel_rows[8:9, span] * values[:, span].astype(f32)
            total = total * jax.nn.silu(gate_ref[:, span].astype(f32))
            y[:, span] = total
            for d in range(0, tile, 128):
                squares = squares + total[:, d : d + 128] * total[:, d : d + 128]
        scale = lax.rsqrt(jnp.sum(squares, axis=1, keepdims=True) / group_width + 1e-05)
        for c, span in enumerate(spans):
            gat[0, g, :, c * tile : (c + 1) * tile] = (
                y[:, span] * scale * gain_ref[:, span]
            ).astype(bf16)
        partner_copy(1, g).start()
        if chips > 1:
            across_copy(1, g).start()

    def chain_z(step, j, buffer, send, recv, to):
        return pltpu.make_async_remote_copy(
            src_ref=part.at[step, pl.ds(j * rows, rows)],
            dst_ref=buffer.at[step, pl.ds(j * rows, rows)],
            send_sem=send.at[step, j],
            recv_sem=recv.at[step, j],
            device_id=(me, to),
            device_id_type=mesh_ids,
        )

    def owner(step):
        who = core + lax.rem(step, 2) * (1 - 2 * core)
        return 2 * chip_at(source_mask(lax.div(step, 2), who)) + who

    def columns(sender):
        return pl.ds(pl.multiple_of(sender * width, width), width)

    def own_rows():
        return pl.ds(pl.multiple_of(z * rows, rows), rows)

    def out_copy(step, sender):
        return pltpu.make_async_remote_copy(
            src_ref=part.at[step, own_rows()],
            dst_ref=out_ref.at[:, columns(sender)],
            send_sem=out_send.at[step],
            recv_sem=out_recv.at[sender],
            device_id=(owner(step), z),
            device_id_type=mesh_ids,
        )

    def added(step, j, buffer):
        span = pl.ds(j * rows, rows)
        part[step, span] = (
            part[step, span].astype(f32) + buffer[step, span].astype(f32)
        ).astype(bf16)

    up_lag, down_lag = z, m - 1 - z
    last_lag = jnp.maximum(up_lag, down_lag)
    wide = min(width, 256)

    loads[14].wait()

    def turn(tau, carry):
        @pl.when(tau < n)
        def _():
            direct = (tau > 0) & (lax.rem(tau, 2) == 0)

            @pl.when(direct)
            def _():
                for g in range(groups_here):
                    arrival(tau, g).wait_send()

            @pl.when(direct & (tau < n - 2))
            def _():
                for g in range(groups_here):
                    across_copy(lax.div(tau, 2) + 1, g).start()

            @pl.when(tau > 0)
            def _():
                for g in range(groups_here):
                    arrival(tau, g).wait_recv()

            @pl.when(direct)
            def _():
                for g in range(groups_here):
                    partner_copy(tau + 1, g).start()

            for c in range(0, width, wide):
                total = jnp.zeros((length, wide), f32)
                for g in range(groups_here):
                    total = total + jnp.dot(
                        gat[tau, g],
                        w_ref[g * group_width : (g + 1) * group_width, c : c + wide],
                        preferred_element_type=f32,
                    )
                part[tau, :, c : c + wide] = total.astype(bf16)

        t_up = tau - up_lag

        @pl.when((t_up >= 0) & (t_up < n))
        def _():
            for j in range(m - 1, 0, -1):
                @pl.when(z < j)
                def _():
                    copy = chain_z(t_up, j, up, up_send, up_recv, z + 1)

                    @pl.when(z > 0)
                    def _():
                        copy.wait_recv()
                        added(t_up, j, up)

                    copy.start()

        t_down = tau - down_lag

        @pl.when((t_down >= 0) & (t_down < n))
        def _():
            for j in range(m - 1):
                @pl.when(z > j)
                def _():
                    copy = chain_z(t_down, j, down, down_send, down_recv, z - 1)

                    @pl.when(z < m - 1)
                    def _():
                        copy.wait_recv()
                        added(t_down, j, down)

                    copy.start()

        t_last = tau - last_lag

        @pl.when((t_last >= 0) & (t_last < n))
        def _():
            for j in range(m):
                @pl.when(z == j)
                def _():
                    span = pl.ds(j * rows, rows)
                    total = part[t_last, span].astype(f32)
                    if j > 0:
                        chain_z(t_last, j, up, up_send, up_recv, z).wait_recv()
                        total = total + up[t_last, span].astype(f32)
                    if j < m - 1:
                        chain_z(t_last, j, down, down_send, down_recv, z).wait_recv()
                        total = total + down[t_last, span].astype(f32)
                    part[t_last, span] = total.astype(bf16)

            @pl.when(t_last == 0)
            def _():
                out_ref[:, columns(me)] = part[0, own_rows()]

            @pl.when(t_last > 0)
            def _():
                out_copy(t_last, me).start()

        return carry

    lax.fori_loop(0, n + m - 1, turn, 0)

    def finish(step, carry):
        @pl.when(lax.rem(step, 2) == 1)
        def _():
            for g in range(groups_here):
                arrival(step, g).wait_send()

        @pl.when(step > 0)
        def _():
            end_copy(step, me).wait_send()

        for j in range(m):
            @pl.when(z < j)
            def _():
                chain_z(step, j, up, up_send, up_recv, z).wait_send()

            @pl.when(z > j)
            def _():
                chain_z(step, j, down, down_send, down_recv, z).wait_send()

        @pl.when(step > 0)
        def _():
            out_copy(step, me).wait_send()
            out_copy(step, lax.rem(me + step, n)).wait_recv()

        return carry

    lax.fori_loop(0, n, finish, 0)

    @pl.when(has_right)
    def _():
        for which in range(3):
            rim_copy(which).wait_send()

    def sent(c, carry):
        for level in range(levels):
            @pl.when(sends(level))
            def _():
                for hop in hops(level):
                    chain_send_copy(level, hop, c).wait_send()

            if level > 0:
                @pl.when(gets(level) & odd)
                def _():
                    chain_forward(level, c).wait_send()

        return carry

    lax.fori_loop(0, tiles, sent, 0)


def layer(x, gate, maps, step_raw, rate, skip, taps, base, map_taps, map_base, gain, weight):
    n, m = lax.axis_size("seq"), lax.axis_size("tp")
    length, channels = x.shape
    heads = rate.shape[0]
    per_group = HEADS // GROUPS
    groups_here = heads // per_group
    tile = max(128, channels // 8)
    tiles = channels // tile
    width = weight.shape[1]
    span_maps = 2 * groups_here * STATE
    rim = 16
    levels = n.bit_length() - 1
    lanes = -(-heads // 128) * 128
    bf16, f32 = jnp.bfloat16, jnp.float32
    dma = pltpu.SemaphoreType.DMA
    operands = (
        x, gate, maps, step_raw.T, rate[None], skip[None], taps, base[None],
        map_taps, map_base[None], gain[None], weight,
    )
    blocks = pltpu.VMEM((n, length, width), bf16)
    return pl.pallas_call(
        functools.partial(layer_kernel, n, m, per_group),
        out_shape=jax.ShapeDtypeStruct((length // m, n * width), bf16),
        in_specs=[pl.BlockSpec(memory_space=pl.ANY)] * len(operands),
        out_specs=pl.BlockSpec(memory_space=pltpu.VMEM),
        scratch_shapes=[
            pltpu.VMEM((length, channels), bf16),
            pltpu.VMEM((length, channels), bf16),
            pltpu.VMEM((length, span_maps), bf16),
            pltpu.VMEM((heads, length), f32),
            pltpu.VMEM((1, heads), f32),
            pltpu.VMEM((1, heads), f32),
            pltpu.VMEM((CONV, channels), f32),
            pltpu.VMEM((1, channels), f32),
            pltpu.VMEM((CONV, span_maps), f32),
            pltpu.VMEM((1, span_maps), f32),
            pltpu.VMEM((1, channels), f32),
            pltpu.VMEM(weight.shape, bf16),
            dma((15,)),
            pltpu.VMEM((rim, channels), bf16),
            pltpu.VMEM((rim, span_maps), bf16),
            pltpu.VMEM((length, max(tile, STATE)), f32),
            pltpu.VMEM((length, channels), bf16),
            pltpu.VMEM((length, span_maps), bf16),
            pltpu.VMEM((length, channels), f32),
            pltpu.VMEM((groups_here, length, length), f32),
            pltpu.VMEM((tiles, STATE, tile), f32),
            pltpu.VMEM((tiles, STATE, tile), f32),
            pltpu.VMEM((levels, tiles, STATE, tile), bf16),
            pltpu.VMEM((tiles, STATE, tile), bf16),
            pltpu.VMEM((length, 8 * heads), bf16),
            pltpu.VMEM((8 * heads, length), bf16),
            pltpu.VMEM((groups_here, STATE, length), bf16),
            pltpu.VMEM((length, 4 * heads), bf16),
            pltpu.VMEM((length, 4 * heads), bf16),
            pltpu.VMEM((8, lanes), f32),
            pltpu.VMEM((n, 8, lanes), f32),
            pltpu.VMEM((4 * heads, channels), bf16),
            pltpu.VMEM((16, channels), f32),
            pltpu.VMEM((levels, 16, channels), f32),
            pltpu.VMEM((n, groups_here, length, channels // groups_here), bf16),
            blocks,
            blocks,
            blocks,
            dma((3,)),
            dma((3,)),
            dma((n,)),
            dma((n,)),
            dma((max(1, n // 4), tiles)),
            dma((levels, tiles)),
            dma((levels, tiles)),
            dma((n, groups_here)),
            dma((n, groups_here)),
            dma((n, m)),
            dma((n, m)),
            dma((n, m)),
            dma((n, m)),
            dma((n,)),
            dma((n,)),
        ],
        compiler_params=pltpu.CompilerParams(
            collective_id=2, has_side_effects=True, vmem_limit_bytes=60 << 20
        ),
        cost_estimate=pl.CostEstimate(
            flops=2 * n * length * channels * width,
            bytes_accessed=2 * (channels * width + 3 * length * channels),
            transcendentals=0,
        ),
    )(*operands)


def shards(
    conv_values,
    gate_values,
    conv_maps,
    step_raw,
    decay_log,
    skip_gain,
    values_kernel,
    values_offset,
    maps_kernel,
    maps_offset,
    norm_weight,
    out_weight,
    residual,
):
    length = conv_values.shape[0]
    heads_dev = decay_log.shape[0]
    per_group = HEADS // GROUPS
    whole_groups = heads_dev % per_group == 0
    chips = lax.axis_size("seq") // 2
    paired = lax.axis_size("seq") == 2 * chips and chips & (chips - 1) == 0
    if whole_groups and paired and heads_dev % 32 == 0:
        summed = layer(
            conv_values, gate_values, conv_maps, step_raw, decay_log, skip_gain, values_kernel,
            values_offset, maps_kernel, maps_offset, norm_weight, out_weight,
        )
        return residual.astype(jnp.float32) + summed.astype(jnp.float32)
    step_size = jax.nn.softplus(step_raw)
    place = jnp.arange(length, dtype=jnp.int32)
    cum_log = jnp.dot(
        (place[:, None] >= place[None, :]).astype(jnp.float32),
        -jnp.exp(decay_log)[None, :] * step_size,
        precision=lax.Precision.HIGHEST,
    )
    normed = front(
        conv_values, gate_values, conv_maps, cum_log, step_size, skip_gain, values_kernel,
        values_offset, maps_kernel, maps_offset, norm_weight, whole_groups,
    )
    if not whole_groups:
        gated_out = normed.reshape(length, heads_dev, HEAD_DIM)
        head_squares = jnp.sum(gated_out * gated_out, axis=2)
        all_heads = lax.all_gather(head_squares, "tp", axis=1, tiled=True)
        group_totals = jnp.sum(all_heads.reshape(length, GROUPS, per_group), axis=2)
        heads_here = lax.axis_index("tp") * heads_dev + jnp.arange(heads_dev, dtype=jnp.int32)
        inv_rms = lax.rsqrt(
            group_totals[:, heads_here // per_group] / (per_group * HEAD_DIM) + 1e-05
        )
        normed = (
            (gated_out * inv_rms[:, :, None]).reshape(length, heads_dev * HEAD_DIM)
            * norm_weight[None, :]
        ).astype(jnp.bfloat16)
    blocks = mix(normed, out_weight)
    summed = jnp.transpose(blocks, (1, 0, 2)).reshape(residual.shape).astype(jnp.float32)
    return residual.astype(jnp.float32) + summed


def solution(mesh):
    placed = (
        P("seq", "tp"),
        P("seq", "tp"),
        P("seq", None),
        P("seq", "tp"),
        P("tp"),
        P("tp"),
        P(None, "tp"),
        P("tp"),
        P(),
        P(),
        P("tp"),
        P("tp", "seq"),
        P(("seq", "tp"), None),
    )
    return jax.shard_map(
        shards, mesh=mesh, in_specs=placed, out_specs=P(("seq", "tp"), None), check_vma=False
    )
```

```python
import functools

import jax
import jax.numpy as jnp
from jax import lax
from jax.experimental import pallas as pl
from jax.experimental.pallas import tpu as pltpu
from jax.sharding import PartitionSpec as P

HEADS = 128
HEAD_DIM = 64
STATE = 128
GROUPS = 8
CONV = 4


def ring_place(spot, size):
    if size % 4:
        return spot
    half = size // 2
    past = spot - half
    turned = half + (half - 2 - 2 * lax.div(past, 2)) + lax.rem(past, 2)
    return jnp.where(spot < half, spot, turned)


def mix_kernel(
    n, m, x_ref, w_ref, out_ref, gat, part, up, down,
    own_sem, gat_send, gat_recv, up_send, up_recv, down_send, down_recv, out_send, out_recv,
):
    mesh_ids = pl.DeviceIdType.MESH
    me, z = lax.axis_index("seq"), lax.axis_index("tp")
    spot = ring_place(me, n)
    right = ring_place(lax.rem(spot + 1, n), n)
    left = ring_place(lax.rem(spot + n - 1, n), n)
    half = gat.shape[2]
    depth = gat.shape[3]
    width = w_ref.shape[1]
    rows = part.shape[1] // m
    tile = min(width, 256)

    own = [
        pltpu.make_async_copy(x_ref.at[pl.ds(d * half, half)], gat.at[0, d], own_sem.at[d])
        for d in range(2)
    ]
    for copy in own:
        copy.start()

    barrier = pltpu.get_barrier_semaphore()

    def greet(step, carry):
        pl.semaphore_signal(
            barrier, inc=1, device_id=(lax.rem(me + step, n), z), device_id_type=mesh_ids
        )
        return carry

    lax.fori_loop(1, n, greet, 0)

    @pl.when(z > 0)
    def _():
        pl.semaphore_signal(barrier, inc=1, device_id=(me, z - 1), device_id_type=mesh_ids)

    @pl.when(z < m - 1)
    def _():
        pl.semaphore_signal(barrier, inc=1, device_id=(me, z + 1), device_id_type=mesh_ids)

    beside = (z > 0).astype(jnp.int32) + (z < m - 1).astype(jnp.int32)
    pl.semaphore_wait(barrier, n - 1 + beside)

    for copy in own:
        copy.wait()

    def gather_copy(step, d):
        return pltpu.make_async_remote_copy(
            src_ref=gat.at[step, d],
            dst_ref=gat.at[step + 1, d],
            send_sem=gat_send.at[step, d],
            recv_sem=gat_recv.at[step + 1, d],
            device_id=(right if d == 0 else left, z),
            device_id_type=mesh_ids,
        )

    def gather_arrival(step, d):
        return pltpu.make_async_remote_copy(
            src_ref=gat.at[step, d],
            dst_ref=gat.at[step, d],
            send_sem=gat_send.at[step, d],
            recv_sem=gat_recv.at[step, d],
            device_id=(right if d == 0 else left, z),
            device_id_type=mesh_ids,
        )

    def chain_copy(step, j, buffer, send, recv, to):
        return pltpu.make_async_remote_copy(
            src_ref=part.at[step, pl.ds(j * rows, rows)],
            dst_ref=buffer.at[step, pl.ds(j * rows, rows)],
            send_sem=send.at[step, j],
            recv_sem=recv.at[step, j],
            device_id=(me, to),
            device_id_type=mesh_ids,
        )

    def owner(step):
        there = jnp.where(z < m // 2, spot - step + n, spot + step)
        return ring_place(lax.rem(there, n), n)

    def out_copy(step, sender):
        return pltpu.make_async_remote_copy(
            src_ref=part.at[step, pl.ds(pl.multiple_of(z * rows, rows), rows)],
            dst_ref=out_ref.at[sender],
            send_sem=out_send.at[step],
            recv_sem=out_recv.at[sender],
            device_id=(owner(step), z),
            device_id_type=mesh_ids,
        )

    def added(step, j, buffer):
        span = pl.ds(j * rows, rows)
        part[step, span] = (
            part[step, span].astype(jnp.float32) + buffer[step, span].astype(jnp.float32)
        ).astype(jnp.bfloat16)

    up_lag, down_lag = z, m - 1 - z
    last_lag = jnp.maximum(up_lag, down_lag)

    def turn(tau, carry):
        @pl.when(tau < n)
        def _():
            @pl.when(tau > 0)
            def _():
                for d in range(2):
                    gather_arrival(tau, d).wait_recv()

            @pl.when(tau < n - 1)
            def _():
                for d in range(2):
                    gather_copy(tau, d).start()

            block = gat[tau].reshape(2 * half, depth)
            for c in range(0, width, tile):
                part[tau, :, c : c + tile] = jnp.dot(
                    block, w_ref[:, c : c + tile], preferred_element_type=jnp.float32
                ).astype(jnp.bfloat16)

        t_up = tau - up_lag

        @pl.when((t_up >= 0) & (t_up < n))
        def _():
            for j in range(m - 1, 0, -1):
                @pl.when(z < j)
                def _():
                    copy = chain_copy(t_up, j, up, up_send, up_recv, z + 1)

                    @pl.when(z > 0)
                    def _():
                        copy.wait_recv()
                        added(t_up, j, up)

                    copy.start()

        t_down = tau - down_lag

        @pl.when((t_down >= 0) & (t_down < n))
        def _():
            for j in range(m - 1):
                @pl.when(z > j)
                def _():
                    copy = chain_copy(t_down, j, down, down_send, down_recv, z - 1)

                    @pl.when(z < m - 1)
                    def _():
                        copy.wait_recv()
                        added(t_down, j, down)

                    copy.start()

        t_last = tau - last_lag

        @pl.when((t_last >= 0) & (t_last < n))
        def _():
            for j in range(m):
                @pl.when(z == j)
                def _():
                    span = pl.ds(j * rows, rows)
                    total = part[t_last, span].astype(jnp.float32)
                    if j > 0:
                        chain_copy(t_last, j, up, up_send, up_recv, z).wait_recv()
                        total = total + up[t_last, span].astype(jnp.float32)
                    if j < m - 1:
                        chain_copy(t_last, j, down, down_send, down_recv, z).wait_recv()
                        total = total + down[t_last, span].astype(jnp.float32)
                    part[t_last, span] = total.astype(jnp.bfloat16)

            @pl.when(t_last == 0)
            def _():
                out_ref[me] = part[0, pl.ds(pl.multiple_of(z * rows, rows), rows)]

            @pl.when(t_last > 0)
            def _():
                out_copy(t_last, me).start()

        return carry

    lax.fori_loop(0, n + m - 1, turn, 0)

    def finish(step, carry):
        @pl.when(step < n - 1)
        def _():
            for d in range(2):
                gather_copy(step, d).wait_send()

        for j in range(m):
            @pl.when(z < j)
            def _():
                chain_copy(step, j, up, up_send, up_recv, z).wait_send()

            @pl.when(z > j)
            def _():
                chain_copy(step, j, down, down_send, down_recv, z).wait_send()

        @pl.when(step > 0)
        def _():
            out_copy(step, me).wait_send()
            out_copy(step, lax.rem(me + step, n)).wait_recv()

        return carry

    lax.fori_loop(0, n, finish, 0)


def mix(normed, weight):
    n, m = lax.axis_size("seq"), lax.axis_size("tp")
    length, depth = normed.shape
    width = weight.shape[1]
    rows = length // m
    half = length // 2
    slots = pltpu.VMEM((n, length, width), jnp.bfloat16)
    dma = pltpu.SemaphoreType.DMA
    vmem = pl.BlockSpec(memory_space=pltpu.VMEM)
    return pl.pallas_call(
        functools.partial(mix_kernel, n, m),
        out_shape=jax.ShapeDtypeStruct((n, rows, width), jnp.bfloat16),
        in_specs=[pl.BlockSpec(memory_space=pl.ANY), vmem],
        out_specs=vmem,
        scratch_shapes=[
            pltpu.VMEM((n, 2, half, depth), jnp.bfloat16),
            slots,
            slots,
            slots,
            dma((2,)),
            dma((n, 2)),
            dma((n, 2)),
            dma((n, m)),
            dma((n, m)),
            dma((n, m)),
            dma((n, m)),
            dma((n,)),
            dma((n,)),
        ],
        compiler_params=pltpu.CompilerParams(
            collective_id=0, has_side_effects=True, vmem_limit_bytes=48 << 20
        ),
        cost_estimate=pl.CostEstimate(
            flops=2 * n * length * depth * width,
            bytes_accessed=2 * (depth * width + length * depth),
            transcendentals=0,
        ),
    )(normed, weight)


def front_kernel(
    n, per_group, whole_groups, x_ref, gate_ref, maps_ref, cum_ref, cum_t_ref, step_ref, step_t_ref,
    decay_ref, skip_ref, taps_ref, base_ref, map_taps_ref, map_base_ref, gain_ref, out_ref,
    rim_x, rim_maps, pad, values, y, b_maps, c_maps, scores, local, arrived, leaving,
    rim_send, rim_recv, chain_send, chain_recv,
):
    mesh_ids = pl.DeviceIdType.MESH
    exact = lax.Precision.HIGHEST
    me, z = lax.axis_index("seq"), lax.axis_index("tp")
    length, channels = x_ref.shape
    heads = cum_ref.shape[1]
    groups_here = scores.shape[0]
    first_group = lax.div(z * heads, per_group)
    tile = arrived.shape[2]
    tiles = channels // tile
    group_width = channels // groups_here
    rim = rim_x.shape[0]

    barrier = pltpu.get_barrier_semaphore()
    has_left, has_right = me > 0, me < n - 1

    @pl.when(has_left)
    def _():
        pl.semaphore_signal(barrier, inc=1, device_id=(me - 1, z), device_id_type=mesh_ids)

    @pl.when(has_right)
    def _():
        pl.semaphore_signal(barrier, inc=1, device_id=(me + 1, z), device_id_type=mesh_ids)

    pl.semaphore_wait(barrier, has_left.astype(jnp.int32) + has_right.astype(jnp.int32))

    def rim_copy(which):
        source, target = ((x_ref, rim_x), (maps_ref, rim_maps))[which]
        return pltpu.make_async_remote_copy(
            src_ref=source.at[pl.ds(length - rim, rim)],
            dst_ref=target,
            send_sem=rim_send.at[which],
            recv_sem=rim_recv.at[which],
            device_id=(me + 1, z),
            device_id_type=mesh_ids,
        )

    @pl.when(has_right)
    def _():
        for which in range(2):
            rim_copy(which).start()

    @pl.when(has_left)
    def _():
        for which in range(2):
            rim_copy(which).wait_recv()

    @pl.when(jnp.logical_not(has_left))
    def _():
        rim_x[...] = jnp.zeros_like(rim_x)
        rim_maps[...] = jnp.zeros_like(rim_maps)

    def conv(rows_ref, rim_ref, taps, base, start, size):
        span = pl.ds(start, size)
        pad[0:rim, 0:size] = rim_ref[:, span].astype(jnp.float32)
        pad[rim : rim + length, 0:size] = rows_ref[:, span].astype(jnp.float32)
        total = base[:, span]
        for k in range(CONV):
            at = rim - (CONV - 1) + k
            total = total + taps[k : k + 1, span] * pad[at : at + length, 0:size]
        return jax.nn.silu(total).astype(jnp.bfloat16)

    for g in range(groups_here):
        at = pl.multiple_of((first_group + g) * STATE, STATE)
        b_maps[g] = conv(maps_ref, rim_maps, map_taps_ref, map_base_ref, at, STATE)
        at = pl.multiple_of((GROUPS + first_group + g) * STATE, STATE)
        c_maps[g] = conv(maps_ref, rim_maps, map_taps_ref, map_base_ref, at, STATE)
        scores[g] = lax.dot_general(
            c_maps[g], b_maps[g], (((1,), (1,)), ((), ())), preferred_element_type=jnp.float32
        )

    def spread(per_head, start):
        head = lax.broadcasted_iota(jnp.int32, (heads, tile), 0) * HEAD_DIM
        lane = lax.broadcasted_iota(jnp.int32, (heads, tile), 1) + start
        chosen = ((lane >= head) & (lane < head + HEAD_DIM)).astype(jnp.float32)
        return jnp.dot(
            per_head, chosen, precision=exact, preferred_element_type=jnp.float32
        )

    cum = cum_ref[...]
    end_weight = jnp.exp(cum[length - 1 : length] - cum) * step_ref[...]
    grown = jnp.exp(cum)

    def states(c, carry):
        start = pl.multiple_of(c * tile, tile)
        span = pl.ds(start, tile)
        value = conv(x_ref, rim_x, taps_ref, base_ref, start, tile)
        values[:, span] = value
        weighted = (value.astype(jnp.float32) * spread(end_weight, start)).astype(jnp.bfloat16)
        g = lax.div(start, group_width)
        local[c] = lax.dot_general(
            b_maps[g], weighted, (((0,), (0,)), ((), ())), preferred_element_type=jnp.float32
        )
        return carry

    lax.fori_loop(0, tiles, states, 0)

    def chain_copy(c):
        return pltpu.make_async_remote_copy(
            src_ref=leaving.at[c],
            dst_ref=arrived.at[c],
            send_sem=chain_send.at[c],
            recv_sem=chain_recv.at[c],
            device_id=(me + 1, z),
            device_id_type=mesh_ids,
        )

    def link(c, carry):
        span = pl.ds(pl.multiple_of(c * tile, tile), tile)

        @pl.when(has_left)
        def _():
            chain_copy(c).wait_recv()

        @pl.when(jnp.logical_not(has_left))
        def _():
            arrived[c] = jnp.zeros_like(arrived[c])

        @pl.when(has_right)
        def _():
            leaving[c] = (
                decay_ref[:, span] * arrived[c].astype(jnp.float32) + local[c]
            ).astype(jnp.bfloat16)
            chain_copy(c).start()

        return carry

    pair = 2 * HEAD_DIM
    causal = lax.broadcasted_iota(jnp.int32, (length, length), 0) >= lax.broadcasted_iota(
        jnp.int32, (length, length), 1
    )

    def within(q, carry):
        span = pl.ds(pl.multiple_of(q * pair, pair), pair)
        value = values[:, span]
        g = lax.div(q * pair, group_width)
        sums = []
        for e in range(2):
            h = 2 * q + e
            lane = lax.broadcasted_iota(jnp.int32, (length, heads), 1)
            column = jnp.sum(jnp.where(lane == h, cum_ref[...], 0.0), axis=1, keepdims=True)
            gap = column - cum_t_ref[pl.ds(h, 1), :]
            kernel = jnp.where(causal, jnp.exp(jnp.where(causal, gap, 0.0)), 0.0)
            mixing = kernel * scores[g] * step_t_ref[pl.ds(h, 1), :]
            sums.append(
                jnp.dot(mixing.astype(jnp.bfloat16), value, preferred_element_type=jnp.float32)
            )
        first = lax.broadcasted_iota(jnp.int32, (length, pair), 1) < HEAD_DIM
        y[:, span] = jnp.where(first, sums[0], sums[1])
        return carry

    late = me >= n // 2

    def phase(turn, carry):
        @pl.when((turn == 0) == late)
        def _():
            lax.fori_loop(0, channels // pair, within, 0)

        @pl.when(turn == 0)
        def _():
            lax.fori_loop(0, tiles, link, 0)

        return carry

    lax.fori_loop(0, 2, phase, 0)

    for g in range(groups_here):
        per = group_width // tile

        def gated(c, squares):
            c = c + g * per
            start = pl.multiple_of(c * tile, tile)
            span = pl.ds(start, tile)
            carried = jnp.dot(
                c_maps[g], arrived[c], preferred_element_type=jnp.float32
            ) * spread(grown, start)
            total = y[:, span] + carried + skip_ref[:, span] * values[:, span].astype(jnp.float32)
            total = total * jax.nn.silu(gate_ref[:, span].astype(jnp.float32))
            y[:, span] = total
            return squares + jnp.sum(total * total, axis=1, keepdims=True)

        squares = lax.fori_loop(0, per, gated, jnp.zeros((length, 1), jnp.float32))
        scale = lax.rsqrt(squares / group_width + 1e-05)

        def scaled(c, carry):
            span = pl.ds(pl.multiple_of((c + g * per) * tile, tile), tile)
            if whole_groups:
                out_ref[:, span] = (y[:, span] * scale * gain_ref[:, span]).astype(out_ref.dtype)
            else:
                out_ref[:, span] = y[:, span]
            return carry

        lax.fori_loop(0, per, scaled, 0)

    @pl.when(has_right)
    def _():
        for which in range(2):
            rim_copy(which).wait_send()

        def sent(c, carry):
            chain_copy(c).wait_send()
            return carry

        lax.fori_loop(0, tiles, sent, 0)


def front(x, gate, maps, cum, step, skip, taps, base, map_taps, map_base, gain, whole_groups):
    n = lax.axis_size("seq")
    length, channels = x.shape
    heads = cum.shape[1]
    per_group = HEADS // GROUPS
    groups_here = max(1, heads // per_group)
    tile = max(128, channels // 8)
    tiles = channels // tile
    rim = 16
    bf16, f32 = jnp.bfloat16, jnp.float32
    dma = pltpu.SemaphoreType.DMA
    vmem = pl.BlockSpec(memory_space=pltpu.VMEM)
    decay = jnp.repeat(jnp.exp(cum[-1]), HEAD_DIM)[None]
    skips = jnp.repeat(skip, HEAD_DIM)[None]
    operands = (
        x, gate, maps, cum, cum.T, step, step.T, decay, skips,
        taps, base[None], map_taps, map_base[None], gain[None],
    )
    return pl.pallas_call(
        functools.partial(front_kernel, n, per_group, whole_groups),
        out_shape=jax.ShapeDtypeStruct((length, channels), bf16 if whole_groups else f32),
        in_specs=[vmem] * len(operands),
        out_specs=vmem,
        scratch_shapes=[
            pltpu.VMEM((rim, channels), bf16),
            pltpu.VMEM((rim, maps.shape[1]), bf16),
            pltpu.VMEM((rim + length, max(tile, STATE)), f32),
            pltpu.VMEM((length, channels), bf16),
            pltpu.VMEM((length, channels), f32),
            pltpu.VMEM((groups_here, length, STATE), bf16),
            pltpu.VMEM((groups_here, length, STATE), bf16),
            pltpu.VMEM((groups_here, length, length), f32),
            pltpu.VMEM((tiles, STATE, tile), f32),
            pltpu.VMEM((tiles, STATE, tile), bf16),
            pltpu.VMEM((tiles, STATE, tile), bf16),
            dma((2,)),
            dma((2,)),
            dma((tiles,)),
            dma((tiles,)),
        ],
        compiler_params=pltpu.CompilerParams(
            collective_id=1, has_side_effects=True, vmem_limit_bytes=48 << 20
        ),
    )(*operands)


LOG2E = 1.4426950408889634


def three(value):
    high = value.astype(jnp.bfloat16)
    rest = value - high.astype(jnp.float32)
    middle = rest.astype(jnp.bfloat16)
    low = (rest - middle.astype(jnp.float32)).astype(jnp.bfloat16)
    return high, middle, low


def layer_kernel(
    n, m, per_group, x_hbm, gate_hbm, maps_hbm, step_hbm, rate_hbm, skip_hbm, taps_hbm, base_hbm,
    map_taps_hbm, map_base_hbm, gain_hbm, w_hbm, out_ref,
    x_ref, gate_ref, maps_ref, step_ref, rate_ref, skip_ref, taps_ref, base_ref, map_taps_ref,
    map_base_ref, gain_ref, w_ref, in_sem,
    rim_x, rim_maps, pad, values, maps_conv, y, scores, local, state, arrived, leaving,
    gap_left, gap_right, turned_maps, ends, growth, own_end, all_ends, chosen, channel_rows, prefix_rows,
    gat, part, up, down,
    rim_send, rim_recv, end_send, end_recv, chain_send, chain_recv, forward_send,
    gat_send, gat_recv, up_send, up_recv, down_send, down_recv, out_send, out_recv,
    own_sem,
):
    mesh_ids = pl.DeviceIdType.MESH
    exact = lax.Precision.HIGHEST
    f32, bf16 = jnp.float32, jnp.bfloat16
    me, z = lax.axis_index("seq"), lax.axis_index("tp")
    chips = n // 2
    chip, core = lax.div(me, 2), lax.rem(me, 2)
    partner = me + 1 - 2 * core
    length, channels = x_ref.shape
    heads = step_ref.shape[0]
    levels = arrived.shape[0]
    groups_here = scores.shape[0]
    first_group = z * groups_here
    span_maps = groups_here * STATE
    tile = arrived.shape[3]
    tiles = channels // tile
    group_width = channels // groups_here
    rim = rim_x.shape[0]
    width = w_ref.shape[1]
    rows = length // m
    half = length // 2

    at_b = pl.ds(pl.multiple_of(first_group * STATE, STATE), span_maps)
    at_c = pl.ds(pl.multiple_of((GROUPS + first_group) * STATE, STATE), span_maps)
    to_b, to_c = pl.ds(0, span_maps), pl.ds(span_maps, span_maps)
    fetches = (
        (step_hbm, step_ref),
        (rate_hbm, rate_ref),
        (skip_hbm, skip_ref),
        (maps_hbm.at[:, at_b], maps_ref.at[:, to_b]),
        (maps_hbm.at[:, at_c], maps_ref.at[:, to_c]),
        (map_taps_hbm.at[:, at_b], map_taps_ref.at[:, to_b]),
        (map_taps_hbm.at[:, at_c], map_taps_ref.at[:, to_c]),
        (map_base_hbm.at[:, at_b], map_base_ref.at[:, to_b]),
        (map_base_hbm.at[:, at_c], map_base_ref.at[:, to_c]),
        (taps_hbm, taps_ref),
        (base_hbm, base_ref),
        (x_hbm, x_ref),
        (gate_hbm, gate_ref),
        (gain_hbm, gain_ref),
        (w_hbm, w_ref),
    )
    loads = [
        pltpu.make_async_copy(source, target, in_sem.at[i])
        for i, (source, target) in enumerate(fetches)
    ]

    barrier = pltpu.get_barrier_semaphore()

    def greet(step, carry):
        pl.semaphore_signal(
            barrier, inc=1, device_id=(lax.rem(me + step, n), z), device_id_type=mesh_ids
        )
        return carry

    lax.fori_loop(1, n, greet, 0)

    @pl.when(z > 0)
    def _():
        pl.semaphore_signal(barrier, inc=1, device_id=(me, z - 1), device_id_type=mesh_ids)

    @pl.when(z < m - 1)
    def _():
        pl.semaphore_signal(barrier, inc=1, device_id=(me, z + 1), device_id_type=mesh_ids)

    for load in loads[:12]:
        load.start()

    has_left, has_right = me > 0, me < n - 1
    odd = core == 1

    for load in loads[:3]:
        load.wait()

    def turned(value):
        size = value.shape[0]
        same = lax.broadcasted_iota(jnp.int32, (size, size), 0) == lax.broadcasted_iota(
            jnp.int32, (size, size), 1
        )
        return lax.dot_general(
            value, same.astype(f32), (((0,), (0,)), ((), ())), precision=exact,
            preferred_element_type=f32,
        )

    step = jax.nn.softplus(turned(step_ref[...]))
    log_decay = -jnp.exp(rate_ref[...]) * step
    row = lax.broadcasted_iota(jnp.int32, (length, length), 0)
    column = lax.broadcasted_iota(jnp.int32, (length, length), 1)
    lower = (row >= column).astype(f32)
    cum = jnp.dot(lower, log_decay, precision=exact, preferred_element_type=f32)
    final = cum[length - 1 : length]
    ones = jnp.ones((length, heads), bf16)
    blank = jnp.zeros((length, heads), bf16)
    gap_left[...] = jnp.concatenate(
        [*three(cum * LOG2E), ones, ones, ones, blank, blank], axis=1
    )
    source_log = jnp.log(step) * LOG2E - cum * LOG2E
    source_rows = turned(source_log)
    unit = jnp.ones((heads, length), bf16)
    gap_right[...] = jnp.concatenate(
        [unit, unit, unit, *three(source_rows), unit, unit], axis=0
    )
    ends[...] = jnp.concatenate([*three(jnp.exp(final - cum) * step), blank], axis=1)
    growth[...] = jnp.concatenate([*three(jnp.exp(cum)), blank], axis=1)
    lanes = own_end.shape[1]
    own_end[...] = jnp.zeros_like(own_end)
    own_end[:, 0:heads] = jnp.broadcast_to(final, (8, heads))
    all_ends[me] = jnp.zeros((8, lanes), f32)

    first_row = lax.broadcasted_iota(jnp.int32, (16, heads), 0) < 8
    two = jnp.where(first_row, jnp.exp(final), skip_ref[...])
    two = jnp.concatenate([*three(two), jnp.zeros((16, heads), bf16)], axis=1)

    def choose(c, carry):
        start = pl.multiple_of(c * tile, tile)
        slot = lax.broadcasted_iota(jnp.int32, (4 * heads, tile), 0)
        head = lax.rem(slot, heads) * HEAD_DIM
        lane = lax.broadcasted_iota(jnp.int32, (4 * heads, tile), 1) + start
        chosen[:, pl.ds(start, tile)] = (
            ((lane >= head) & (lane < head + HEAD_DIM)).astype(f32).astype(bf16)
        )
        return carry

    lax.fori_loop(0, tiles, choose, 0)

    def spread(per_head, span):
        return jnp.dot(per_head, chosen[:, span], preferred_element_type=f32)

    channel_rows[...] = spread(two, slice(None))
    for load in loads[3:9]:
        load.wait()

    def smooth(rows_ref, taps, base, out, start, size):
        span = pl.ds(start, size)
        pad[:, 0:size] = rows_ref[:, span].astype(f32)
        total = base[:, span]
        for k in range(CONV):
            at = rim - (CONV - 1) + k
            total = total + taps[k : k + 1, span] * pad[at : at + length - rim, 0:size]
        out[rim:length, span] = jax.nn.silu(total).astype(bf16)

    for c in range(0, 2 * span_maps, tile):
        smooth(maps_ref, map_taps_ref, map_base_ref, maps_conv, c, tile)

    beside = (z > 0).astype(jnp.int32) + (z < m - 1).astype(jnp.int32)
    pl.semaphore_wait(barrier, n - 1 + beside)

    last_rows = pl.ds(length - rim, rim)

    def rim_copy(which):
        source, target = (
            (x_hbm.at[last_rows], rim_x),
            (maps_hbm.at[last_rows, at_b], rim_maps.at[:, to_b]),
            (maps_hbm.at[last_rows, at_c], rim_maps.at[:, to_c]),
        )[which]
        return pltpu.make_async_remote_copy(
            src_ref=source,
            dst_ref=target,
            send_sem=rim_send.at[which],
            recv_sem=rim_recv.at[which],
            device_id=(me + 1, z),
            device_id_type=mesh_ids,
        )

    @pl.when(has_right)
    def _():
        for which in range(3):
            rim_copy(which).start()

    def end_copy(offset, sender):
        return pltpu.make_async_remote_copy(
            src_ref=own_end,
            dst_ref=all_ends.at[sender],
            send_sem=end_send.at[offset],
            recv_sem=end_recv.at[sender],
            device_id=(lax.rem(me + offset, n), z),
            device_id_type=mesh_ids,
        )

    def send_end(offset, carry):
        end_copy(offset, me).start()
        return carry

    lax.fori_loop(1, n, send_end, 0)

    for load in loads[9:12]:
        load.wait()
    for load in loads[12:]:
        load.start()

    def smooth_rim(rows_ref, rim_ref, taps, base, out, start, size):
        span = pl.ds(start, size)
        pad[0:rim, 0:size] = rim_ref[:, span].astype(f32)
        pad[rim : 2 * rim, 0:size] = rows_ref[0:rim, span].astype(f32)
        total = base[:, span]
        for k in range(CONV):
            at = rim - (CONV - 1) + k
            total = total + taps[k : k + 1, span] * pad[at : at + rim, 0:size]
        out[0:rim, span] = jax.nn.silu(total).astype(bf16)

    def smooth_tile(c, carry):
        smooth(x_ref, taps_ref, base_ref, values, pl.multiple_of(c * tile, tile), tile)
        return carry

    lax.fori_loop(0, tiles, smooth_tile, 0)

    def chain_send_copy(level, hop, c):
        return pltpu.make_async_remote_copy(
            src_ref=leaving.at[c],
            dst_ref=arrived.at[level, c],
            send_sem=chain_send.at[hop, c],
            recv_sem=chain_recv.at[level, c],
            device_id=(me + 1 if level == 0 else me + 2 * (hop + 1), z),
            device_id_type=mesh_ids,
        )

    def chain_forward(level, c):
        return pltpu.make_async_remote_copy(
            src_ref=arrived.at[level, c],
            dst_ref=arrived.at[level, c],
            send_sem=forward_send.at[level, c],
            recv_sem=chain_recv.at[level, c],
            device_id=(partner, z),
            device_id_type=mesh_ids,
        )

    def hops(level):
        return range(max(1, 2**level // 2))

    def sends(level):
        return lax.rem(me, 2 ** (level + 1)) == 2**level - 1

    def gets(level):
        return lax.rem(lax.div(me, 2**level), 2) == 1

    per = group_width // tile

    maps_conv[0:rim] = jnp.zeros((rim, 2 * span_maps), bf16)
    values[0:rim] = jnp.zeros((rim, channels), bf16)

    for g in range(groups_here):
        turned_maps[g] = turned(
            maps_conv[:, g * STATE : (g + 1) * STATE].astype(f32)
        ).astype(bf16)

    for g in range(groups_here):
        mine = range(g * per, (g + 1) * per)
        spans = [slice(c * tile, (c + 1) * tile) for c in mine]
        weighted = [
            (values[:, span].astype(f32) * spread(ends[...], span)).astype(bf16)
            for span in spans
        ]
        for c, w in zip(mine, weighted):
            local[c] = jnp.dot(turned_maps[g], w, preferred_element_type=f32)

    @pl.when(has_left)
    def _():
        for which in range(3):
            rim_copy(which).wait_recv()

    @pl.when(jnp.logical_not(has_left))
    def _():
        rim_x[...] = jnp.zeros_like(rim_x)
        rim_maps[...] = jnp.zeros_like(rim_maps)

    for c in range(0, 2 * span_maps, tile):
        smooth_rim(maps_ref, rim_maps, map_taps_ref, map_base_ref, maps_conv, c, tile)
    for c in range(0, channels, tile):
        smooth_rim(x_ref, rim_x, taps_ref, base_ref, values, c, tile)

    for g in range(groups_here):
        mine = range(g * per, (g + 1) * per)
        spans = [slice(c * tile, (c + 1) * tile) for c in mine]
        first_maps = maps_conv[0:rim, g * STATE : (g + 1) * STATE]
        weighted = [
            (values[0:rim, span].astype(f32) * spread(ends[0:rim], span)).astype(bf16)
            for span in spans
        ]
        for c, w in zip(mine, weighted):
            total = local[c] + lax.dot_general(
                first_maps, w, (((0,), (0,)), ((), ())), preferred_element_type=f32
            )
            local[c] = total
            state[c] = jnp.zeros_like(total)
            leaving[c] = total.astype(bf16)

        @pl.when(sends(0))
        def _():
            for c in mine:
                chain_send_copy(0, 0, c).start()

    def link(level, c):
        span = pl.ds(pl.multiple_of(c * tile, tile), tile)

        @pl.when(gets(level))
        def _():
            chain_forward(level, c).wait_recv()
            if level == 0:
                state[c] = arrived[level, c].astype(f32)
            else:
                @pl.when(odd)
                def _():
                    chain_forward(level, c).start()

                state[c] = state[c] + prefix_rows[level, 0:1, span] * arrived[level, c].astype(f32)

        if level + 1 < levels:
            @pl.when(sends(level + 1))
            def _():
                leaving[c] = (channel_rows[0:1, span] * state[c] + local[c]).astype(bf16)
                for hop in hops(level + 1):
                    chain_send_copy(level + 1, hop, c).start()

    def link_all(level, first, last):
        def body(c, carry):
            link(level, c)
            return carry

        lax.fori_loop(first, last, body, 0)

    link_all(0, 0, tiles)

    for g in range(groups_here):
        scores[g] = lax.dot_general(
            maps_conv[:, span_maps + g * STATE : span_maps + (g + 1) * STATE],
            maps_conv[:, g * STATE : (g + 1) * STATE],
            (((1,), (1,)), ((), ())),
            preferred_element_type=f32,
        )

    def get_end(offset, carry):
        end_copy(offset, lax.rem(me + offset, n)).wait_recv()
        return carry

    lax.fori_loop(1, n, get_end, 0)

    for level in range(1, levels):
        base = me - lax.rem(me, 2**level)
        total = jnp.zeros((8, lanes), f32)
        for i in range(n):
            total = total + jnp.where((base <= i) & (i < me), all_ends[i], 0.0)
        passed = jnp.exp(total[:, 0:heads])
        passed = jnp.concatenate([passed, passed], axis=0)
        passed = jnp.concatenate([*three(passed), jnp.zeros((16, heads), bf16)], axis=1)

        prefix_rows[level] = spread(passed, slice(None))

    pair = 2 * HEAD_DIM
    lane = lax.broadcasted_iota(jnp.int32, (half, pair), 1)
    batch = 4

    def mask_of(head):
        slot = lax.broadcasted_iota(jnp.int32, (1, 8 * heads), 1)
        return ((lax.rem(slot, heads) == head) & (slot < 6 * heads)).astype(f32).astype(bf16)

    def within(turn, carry):
        g = lax.div(turn * batch * pair, group_width)
        gaps = []
        for e in range(2 * batch):
            left = gap_left[...] * mask_of(2 * batch * turn + e)
            gaps.append((
                jnp.dot(left[0:half], gap_right[:, 0:half], preferred_element_type=f32),
                jnp.dot(left[half:length], gap_right[...], preferred_element_type=f32),
            ))
        causal = lax.broadcasted_iota(jnp.int32, (half, half), 0) >= lax.broadcasted_iota(
            jnp.int32, (half, half), 1
        )
        causal_late = lax.broadcasted_iota(jnp.int32, (half, length), 0) + half >= (
            lax.broadcasted_iota(jnp.int32, (half, length), 1)
        )
        mixing = [
            (
                (jnp.where(causal, jnp.exp2(a), 0.0) * scores[g, 0:half, 0:half]).astype(bf16),
                (jnp.where(causal_late, jnp.exp2(b), 0.0) * scores[g, half:length]).astype(bf16),
            )
            for a, b in gaps
        ]
        for q in range(batch):
            span = pl.ds(pl.multiple_of((turn * batch + q) * pair, pair), pair)
            early, late = [], []
            for a, b in mixing[2 * q : 2 * q + 2]:
                early.append(jnp.dot(a, values[0:half, span], preferred_element_type=f32))
                late.append(jnp.dot(b, values[:, span], preferred_element_type=f32))
            y[0:half, span] = jnp.where(lane < HEAD_DIM, early[0], early[1])
            y[half:length, span] = jnp.where(lane < HEAD_DIM, late[0], late[1])
        return carry

    batches = channels // (pair * batch)
    share = tiles // batches

    def within_level(turn, carry):
        for c in range(share):
            if levels > 2:
                link(1, turn * share + c)
        return within(turn, carry)

    lax.fori_loop(0, batches, within_level, 0)

    for level in range(2, levels - 1):
        link_all(level, 0, tiles)

    for load in loads[12:14]:
        load.wait()

    def partner_copy(slot, g):
        return pltpu.make_async_remote_copy(
            src_ref=gat.at[slot - 1, g],
            dst_ref=gat.at[slot, g],
            send_sem=gat_send.at[slot, g],
            recv_sem=gat_recv.at[slot, g],
            device_id=(partner, z),
            device_id_type=mesh_ids,
        )

    def source_mask(i, who):
        swap = (who == 1) & (chips >= 4)
        return i + jnp.where(swap & (i == 1), 1, 0) - jnp.where(swap & (i == 2), 1, 0)

    def chip_at(mask):
        there, bit = chip, 1
        while bit < chips:
            on = lax.rem(lax.div(mask, bit), 2)
            there = there + on * (bit - 2 * bit * lax.rem(lax.div(chip, bit), 2))
            bit *= 2
        return there

    def across_copy(i, g):
        return pltpu.make_async_remote_copy(
            src_ref=gat.at[0, g],
            dst_ref=gat.at[2 * i, g],
            send_sem=gat_send.at[2 * i, g],
            recv_sem=gat_recv.at[2 * i, g],
            device_id=(2 * chip_at(source_mask(i, core)) + core, z),
            device_id_type=mesh_ids,
        )

    relayed = chips == 4

    def relay_copy(slot, g):
        mask = source_mask(lax.div(slot, 2), core)
        return pltpu.make_async_remote_copy(
            src_ref=gat.at[slot, g],
            dst_ref=gat.at[6, g],
            send_sem=gat_send.at[6, g],
            recv_sem=gat_recv.at[6, g],
            device_id=(2 * chip_at(3 - mask) + core, z),
            device_id_type=mesh_ids,
        )

    def arrival(slot, g):
        return pltpu.make_async_remote_copy(
            src_ref=gat.at[slot, g],
            dst_ref=gat.at[slot, g],
            send_sem=gat_send.at[slot, g],
            recv_sem=gat_recv.at[slot, g],
            device_id=(partner, z),
            device_id_type=mesh_ids,
        )

    for g in range(groups_here):
        mine = range(g * per, (g + 1) * per)
        spans = [slice(c * tile, (c + 1) * tile) for c in mine]
        output_map = maps_conv[:, span_maps + g * STATE : span_maps + (g + 1) * STATE]
        squares = jnp.zeros((length, 128), f32)
        for first in range(0, per, 2):
            link_all(levels - 1, g * per + first, g * per + first + 2)
            carried = [
                jnp.dot(output_map, state[c].astype(bf16), preferred_element_type=f32)
                for c in mine[first : first + 2]
            ]
            grown = [spread(growth[...], span) for span in spans[first : first + 2]]
            for span, more, scale in zip(spans[first : first + 2], carried, grown):
                total = y[:, span] + more * scale
                total = total + channel_rows[8:9, span] * values[:, span].astype(f32)
                total = total * jax.nn.silu(gate_ref[:, span].astype(f32))
                y[:, span] = total
                for d in range(0, tile, 128):
                    squares = squares + total[:, d : d + 128] * total[:, d : d + 128]
        scale = lax.rsqrt(jnp.sum(squares, axis=1, keepdims=True) / group_width + 1e-05)
        for c, span in enumerate(spans):
            gat[0, g, :, c * tile : (c + 1) * tile] = (
                y[:, span] * scale * gain_ref[:, span]
            ).astype(bf16)
        partner_copy(1, g).start()
        if chips > 1:
            across_copy(1, g).start()

    def chain_z(step, j, buffer, send, recv, to):
        return pltpu.make_async_remote_copy(
            src_ref=part.at[step, pl.ds(j * rows, rows)],
            dst_ref=buffer.at[step, pl.ds(j * rows, rows)],
            send_sem=send.at[step, j],
            recv_sem=recv.at[step, j],
            device_id=(me, to),
            device_id_type=mesh_ids,
        )

    def owner(step):
        who = core + lax.rem(step, 2) * (1 - 2 * core)
        return 2 * chip_at(source_mask(lax.div(step, 2), who)) + who

    def columns(sender):
        return pl.ds(pl.multiple_of(sender * width, width), width)

    def own_rows():
        return pl.ds(pl.multiple_of(z * rows, rows), rows)

    def out_copy(step, sender):
        return pltpu.make_async_remote_copy(
            src_ref=part.at[step, own_rows()],
            dst_ref=out_ref.at[:, columns(sender)],
            send_sem=out_send.at[step],
            recv_sem=out_recv.at[sender],
            device_id=(owner(step), z),
            device_id_type=mesh_ids,
        )

    def own_copy():
        return pltpu.make_async_copy(part.at[0, own_rows()], out_ref.at[:, columns(me)], own_sem)

    def added(step, j, buffer):
        span = pl.ds(j * rows, rows)
        part[step, span] = (
            part[step, span].astype(f32) + buffer[step, span].astype(f32)
        ).astype(bf16)

    up_lag, down_lag = z, m - 1 - z
    last_lag = jnp.maximum(up_lag, down_lag)
    wide = min(width, 256)

    loads[14].wait()

    def turn(tau, carry):
        @pl.when(tau < n)
        def _():
            slot = tau
            direct = (slot > 0) & (lax.rem(slot, 2) == 0)

            @pl.when(direct)
            def _():
                for g in range(groups_here):
                    arrival(slot, g).wait_send()

            @pl.when(direct & (slot < (4 if relayed else n - 2)))
            def _():
                for g in range(groups_here):
                    across_copy(lax.div(slot, 2) + 1, g).start()

            @pl.when(tau > 0)
            def _():
                for g in range(groups_here):
                    arrival(slot, g).wait_recv()

            @pl.when(direct)
            def _():
                for g in range(groups_here):
                    partner_copy(slot + 1, g).start()

            if relayed:
                @pl.when((slot == 3) | (slot == 5))
                def _():
                    along = source_mask(lax.div(slot, 2), core) == 1
                    for g in range(groups_here):
                        @pl.when(along == (g < (groups_here + 1) // 2))
                        def _():
                            relay_copy(slot - 1, g).start()

            for c in range(0, width, wide):
                total = jnp.zeros((length, wide), f32)
                for g in range(groups_here):
                    total = total + jnp.dot(
                        gat[slot, g],
                        w_ref[g * group_width : (g + 1) * group_width, c : c + wide],
                        preferred_element_type=f32,
                    )
                part[tau, :, c : c + wide] = total.astype(bf16)

        t_up = tau - up_lag

        @pl.when((t_up >= 0) & (t_up < n))
        def _():
            for j in range(m - 1, 0, -1):
                @pl.when(z < j)
                def _():
                    copy = chain_z(t_up, j, up, up_send, up_recv, z + 1)

                    @pl.when(z > 0)
                    def _():
                        copy.wait_recv()
                        added(t_up, j, up)

                    if j == 1:
                        @pl.when(t_up == n - 1)
                        def _():
                            chain_z(n - 2, j, up, up_send, up_recv, z + 1).start()

                        @pl.when(t_up != n - 2)
                        def _():
                            copy.start()
                    else:
                        copy.start()

        t_down = tau - down_lag

        @pl.when((t_down >= 0) & (t_down < n))
        def _():
            for j in range(m - 1):
                @pl.when(z > j)
                def _():
                    copy = chain_z(t_down, j, down, down_send, down_recv, z - 1)

                    @pl.when(z < m - 1)
                    def _():
                        copy.wait_recv()
                        added(t_down, j, down)

                    if j == m - 2:
                        @pl.when(t_down == n - 1)
                        def _():
                            chain_z(n - 2, j, down, down_send, down_recv, z - 1).start()

                        @pl.when(t_down != n - 2)
                        def _():
                            copy.start()
                    else:
                        copy.start()

        t_last = tau - last_lag

        @pl.when((t_last >= 0) & (t_last < n))
        def _():
            for j in range(m):
                @pl.when(z == j)
                def _():
                    span = pl.ds(j * rows, rows)
                    total = part[t_last, span].astype(f32)
                    if j > 0:
                        chain_z(t_last, j, up, up_send, up_recv, z).wait_recv()
                        total = total + up[t_last, span].astype(f32)
                    if j < m - 1:
                        chain_z(t_last, j, down, down_send, down_recv, z).wait_recv()
                        total = total + down[t_last, span].astype(f32)
                    part[t_last, span] = total.astype(bf16)

            @pl.when(t_last == 0)
            def _():
                own_copy().start()

            @pl.when(t_last > 0)
            def _():
                out_copy(t_last, me).start()

        return carry

    lax.fori_loop(0, n + m - 1, turn, 0)

    def finish(step, carry):
        @pl.when(lax.rem(step, 2) == 1)
        def _():
            for g in range(groups_here):
                arrival(step, g).wait_send()

        @pl.when(step > 0)
        def _():
            end_copy(step, me).wait_send()

        for j in range(m):
            @pl.when(z < j)
            def _():
                chain_z(step, j, up, up_send, up_recv, z).wait_send()

            @pl.when(z > j)
            def _():
                chain_z(step, j, down, down_send, down_recv, z).wait_send()

        @pl.when(step > 0)
        def _():
            out_copy(step, me).wait_send()
            out_copy(step, lax.rem(me + step, n)).wait_recv()

        return carry

    lax.fori_loop(0, n, finish, 0)
    own_copy().wait()

    @pl.when(has_right)
    def _():
        for which in range(3):
            rim_copy(which).wait_send()

    def sent(c, carry):
        for level in range(levels):
            @pl.when(sends(level))
            def _():
                for hop in hops(level):
                    chain_send_copy(level, hop, c).wait_send()

            if level > 0:
                @pl.when(gets(level) & odd)
                def _():
                    chain_forward(level, c).wait_send()

        return carry

    lax.fori_loop(0, tiles, sent, 0)


def layer(x, gate, maps, step_raw, rate, skip, taps, base, map_taps, map_base, gain, weight):
    n, m = lax.axis_size("seq"), lax.axis_size("tp")
    length, channels = x.shape
    heads = rate.shape[0]
    per_group = HEADS // GROUPS
    groups_here = heads // per_group
    tile = max(128, channels // 8)
    tiles = channels // tile
    width = weight.shape[1]
    span_maps = 2 * groups_here * STATE
    rim = 16
    levels = n.bit_length() - 1
    lanes = -(-heads // 128) * 128
    bf16, f32 = jnp.bfloat16, jnp.float32
    dma = pltpu.SemaphoreType.DMA
    operands = (
        x, gate, maps, step_raw.T, rate[None], skip[None], taps, base[None],
        map_taps, map_base[None], gain[None], weight,
    )
    blocks = pltpu.VMEM((n, length, width), bf16)
    return pl.pallas_call(
        functools.partial(layer_kernel, n, m, per_group),
        out_shape=jax.ShapeDtypeStruct((length // m, n * width), bf16),
        in_specs=[pl.BlockSpec(memory_space=pl.ANY)] * len(operands),
        out_specs=pl.BlockSpec(memory_space=pl.ANY),
        scratch_shapes=[
            pltpu.VMEM((length, channels), bf16),
            pltpu.VMEM((length, channels), bf16),
            pltpu.VMEM((length, span_maps), bf16),
            pltpu.VMEM((heads, length), f32),
            pltpu.VMEM((1, heads), f32),
            pltpu.VMEM((1, heads), f32),
            pltpu.VMEM((CONV, channels), f32),
            pltpu.VMEM((1, channels), f32),
            pltpu.VMEM((CONV, span_maps), f32),
            pltpu.VMEM((1, span_maps), f32),
            pltpu.VMEM((1, channels), f32),
            pltpu.VMEM(weight.shape, bf16),
            dma((15,)),
            pltpu.VMEM((rim, channels), bf16),
            pltpu.VMEM((rim, span_maps), bf16),
            pltpu.VMEM((length, max(tile, STATE)), f32),
            pltpu.VMEM((length, channels), bf16),
            pltpu.VMEM((length, span_maps), bf16),
            pltpu.VMEM((length, channels), f32),
            pltpu.VMEM((groups_here, length, length), f32),
            pltpu.VMEM((tiles, STATE, tile), f32),
            pltpu.VMEM((tiles, STATE, tile), f32),
            pltpu.VMEM((levels, tiles, STATE, tile), bf16),
            pltpu.VMEM((tiles, STATE, tile), bf16),
            pltpu.VMEM((length, 8 * heads), bf16),
            pltpu.VMEM((8 * heads, length), bf16),
            pltpu.VMEM((groups_here, STATE, length), bf16),
            pltpu.VMEM((length, 4 * heads), bf16),
            pltpu.VMEM((length, 4 * heads), bf16),
            pltpu.VMEM((8, lanes), f32),
            pltpu.VMEM((n, 8, lanes), f32),
            pltpu.VMEM((4 * heads, channels), bf16),
            pltpu.VMEM((16, channels), f32),
            pltpu.VMEM((levels, 16, channels), f32),
            pltpu.VMEM((n, groups_here, length, channels // groups_here), bf16),
            blocks,
            blocks,
            blocks,
            dma((3,)),
            dma((3,)),
            dma((n,)),
            dma((n,)),
            dma((max(1, n // 4), tiles)),
            dma((levels, tiles)),
            dma((levels, tiles)),
            dma((n, groups_here)),
            dma((n, groups_here)),
            dma((n, m)),
            dma((n, m)),
            dma((n, m)),
            dma((n, m)),
            dma((n,)),
            dma((n,)),
            dma(()),
        ],
        compiler_params=pltpu.CompilerParams(
            collective_id=2, has_side_effects=True, vmem_limit_bytes=60 << 20
        ),
        cost_estimate=pl.CostEstimate(
            flops=2 * n * length * channels * width,
            bytes_accessed=2 * (channels * width + 3 * length * channels),
            transcendentals=0,
        ),
    )(*operands)


def shards(
    conv_values,
    gate_values,
    conv_maps,
    step_raw,
    decay_log,
    skip_gain,
    values_kernel,
    values_offset,
    maps_kernel,
    maps_offset,
    norm_weight,
    out_weight,
    residual,
):
    length = conv_values.shape[0]
    heads_dev = decay_log.shape[0]
    per_group = HEADS // GROUPS
    whole_groups = heads_dev % per_group == 0
    chips = lax.axis_size("seq") // 2
    paired = lax.axis_size("seq") == 2 * chips and chips & (chips - 1) == 0
    if whole_groups and paired and heads_dev % 32 == 0:
        summed = layer(
            conv_values, gate_values, conv_maps, step_raw, decay_log, skip_gain, values_kernel,
            values_offset, maps_kernel, maps_offset, norm_weight, out_weight,
        )
        return residual.astype(jnp.float32) + summed.astype(jnp.float32)
    step_size = jax.nn.softplus(step_raw)
    place = jnp.arange(length, dtype=jnp.int32)
    cum_log = jnp.dot(
        (place[:, None] >= place[None, :]).astype(jnp.float32),
        -jnp.exp(decay_log)[None, :] * step_size,
        precision=lax.Precision.HIGHEST,
    )
    normed = front(
        conv_values, gate_values, conv_maps, cum_log, step_size, skip_gain, values_kernel,
        values_offset, maps_kernel, maps_offset, norm_weight, whole_groups,
    )
    if not whole_groups:
        gated_out = normed.reshape(length, heads_dev, HEAD_DIM)
        head_squares = jnp.sum(gated_out * gated_out, axis=2)
        all_heads = lax.all_gather(head_squares, "tp", axis=1, tiled=True)
        group_totals = jnp.sum(all_heads.reshape(length, GROUPS, per_group), axis=2)
        heads_here = lax.axis_index("tp") * heads_dev + jnp.arange(heads_dev, dtype=jnp.int32)
        inv_rms = lax.rsqrt(
            group_totals[:, heads_here // per_group] / (per_group * HEAD_DIM) + 1e-05
        )
        normed = (
            (gated_out * inv_rms[:, :, None]).reshape(length, heads_dev * HEAD_DIM)
            * norm_weight[None, :]
        ).astype(jnp.bfloat16)
    blocks = mix(normed, out_weight)
    summed = jnp.transpose(blocks, (1, 0, 2)).reshape(residual.shape).astype(jnp.float32)
    return residual.astype(jnp.float32) + summed


def solution(mesh):
    placed = (
        P("seq", "tp"),
        P("seq", "tp"),
        P("seq", None),
        P("seq", "tp"),
        P("tp"),
        P("tp"),
        P(None, "tp"),
        P("tp"),
        P(),
        P(),
        P("tp"),
        P("tp", "seq"),
        P(("seq", "tp"), None),
    )
    return jax.shard_map(
        shards, mesh=mesh, in_specs=placed, out_specs=P(("seq", "tp"), None), check_vma=False
    )
```

```python
import functools

import jax
import jax.numpy as jnp
from jax import lax
from jax.experimental import pallas as pl
from jax.experimental.pallas import tpu as pltpu
from jax.sharding import PartitionSpec as P

HEADS = 128
HEAD_DIM = 64
STATE = 128
GROUPS = 8
CONV = 4


def ring_place(spot, size):
    if size % 4:
        return spot
    half = size // 2
    past = spot - half
    turned = half + (half - 2 - 2 * lax.div(past, 2)) + lax.rem(past, 2)
    return jnp.where(spot < half, spot, turned)


def mix_kernel(
    n, m, x_ref, w_ref, out_ref, gat, part, up, down,
    own_sem, gat_send, gat_recv, up_send, up_recv, down_send, down_recv, out_send, out_recv,
):
    mesh_ids = pl.DeviceIdType.MESH
    me, z = lax.axis_index("seq"), lax.axis_index("tp")
    spot = ring_place(me, n)
    right = ring_place(lax.rem(spot + 1, n), n)
    left = ring_place(lax.rem(spot + n - 1, n), n)
    half = gat.shape[2]
    depth = gat.shape[3]
    width = w_ref.shape[1]
    rows = part.shape[1] // m
    tile = min(width, 256)

    own = [
        pltpu.make_async_copy(x_ref.at[pl.ds(d * half, half)], gat.at[0, d], own_sem.at[d])
        for d in range(2)
    ]
    for copy in own:
        copy.start()

    barrier = pltpu.get_barrier_semaphore()

    def greet(step, carry):
        pl.semaphore_signal(
            barrier, inc=1, device_id=(lax.rem(me + step, n), z), device_id_type=mesh_ids
        )
        return carry

    lax.fori_loop(1, n, greet, 0)

    @pl.when(z > 0)
    def _():
        pl.semaphore_signal(barrier, inc=1, device_id=(me, z - 1), device_id_type=mesh_ids)

    @pl.when(z < m - 1)
    def _():
        pl.semaphore_signal(barrier, inc=1, device_id=(me, z + 1), device_id_type=mesh_ids)

    beside = (z > 0).astype(jnp.int32) + (z < m - 1).astype(jnp.int32)
    pl.semaphore_wait(barrier, n - 1 + beside)

    for copy in own:
        copy.wait()

    def gather_copy(step, d):
        return pltpu.make_async_remote_copy(
            src_ref=gat.at[step, d],
            dst_ref=gat.at[step + 1, d],
            send_sem=gat_send.at[step, d],
            recv_sem=gat_recv.at[step + 1, d],
            device_id=(right if d == 0 else left, z),
            device_id_type=mesh_ids,
        )

    def gather_arrival(step, d):
        return pltpu.make_async_remote_copy(
            src_ref=gat.at[step, d],
            dst_ref=gat.at[step, d],
            send_sem=gat_send.at[step, d],
            recv_sem=gat_recv.at[step, d],
            device_id=(right if d == 0 else left, z),
            device_id_type=mesh_ids,
        )

    def chain_copy(step, j, buffer, send, recv, to):
        return pltpu.make_async_remote_copy(
            src_ref=part.at[step, pl.ds(j * rows, rows)],
            dst_ref=buffer.at[step, pl.ds(j * rows, rows)],
            send_sem=send.at[step, j],
            recv_sem=recv.at[step, j],
            device_id=(me, to),
            device_id_type=mesh_ids,
        )

    def owner(step):
        there = jnp.where(z < m // 2, spot - step + n, spot + step)
        return ring_place(lax.rem(there, n), n)

    def out_copy(step, sender):
        return pltpu.make_async_remote_copy(
            src_ref=part.at[step, pl.ds(pl.multiple_of(z * rows, rows), rows)],
            dst_ref=out_ref.at[sender],
            send_sem=out_send.at[step],
            recv_sem=out_recv.at[sender],
            device_id=(owner(step), z),
            device_id_type=mesh_ids,
        )

    def added(step, j, buffer):
        span = pl.ds(j * rows, rows)
        part[step, span] = (
            part[step, span].astype(jnp.float32) + buffer[step, span].astype(jnp.float32)
        ).astype(jnp.bfloat16)

    up_lag, down_lag = z, m - 1 - z
    last_lag = jnp.maximum(up_lag, down_lag)

    def turn(tau, carry):
        @pl.when(tau < n)
        def _():
            @pl.when(tau > 0)
            def _():
                for d in range(2):
                    gather_arrival(tau, d).wait_recv()

            @pl.when(tau < n - 1)
            def _():
                for d in range(2):
                    gather_copy(tau, d).start()

            block = gat[tau].reshape(2 * half, depth)
            for c in range(0, width, tile):
                part[tau, :, c : c + tile] = jnp.dot(
                    block, w_ref[:, c : c + tile], preferred_element_type=jnp.float32
                ).astype(jnp.bfloat16)

        t_up = tau - up_lag

        @pl.when((t_up >= 0) & (t_up < n))
        def _():
            for j in range(m - 1, 0, -1):
                @pl.when(z < j)
                def _():
                    copy = chain_copy(t_up, j, up, up_send, up_recv, z + 1)

                    @pl.when(z > 0)
                    def _():
                        copy.wait_recv()
                        added(t_up, j, up)

                    copy.start()

        t_down = tau - down_lag

        @pl.when((t_down >= 0) & (t_down < n))
        def _():
            for j in range(m - 1):
                @pl.when(z > j)
                def _():
                    copy = chain_copy(t_down, j, down, down_send, down_recv, z - 1)

                    @pl.when(z < m - 1)
                    def _():
                        copy.wait_recv()
                        added(t_down, j, down)

                    copy.start()

        t_last = tau - last_lag

        @pl.when((t_last >= 0) & (t_last < n))
        def _():
            for j in range(m):
                @pl.when(z == j)
                def _():
                    span = pl.ds(j * rows, rows)
                    total = part[t_last, span].astype(jnp.float32)
                    if j > 0:
                        chain_copy(t_last, j, up, up_send, up_recv, z).wait_recv()
                        total = total + up[t_last, span].astype(jnp.float32)
                    if j < m - 1:
                        chain_copy(t_last, j, down, down_send, down_recv, z).wait_recv()
                        total = total + down[t_last, span].astype(jnp.float32)
                    part[t_last, span] = total.astype(jnp.bfloat16)

            @pl.when(t_last == 0)
            def _():
                out_ref[me] = part[0, pl.ds(pl.multiple_of(z * rows, rows), rows)]

            @pl.when(t_last > 0)
            def _():
                out_copy(t_last, me).start()

        return carry

    lax.fori_loop(0, n + m - 1, turn, 0)

    def finish(step, carry):
        @pl.when(step < n - 1)
        def _():
            for d in range(2):
                gather_copy(step, d).wait_send()

        for j in range(m):
            @pl.when(z < j)
            def _():
                chain_copy(step, j, up, up_send, up_recv, z).wait_send()

            @pl.when(z > j)
            def _():
                chain_copy(step, j, down, down_send, down_recv, z).wait_send()

        @pl.when(step > 0)
        def _():
            out_copy(step, me).wait_send()
            out_copy(step, lax.rem(me + step, n)).wait_recv()

        return carry

    lax.fori_loop(0, n, finish, 0)


def mix(normed, weight):
    n, m = lax.axis_size("seq"), lax.axis_size("tp")
    length, depth = normed.shape
    width = weight.shape[1]
    rows = length // m
    half = length // 2
    slots = pltpu.VMEM((n, length, width), jnp.bfloat16)
    dma = pltpu.SemaphoreType.DMA
    vmem = pl.BlockSpec(memory_space=pltpu.VMEM)
    return pl.pallas_call(
        functools.partial(mix_kernel, n, m),
        out_shape=jax.ShapeDtypeStruct((n, rows, width), jnp.bfloat16),
        in_specs=[pl.BlockSpec(memory_space=pl.ANY), vmem],
        out_specs=vmem,
        scratch_shapes=[
            pltpu.VMEM((n, 2, half, depth), jnp.bfloat16),
            slots,
            slots,
            slots,
            dma((2,)),
            dma((n, 2)),
            dma((n, 2)),
            dma((n, m)),
            dma((n, m)),
            dma((n, m)),
            dma((n, m)),
            dma((n,)),
            dma((n,)),
        ],
        compiler_params=pltpu.CompilerParams(
            collective_id=0, has_side_effects=True, vmem_limit_bytes=48 << 20
        ),
        cost_estimate=pl.CostEstimate(
            flops=2 * n * length * depth * width,
            bytes_accessed=2 * (depth * width + length * depth),
            transcendentals=0,
        ),
    )(normed, weight)


def front_kernel(
    n, per_group, whole_groups, x_ref, gate_ref, maps_ref, cum_ref, cum_t_ref, step_ref, step_t_ref,
    decay_ref, skip_ref, taps_ref, base_ref, map_taps_ref, map_base_ref, gain_ref, out_ref,
    rim_x, rim_maps, pad, values, y, b_maps, c_maps, scores, local, arrived, leaving,
    rim_send, rim_recv, chain_send, chain_recv,
):
    mesh_ids = pl.DeviceIdType.MESH
    exact = lax.Precision.HIGHEST
    me, z = lax.axis_index("seq"), lax.axis_index("tp")
    length, channels = x_ref.shape
    heads = cum_ref.shape[1]
    groups_here = scores.shape[0]
    first_group = lax.div(z * heads, per_group)
    tile = arrived.shape[2]
    tiles = channels // tile
    group_width = channels // groups_here
    rim = rim_x.shape[0]

    barrier = pltpu.get_barrier_semaphore()
    has_left, has_right = me > 0, me < n - 1

    @pl.when(has_left)
    def _():
        pl.semaphore_signal(barrier, inc=1, device_id=(me - 1, z), device_id_type=mesh_ids)

    @pl.when(has_right)
    def _():
        pl.semaphore_signal(barrier, inc=1, device_id=(me + 1, z), device_id_type=mesh_ids)

    pl.semaphore_wait(barrier, has_left.astype(jnp.int32) + has_right.astype(jnp.int32))

    def rim_copy(which):
        source, target = ((x_ref, rim_x), (maps_ref, rim_maps))[which]
        return pltpu.make_async_remote_copy(
            src_ref=source.at[pl.ds(length - rim, rim)],
            dst_ref=target,
            send_sem=rim_send.at[which],
            recv_sem=rim_recv.at[which],
            device_id=(me + 1, z),
            device_id_type=mesh_ids,
        )

    @pl.when(has_right)
    def _():
        for which in range(2):
            rim_copy(which).start()

    @pl.when(has_left)
    def _():
        for which in range(2):
            rim_copy(which).wait_recv()

    @pl.when(jnp.logical_not(has_left))
    def _():
        rim_x[...] = jnp.zeros_like(rim_x)
        rim_maps[...] = jnp.zeros_like(rim_maps)

    def conv(rows_ref, rim_ref, taps, base, start, size):
        span = pl.ds(start, size)
        pad[0:rim, 0:size] = rim_ref[:, span].astype(jnp.float32)
        pad[rim : rim + length, 0:size] = rows_ref[:, span].astype(jnp.float32)
        total = base[:, span]
        for k in range(CONV):
            at = rim - (CONV - 1) + k
            total = total + taps[k : k + 1, span] * pad[at : at + length, 0:size]
        return jax.nn.silu(total).astype(jnp.bfloat16)

    for g in range(groups_here):
        at = pl.multiple_of((first_group + g) * STATE, STATE)
        b_maps[g] = conv(maps_ref, rim_maps, map_taps_ref, map_base_ref, at, STATE)
        at = pl.multiple_of((GROUPS + first_group + g) * STATE, STATE)
        c_maps[g] = conv(maps_ref, rim_maps, map_taps_ref, map_base_ref, at, STATE)
        scores[g] = lax.dot_general(
            c_maps[g], b_maps[g], (((1,), (1,)), ((), ())), preferred_element_type=jnp.float32
        )

    def spread(per_head, start):
        head = lax.broadcasted_iota(jnp.int32, (heads, tile), 0) * HEAD_DIM
        lane = lax.broadcasted_iota(jnp.int32, (heads, tile), 1) + start
        chosen = ((lane >= head) & (lane < head + HEAD_DIM)).astype(jnp.float32)
        return jnp.dot(
            per_head, chosen, precision=exact, preferred_element_type=jnp.float32
        )

    cum = cum_ref[...]
    end_weight = jnp.exp(cum[length - 1 : length] - cum) * step_ref[...]
    grown = jnp.exp(cum)

    def states(c, carry):
        start = pl.multiple_of(c * tile, tile)
        span = pl.ds(start, tile)
        value = conv(x_ref, rim_x, taps_ref, base_ref, start, tile)
        values[:, span] = value
        weighted = (value.astype(jnp.float32) * spread(end_weight, start)).astype(jnp.bfloat16)
        g = lax.div(start, group_width)
        local[c] = lax.dot_general(
            b_maps[g], weighted, (((0,), (0,)), ((), ())), preferred_element_type=jnp.float32
        )
        return carry

    lax.fori_loop(0, tiles, states, 0)

    def chain_copy(c):
        return pltpu.make_async_remote_copy(
            src_ref=leaving.at[c],
            dst_ref=arrived.at[c],
            send_sem=chain_send.at[c],
            recv_sem=chain_recv.at[c],
            device_id=(me + 1, z),
            device_id_type=mesh_ids,
        )

    def link(c, carry):
        span = pl.ds(pl.multiple_of(c * tile, tile), tile)

        @pl.when(has_left)
        def _():
            chain_copy(c).wait_recv()

        @pl.when(jnp.logical_not(has_left))
        def _():
            arrived[c] = jnp.zeros_like(arrived[c])

        @pl.when(has_right)
        def _():
            leaving[c] = (
                decay_ref[:, span] * arrived[c].astype(jnp.float32) + local[c]
            ).astype(jnp.bfloat16)
            chain_copy(c).start()

        return carry

    pair = 2 * HEAD_DIM
    causal = lax.broadcasted_iota(jnp.int32, (length, length), 0) >= lax.broadcasted_iota(
        jnp.int32, (length, length), 1
    )

    def within(q, carry):
        span = pl.ds(pl.multiple_of(q * pair, pair), pair)
        value = values[:, span]
        g = lax.div(q * pair, group_width)
        sums = []
        for e in range(2):
            h = 2 * q + e
            lane = lax.broadcasted_iota(jnp.int32, (length, heads), 1)
            column = jnp.sum(jnp.where(lane == h, cum_ref[...], 0.0), axis=1, keepdims=True)
            gap = column - cum_t_ref[pl.ds(h, 1), :]
            kernel = jnp.where(causal, jnp.exp(jnp.where(causal, gap, 0.0)), 0.0)
            mixing = kernel * scores[g] * step_t_ref[pl.ds(h, 1), :]
            sums.append(
                jnp.dot(mixing.astype(jnp.bfloat16), value, preferred_element_type=jnp.float32)
            )
        first = lax.broadcasted_iota(jnp.int32, (length, pair), 1) < HEAD_DIM
        y[:, span] = jnp.where(first, sums[0], sums[1])
        return carry

    late = me >= n // 2

    def phase(turn, carry):
        @pl.when((turn == 0) == late)
        def _():
            lax.fori_loop(0, channels // pair, within, 0)

        @pl.when(turn == 0)
        def _():
            lax.fori_loop(0, tiles, link, 0)

        return carry

    lax.fori_loop(0, 2, phase, 0)

    for g in range(groups_here):
        per = group_width // tile

        def gated(c, squares):
            c = c + g * per
            start = pl.multiple_of(c * tile, tile)
            span = pl.ds(start, tile)
            carried = jnp.dot(
                c_maps[g], arrived[c], preferred_element_type=jnp.float32
            ) * spread(grown, start)
            total = y[:, span] + carried + skip_ref[:, span] * values[:, span].astype(jnp.float32)
            total = total * jax.nn.silu(gate_ref[:, span].astype(jnp.float32))
            y[:, span] = total
            return squares + jnp.sum(total * total, axis=1, keepdims=True)

        squares = lax.fori_loop(0, per, gated, jnp.zeros((length, 1), jnp.float32))
        scale = lax.rsqrt(squares / group_width + 1e-05)

        def scaled(c, carry):
            span = pl.ds(pl.multiple_of((c + g * per) * tile, tile), tile)
            if whole_groups:
                out_ref[:, span] = (y[:, span] * scale * gain_ref[:, span]).astype(out_ref.dtype)
            else:
                out_ref[:, span] = y[:, span]
            return carry

        lax.fori_loop(0, per, scaled, 0)

    @pl.when(has_right)
    def _():
        for which in range(2):
            rim_copy(which).wait_send()

        def sent(c, carry):
            chain_copy(c).wait_send()
            return carry

        lax.fori_loop(0, tiles, sent, 0)


def front(x, gate, maps, cum, step, skip, taps, base, map_taps, map_base, gain, whole_groups):
    n = lax.axis_size("seq")
    length, channels = x.shape
    heads = cum.shape[1]
    per_group = HEADS // GROUPS
    groups_here = max(1, heads // per_group)
    tile = max(128, channels // 8)
    tiles = channels // tile
    rim = 16
    bf16, f32 = jnp.bfloat16, jnp.float32
    dma = pltpu.SemaphoreType.DMA
    vmem = pl.BlockSpec(memory_space=pltpu.VMEM)
    decay = jnp.repeat(jnp.exp(cum[-1]), HEAD_DIM)[None]
    skips = jnp.repeat(skip, HEAD_DIM)[None]
    operands = (
        x, gate, maps, cum, cum.T, step, step.T, decay, skips,
        taps, base[None], map_taps, map_base[None], gain[None],
    )
    return pl.pallas_call(
        functools.partial(front_kernel, n, per_group, whole_groups),
        out_shape=jax.ShapeDtypeStruct((length, channels), bf16 if whole_groups else f32),
        in_specs=[vmem] * len(operands),
        out_specs=vmem,
        scratch_shapes=[
            pltpu.VMEM((rim, channels), bf16),
            pltpu.VMEM((rim, maps.shape[1]), bf16),
            pltpu.VMEM((rim + length, max(tile, STATE)), f32),
            pltpu.VMEM((length, channels), bf16),
            pltpu.VMEM((length, channels), f32),
            pltpu.VMEM((groups_here, length, STATE), bf16),
            pltpu.VMEM((groups_here, length, STATE), bf16),
            pltpu.VMEM((groups_here, length, length), f32),
            pltpu.VMEM((tiles, STATE, tile), f32),
            pltpu.VMEM((tiles, STATE, tile), bf16),
            pltpu.VMEM((tiles, STATE, tile), bf16),
            dma((2,)),
            dma((2,)),
            dma((tiles,)),
            dma((tiles,)),
        ],
        compiler_params=pltpu.CompilerParams(
            collective_id=1, has_side_effects=True, vmem_limit_bytes=48 << 20
        ),
    )(*operands)


LOG2E = 1.4426950408889634


def three(value):
    high = value.astype(jnp.bfloat16)
    rest = value - high.astype(jnp.float32)
    middle = rest.astype(jnp.bfloat16)
    low = (rest - middle.astype(jnp.float32)).astype(jnp.bfloat16)
    return high, middle, low


def layer_kernel(
    n, m, per_group, x_hbm, gate_hbm, maps_hbm, step_hbm, rate_hbm, skip_hbm, taps_hbm, base_hbm,
    map_taps_hbm, map_base_hbm, gain_hbm, w_hbm, out_ref,
    x_ref, gate_ref, maps_ref, step_ref, rate_ref, skip_ref, taps_ref, base_ref, map_taps_ref,
    map_base_ref, gain_ref, w_ref, in_sem,
    rim_x, rim_maps, pad, values, maps_conv, y, scores, local, state, arrived, leaving,
    gap_left, gap_right, turned_maps, ends, growth, own_end, all_ends, chosen, channel_rows, prefix_rows,
    gat, part, up, down,
    rim_send, rim_recv, end_send, end_recv, chain_send, chain_recv, forward_send,
    gat_send, gat_recv, up_send, up_recv, down_send, down_recv, out_send, out_recv,
    own_sem,
):
    mesh_ids = pl.DeviceIdType.MESH
    exact = lax.Precision.HIGHEST
    f32, bf16 = jnp.float32, jnp.bfloat16
    me, z = lax.axis_index("seq"), lax.axis_index("tp")
    chips = n // 2
    chip, core = lax.div(me, 2), lax.rem(me, 2)
    partner = me + 1 - 2 * core
    length, channels = x_ref.shape
    heads = step_ref.shape[0]
    levels = arrived.shape[0]
    groups_here = scores.shape[0]
    first_group = z * groups_here
    span_maps = groups_here * STATE
    tile = arrived.shape[3]
    tiles = channels // tile
    group_width = channels // groups_here
    rim = rim_x.shape[0]
    width = w_ref.shape[1]
    rows = length // m
    half = length // 2

    at_b = pl.ds(pl.multiple_of(first_group * STATE, STATE), span_maps)
    at_c = pl.ds(pl.multiple_of((GROUPS + first_group) * STATE, STATE), span_maps)
    to_b, to_c = pl.ds(0, span_maps), pl.ds(span_maps, span_maps)
    fetches = (
        (step_hbm, step_ref),
        (rate_hbm, rate_ref),
        (skip_hbm, skip_ref),
        (maps_hbm.at[:, at_b], maps_ref.at[:, to_b]),
        (maps_hbm.at[:, at_c], maps_ref.at[:, to_c]),
        (map_taps_hbm.at[:, at_b], map_taps_ref.at[:, to_b]),
        (map_taps_hbm.at[:, at_c], map_taps_ref.at[:, to_c]),
        (map_base_hbm.at[:, at_b], map_base_ref.at[:, to_b]),
        (map_base_hbm.at[:, at_c], map_base_ref.at[:, to_c]),
        (taps_hbm, taps_ref),
        (base_hbm, base_ref),
        (x_hbm, x_ref),
        (gate_hbm, gate_ref),
        (gain_hbm, gain_ref),
        (w_hbm, w_ref),
    )
    loads = [
        pltpu.make_async_copy(source, target, in_sem.at[i])
        for i, (source, target) in enumerate(fetches)
    ]

    barrier = pltpu.get_barrier_semaphore()

    def greet(step, carry):
        pl.semaphore_signal(
            barrier, inc=1, device_id=(lax.rem(me + step, n), z), device_id_type=mesh_ids
        )
        return carry

    lax.fori_loop(1, n, greet, 0)

    @pl.when(z > 0)
    def _():
        pl.semaphore_signal(barrier, inc=1, device_id=(me, z - 1), device_id_type=mesh_ids)

    @pl.when(z < m - 1)
    def _():
        pl.semaphore_signal(barrier, inc=1, device_id=(me, z + 1), device_id_type=mesh_ids)

    for load in loads[:12]:
        load.start()

    has_left, has_right = me > 0, me < n - 1
    odd = core == 1

    for load in loads[:3]:
        load.wait()

    def turned(value):
        size = value.shape[0]
        same = lax.broadcasted_iota(jnp.int32, (size, size), 0) == lax.broadcasted_iota(
            jnp.int32, (size, size), 1
        )
        return lax.dot_general(
            value, same.astype(f32), (((0,), (0,)), ((), ())), precision=exact,
            preferred_element_type=f32,
        )

    step = jax.nn.softplus(turned(step_ref[...]))
    log_decay = -jnp.exp(rate_ref[...]) * step
    row = lax.broadcasted_iota(jnp.int32, (length, length), 0)
    column = lax.broadcasted_iota(jnp.int32, (length, length), 1)
    lower = (row >= column).astype(f32)
    cum = jnp.dot(lower, log_decay, precision=exact, preferred_element_type=f32)
    final = cum[length - 1 : length]
    ones = jnp.ones((length, heads), bf16)
    blank = jnp.zeros((length, heads), bf16)
    gap_left[...] = jnp.concatenate(
        [*three(cum * LOG2E), ones, ones, ones, blank, blank], axis=1
    )
    source_log = jnp.log(step) * LOG2E - cum * LOG2E
    source_rows = turned(source_log)
    unit = jnp.ones((heads, length), bf16)
    gap_right[...] = jnp.concatenate(
        [unit, unit, unit, *three(source_rows), unit, unit], axis=0
    )
    ends[...] = jnp.concatenate([*three(jnp.exp(final - cum) * step), blank], axis=1)
    growth[...] = jnp.concatenate([*three(jnp.exp(cum)), blank], axis=1)
    lanes = own_end.shape[1]
    own_end[...] = jnp.zeros_like(own_end)
    own_end[:, 0:heads] = jnp.broadcast_to(final, (8, heads))
    all_ends[me] = jnp.zeros((8, lanes), f32)

    first_row = lax.broadcasted_iota(jnp.int32, (16, heads), 0) < 8
    two = jnp.where(first_row, jnp.exp(final), skip_ref[...])
    two = jnp.concatenate([*three(two), jnp.zeros((16, heads), bf16)], axis=1)

    def choose(c, carry):
        start = pl.multiple_of(c * tile, tile)
        slot = lax.broadcasted_iota(jnp.int32, (4 * heads, tile), 0)
        head = lax.rem(slot, heads) * HEAD_DIM
        lane = lax.broadcasted_iota(jnp.int32, (4 * heads, tile), 1) + start
        chosen[:, pl.ds(start, tile)] = (
            ((lane >= head) & (lane < head + HEAD_DIM)).astype(f32).astype(bf16)
        )
        return carry

    lax.fori_loop(0, tiles, choose, 0)

    def spread(per_head, span):
        return jnp.dot(per_head, chosen[:, span], preferred_element_type=f32)

    channel_rows[...] = spread(two, slice(None))
    for load in loads[3:9]:
        load.wait()

    def smooth(rows_ref, taps, base, out, start, size):
        span = pl.ds(start, size)
        pad[:, 0:size] = rows_ref[:, span].astype(f32)
        total = base[:, span]
        for k in range(CONV):
            at = rim - (CONV - 1) + k
            total = total + taps[k : k + 1, span] * pad[at : at + length - rim, 0:size]
        out[rim:length, span] = jax.nn.silu(total).astype(bf16)

    for c in range(0, 2 * span_maps, tile):
        smooth(maps_ref, map_taps_ref, map_base_ref, maps_conv, c, tile)

    beside = (z > 0).astype(jnp.int32) + (z < m - 1).astype(jnp.int32)
    pl.semaphore_wait(barrier, n - 1 + beside)

    last_rows = pl.ds(length - rim, rim)

    def rim_copy(which):
        source, target = (
            (x_hbm.at[last_rows], rim_x),
            (maps_hbm.at[last_rows, at_b], rim_maps.at[:, to_b]),
            (maps_hbm.at[last_rows, at_c], rim_maps.at[:, to_c]),
        )[which]
        return pltpu.make_async_remote_copy(
            src_ref=source,
            dst_ref=target,
            send_sem=rim_send.at[which],
            recv_sem=rim_recv.at[which],
            device_id=(me + 1, z),
            device_id_type=mesh_ids,
        )

    @pl.when(has_right)
    def _():
        for which in range(3):
            rim_copy(which).start()

    def end_copy(offset, sender):
        return pltpu.make_async_remote_copy(
            src_ref=own_end,
            dst_ref=all_ends.at[sender],
            send_sem=end_send.at[offset],
            recv_sem=end_recv.at[sender],
            device_id=(lax.rem(me + offset, n), z),
            device_id_type=mesh_ids,
        )

    def send_end(offset, carry):
        end_copy(offset, me).start()
        return carry

    lax.fori_loop(1, n, send_end, 0)

    for load in loads[9:12]:
        load.wait()
    for load in loads[12:]:
        load.start()

    def smooth_rim(rows_ref, rim_ref, taps, base, out, start, size):
        span = pl.ds(start, size)
        pad[0:rim, 0:size] = rim_ref[:, span].astype(f32)
        pad[rim : 2 * rim, 0:size] = rows_ref[0:rim, span].astype(f32)
        total = base[:, span]
        for k in range(CONV):
            at = rim - (CONV - 1) + k
            total = total + taps[k : k + 1, span] * pad[at : at + rim, 0:size]
        out[0:rim, span] = jax.nn.silu(total).astype(bf16)

    def smooth_tile(c, carry):
        smooth(x_ref, taps_ref, base_ref, values, pl.multiple_of(c * tile, tile), tile)
        return carry

    lax.fori_loop(0, tiles, smooth_tile, 0)

    def chain_send_copy(level, hop, c):
        return pltpu.make_async_remote_copy(
            src_ref=leaving.at[c],
            dst_ref=arrived.at[level, c],
            send_sem=chain_send.at[hop, c],
            recv_sem=chain_recv.at[level, c],
            device_id=(me + 1 if level == 0 else me + 2 * (hop + 1), z),
            device_id_type=mesh_ids,
        )

    def chain_forward(level, c):
        return pltpu.make_async_remote_copy(
            src_ref=arrived.at[level, c],
            dst_ref=arrived.at[level, c],
            send_sem=forward_send.at[level, c],
            recv_sem=chain_recv.at[level, c],
            device_id=(partner, z),
            device_id_type=mesh_ids,
        )

    def hops(level):
        return range(max(1, 2**level // 2))

    def sends(level):
        return lax.rem(me, 2 ** (level + 1)) == 2**level - 1

    def gets(level):
        return lax.rem(lax.div(me, 2**level), 2) == 1

    per = group_width // tile

    maps_conv[0:rim] = jnp.zeros((rim, 2 * span_maps), bf16)
    values[0:rim] = jnp.zeros((rim, channels), bf16)

    for g in range(groups_here):
        turned_maps[g] = turned(
            maps_conv[:, g * STATE : (g + 1) * STATE].astype(f32)
        ).astype(bf16)

    for g in range(groups_here):
        mine = range(g * per, (g + 1) * per)
        spans = [slice(c * tile, (c + 1) * tile) for c in mine]
        weighted = [
            (values[:, span].astype(f32) * spread(ends[...], span)).astype(bf16)
            for span in spans
        ]
        for c, w in zip(mine, weighted):
            local[c] = jnp.dot(turned_maps[g], w, preferred_element_type=f32)

    @pl.when(has_left)
    def _():
        for which in range(3):
            rim_copy(which).wait_recv()

    @pl.when(jnp.logical_not(has_left))
    def _():
        rim_x[...] = jnp.zeros_like(rim_x)
        rim_maps[...] = jnp.zeros_like(rim_maps)

    for c in range(0, 2 * span_maps, tile):
        smooth_rim(maps_ref, rim_maps, map_taps_ref, map_base_ref, maps_conv, c, tile)
    for c in range(0, channels, tile):
        smooth_rim(x_ref, rim_x, taps_ref, base_ref, values, c, tile)

    for g in range(groups_here):
        mine = range(g * per, (g + 1) * per)
        spans = [slice(c * tile, (c + 1) * tile) for c in mine]
        first_maps = maps_conv[0:rim, g * STATE : (g + 1) * STATE]
        weighted = [
            (values[0:rim, span].astype(f32) * spread(ends[0:rim], span)).astype(bf16)
            for span in spans
        ]
        for c, w in zip(mine, weighted):
            total = local[c] + lax.dot_general(
                first_maps, w, (((0,), (0,)), ((), ())), preferred_element_type=f32
            )
            local[c] = total
            state[c] = jnp.zeros_like(total)
            leaving[c] = total.astype(bf16)

        @pl.when(sends(0))
        def _():
            for c in mine:
                chain_send_copy(0, 0, c).start()

    def link(level, c):
        span = pl.ds(pl.multiple_of(c * tile, tile), tile)

        @pl.when(gets(level))
        def _():
            chain_forward(level, c).wait_recv()
            if level == 0:
                state[c] = arrived[level, c].astype(f32)
            else:
                @pl.when(odd)
                def _():
                    chain_forward(level, c).start()

                state[c] = state[c] + prefix_rows[level, 0:1, span] * arrived[level, c].astype(f32)

        if level + 1 < levels:
            @pl.when(sends(level + 1))
            def _():
                leaving[c] = (channel_rows[0:1, span] * state[c] + local[c]).astype(bf16)
                for hop in hops(level + 1):
                    chain_send_copy(level + 1, hop, c).start()

    def link_all(level, first, last):
        def body(c, carry):
            link(level, c)
            return carry

        lax.fori_loop(first, last, body, 0)

    link_all(0, 0, tiles)

    for g in range(groups_here):
        scores[g] = lax.dot_general(
            maps_conv[:, span_maps + g * STATE : span_maps + (g + 1) * STATE],
            maps_conv[:, g * STATE : (g + 1) * STATE],
            (((1,), (1,)), ((), ())),
            preferred_element_type=f32,
        )

    def get_end(offset, carry):
        end_copy(offset, lax.rem(me + offset, n)).wait_recv()
        return carry

    lax.fori_loop(1, n, get_end, 0)

    for level in range(1, levels):
        base = me - lax.rem(me, 2**level)
        total = jnp.zeros((8, lanes), f32)
        for i in range(n):
            total = total + jnp.where((base <= i) & (i < me), all_ends[i], 0.0)
        passed = jnp.exp(total[:, 0:heads])
        passed = jnp.concatenate([passed, passed], axis=0)
        passed = jnp.concatenate([*three(passed), jnp.zeros((16, heads), bf16)], axis=1)

        prefix_rows[level] = spread(passed, slice(None))

    pair = 2 * HEAD_DIM
    lane = lax.broadcasted_iota(jnp.int32, (half, pair), 1)
    batch = 4

    def mask_of(head):
        slot = lax.broadcasted_iota(jnp.int32, (1, 8 * heads), 1)
        return ((lax.rem(slot, heads) == head) & (slot < 6 * heads)).astype(f32).astype(bf16)

    def within(turn, carry):
        g = lax.div(turn * batch * pair, group_width)
        gaps = []
        for e in range(2 * batch):
            left = gap_left[...] * mask_of(2 * batch * turn + e)
            gaps.append((
                jnp.dot(left[0:half], gap_right[:, 0:half], preferred_element_type=f32),
                jnp.dot(left[half:length], gap_right[...], preferred_element_type=f32),
            ))
        causal = lax.broadcasted_iota(jnp.int32, (half, half), 0) >= lax.broadcasted_iota(
            jnp.int32, (half, half), 1
        )
        causal_late = lax.broadcasted_iota(jnp.int32, (half, length), 0) + half >= (
            lax.broadcasted_iota(jnp.int32, (half, length), 1)
        )
        mixing = [
            (
                (jnp.where(causal, jnp.exp2(a), 0.0) * scores[g, 0:half, 0:half]).astype(bf16),
                (jnp.where(causal_late, jnp.exp2(b), 0.0) * scores[g, half:length]).astype(bf16),
            )
            for a, b in gaps
        ]
        for q in range(batch):
            span = pl.ds(pl.multiple_of((turn * batch + q) * pair, pair), pair)
            early, late = [], []
            for a, b in mixing[2 * q : 2 * q + 2]:
                early.append(jnp.dot(a, values[0:half, span], preferred_element_type=f32))
                late.append(jnp.dot(b, values[:, span], preferred_element_type=f32))
            y[0:half, span] = jnp.where(lane < HEAD_DIM, early[0], early[1])
            y[half:length, span] = jnp.where(lane < HEAD_DIM, late[0], late[1])
        return carry

    batches = channels // (pair * batch)
    share = tiles // batches

    def within_level(turn, carry):
        for c in range(share):
            if levels > 2:
                link(1, turn * share + c)
        return within(turn, carry)

    lax.fori_loop(0, batches, within_level, 0)

    for level in range(2, levels - 1):
        link_all(level, 0, tiles)

    for load in loads[12:14]:
        load.wait()

    def partner_copy(slot, g):
        return pltpu.make_async_remote_copy(
            src_ref=gat.at[slot - 1, g],
            dst_ref=gat.at[slot, g],
            send_sem=gat_send.at[slot, g],
            recv_sem=gat_recv.at[slot, g],
            device_id=(partner, z),
            device_id_type=mesh_ids,
        )

    def source_mask(i, who):
        swap = (who == 1) & (chips >= 4)
        return i + jnp.where(swap & (i == 1), 1, 0) - jnp.where(swap & (i == 2), 1, 0)

    def chip_at(mask):
        there, bit = chip, 1
        while bit < chips:
            on = lax.rem(lax.div(mask, bit), 2)
            there = there + on * (bit - 2 * bit * lax.rem(lax.div(chip, bit), 2))
            bit *= 2
        return there

    def across_copy(i, g):
        return pltpu.make_async_remote_copy(
            src_ref=gat.at[0, g],
            dst_ref=gat.at[2 * i, g],
            send_sem=gat_send.at[2 * i, g],
            recv_sem=gat_recv.at[2 * i, g],
            device_id=(2 * chip_at(source_mask(i, core)) + core, z),
            device_id_type=mesh_ids,
        )

    relayed = chips == 4

    def relay_copy(slot, g):
        mask = source_mask(lax.div(slot, 2), core)
        return pltpu.make_async_remote_copy(
            src_ref=gat.at[slot, g],
            dst_ref=gat.at[6, g],
            send_sem=gat_send.at[6, g],
            recv_sem=gat_recv.at[6, g],
            device_id=(2 * chip_at(3 - mask) + core, z),
            device_id_type=mesh_ids,
        )

    def arrival(slot, g):
        return pltpu.make_async_remote_copy(
            src_ref=gat.at[slot, g],
            dst_ref=gat.at[slot, g],
            send_sem=gat_send.at[slot, g],
            recv_sem=gat_recv.at[slot, g],
            device_id=(partner, z),
            device_id_type=mesh_ids,
        )

    for g in range(groups_here):
        mine = range(g * per, (g + 1) * per)
        spans = [slice(c * tile, (c + 1) * tile) for c in mine]
        output_map = maps_conv[:, span_maps + g * STATE : span_maps + (g + 1) * STATE]
        squares = jnp.zeros((length, 128), f32)
        for first in range(0, per, 2):
            link_all(levels - 1, g * per + first, g * per + first + 2)
            carried = [
                jnp.dot(output_map, state[c].astype(bf16), preferred_element_type=f32)
                for c in mine[first : first + 2]
            ]
            grown = [spread(growth[...], span) for span in spans[first : first + 2]]
            for span, more, scale in zip(spans[first : first + 2], carried, grown):
                total = y[:, span] + more * scale
                total = total + channel_rows[8:9, span] * values[:, span].astype(f32)
                total = total * jax.nn.silu(gate_ref[:, span].astype(f32))
                y[:, span] = total
                for d in range(0, tile, 128):
                    squares = squares + total[:, d : d + 128] * total[:, d : d + 128]
        scale = lax.rsqrt(jnp.sum(squares, axis=1, keepdims=True) / group_width + 1e-05)
        for c, span in enumerate(spans):
            gat[0, g, :, c * tile : (c + 1) * tile] = (
                y[:, span] * scale * gain_ref[:, span]
            ).astype(bf16)
        partner_copy(1, g).start()
        if chips > 1:
            across_copy(1, g).start()

    def chain_z(step, j, buffer, send, recv, to):
        return pltpu.make_async_remote_copy(
            src_ref=part.at[step, pl.ds(j * rows, rows)],
            dst_ref=buffer.at[step, pl.ds(j * rows, rows)],
            send_sem=send.at[step, j],
            recv_sem=recv.at[step, j],
            device_id=(me, to),
            device_id_type=mesh_ids,
        )

    def slot_of(step):
        return jnp.where(step == n - 1, n - 3, jnp.where(step >= n - 3, step + 1, step))

    def owner(step):
        slot = slot_of(step)
        who = core + lax.rem(slot, 2) * (1 - 2 * core)
        return 2 * chip_at(source_mask(lax.div(slot, 2), who)) + who

    def columns(sender):
        return pl.ds(pl.multiple_of(sender * width, width), width)

    def own_rows():
        return pl.ds(pl.multiple_of(z * rows, rows), rows)

    def out_copy(step, sender):
        return pltpu.make_async_remote_copy(
            src_ref=part.at[step, own_rows()],
            dst_ref=out_ref.at[:, columns(sender)],
            send_sem=out_send.at[step],
            recv_sem=out_recv.at[sender],
            device_id=(owner(step), z),
            device_id_type=mesh_ids,
        )

    def own_copy():
        return pltpu.make_async_copy(part.at[0, own_rows()], out_ref.at[:, columns(me)], own_sem)

    def added(step, j, buffer):
        span = pl.ds(j * rows, rows)
        part[step, span] = (
            part[step, span].astype(f32) + buffer[step, span].astype(f32)
        ).astype(bf16)

    up_lag, down_lag = z, m - 1 - z
    last_lag = m - 1
    held = min(2, n - 1)
    wide = min(width, 256)

    loads[14].wait()

    def turn(tau, carry):
        @pl.when(tau < n)
        def _():
            slot = slot_of(tau)
            direct = (slot > 0) & (lax.rem(slot, 2) == 0)

            @pl.when(direct)
            def _():
                for g in range(groups_here):
                    arrival(slot, g).wait_send()

            @pl.when(direct & (slot < (4 if relayed else n - 2)))
            def _():
                for g in range(groups_here):
                    across_copy(lax.div(slot, 2) + 1, g).start()

            @pl.when(tau > 0)
            def _():
                for g in range(groups_here):
                    arrival(slot, g).wait_recv()

            @pl.when(direct)
            def _():
                for g in range(groups_here):
                    partner_copy(slot + 1, g).start()

            if relayed:
                @pl.when((slot == 3) | (slot == 4))
                def _():
                    source = jnp.where(slot == 3, 2, 4)
                    along = source_mask(lax.div(source, 2), core) == 1
                    for g in range(groups_here):
                        @pl.when(along == (g < (groups_here + 1) // 2))
                        def _():
                            relay_copy(source, g).start()

            for c in range(0, width, wide):
                total = jnp.zeros((length, wide), f32)
                for g in range(groups_here):
                    total = total + jnp.dot(
                        gat[slot, g],
                        w_ref[g * group_width : (g + 1) * group_width, c : c + wide],
                        preferred_element_type=f32,
                    )
                part[tau, :, c : c + wide] = total.astype(bf16)

        t_up = tau - up_lag

        @pl.when((t_up >= 0) & (t_up < n))
        def _():
            for j in range(m - 1, 0, -1):
                @pl.when(z < j)
                def _():
                    copy = chain_z(t_up, j, up, up_send, up_recv, z + 1)

                    @pl.when(z > 0)
                    def _():
                        copy.wait_recv()
                        added(t_up, j, up)

                    if j == 1:
                        @pl.when(t_up == n - 1)
                        def _():
                            for before in range(held, 0, -1):
                                chain_z(n - 1 - before, j, up, up_send, up_recv, z + 1).start()

                        @pl.when((t_up < n - 1 - held) | (t_up == n - 1))
                        def _():
                            copy.start()
                    else:
                        copy.start()

        t_down = tau - down_lag

        @pl.when((t_down >= 0) & (t_down < n))
        def _():
            for j in range(m - 1):
                @pl.when(z > j)
                def _():
                    copy = chain_z(t_down, j, down, down_send, down_recv, z - 1)

                    @pl.when(z < m - 1)
                    def _():
                        copy.wait_recv()
                        added(t_down, j, down)

                    if j == m - 2:
                        @pl.when(t_down == n - 1)
                        def _():
                            for before in range(held, 0, -1):
                                chain_z(n - 1 - before, j, down, down_send, down_recv, z - 1).start()

                        @pl.when((t_down < n - 1 - held) | (t_down == n - 1))
                        def _():
                            copy.start()
                    else:
                        copy.start()

        t_last = tau - last_lag

        @pl.when((t_last >= 0) & (t_last < n))
        def _():
            for j in range(m):
                @pl.when(z == j)
                def _():
                    span = pl.ds(j * rows, rows)
                    total = part[t_last, span].astype(f32)
                    if j > 0:
                        chain_z(t_last, j, up, up_send, up_recv, z).wait_recv()
                        total = total + up[t_last, span].astype(f32)
                    if j < m - 1:
                        chain_z(t_last, j, down, down_send, down_recv, z).wait_recv()
                        total = total + down[t_last, span].astype(f32)
                    part[t_last, span] = total.astype(bf16)

            @pl.when(t_last == 0)
            def _():
                own_copy().start()

            @pl.when(t_last > 0)
            def _():
                out_copy(t_last, me).start()

        return carry

    lax.fori_loop(0, n + m - 1, turn, 0)

    def finish(step, carry):
        @pl.when(lax.rem(step, 2) == 1)
        def _():
            for g in range(groups_here):
                arrival(step, g).wait_send()

        @pl.when(step > 0)
        def _():
            end_copy(step, me).wait_send()

        for j in range(m):
            @pl.when(z < j)
            def _():
                chain_z(step, j, up, up_send, up_recv, z).wait_send()

            @pl.when(z > j)
            def _():
                chain_z(step, j, down, down_send, down_recv, z).wait_send()

        @pl.when(step > 0)
        def _():
            out_copy(step, me).wait_send()
            out_copy(step, lax.rem(me + step, n)).wait_recv()

        return carry

    lax.fori_loop(0, n, finish, 0)
    own_copy().wait()

    @pl.when(has_right)
    def _():
        for which in range(3):
            rim_copy(which).wait_send()

    def sent(c, carry):
        for level in range(levels):
            @pl.when(sends(level))
            def _():
                for hop in hops(level):
                    chain_send_copy(level, hop, c).wait_send()

            if level > 0:
                @pl.when(gets(level) & odd)
                def _():
                    chain_forward(level, c).wait_send()

        return carry

    lax.fori_loop(0, tiles, sent, 0)


def layer(x, gate, maps, step_raw, rate, skip, taps, base, map_taps, map_base, gain, weight):
    n, m = lax.axis_size("seq"), lax.axis_size("tp")
    length, channels = x.shape
    heads = rate.shape[0]
    per_group = HEADS // GROUPS
    groups_here = heads // per_group
    tile = max(128, channels // 8)
    tiles = channels // tile
    width = weight.shape[1]
    span_maps = 2 * groups_here * STATE
    rim = 16
    levels = n.bit_length() - 1
    lanes = -(-heads // 128) * 128
    bf16, f32 = jnp.bfloat16, jnp.float32
    dma = pltpu.SemaphoreType.DMA
    operands = (
        x, gate, maps, step_raw.T, rate[None], skip[None], taps, base[None],
        map_taps, map_base[None], gain[None], weight,
    )
    blocks = pltpu.VMEM((n, length, width), bf16)
    return pl.pallas_call(
        functools.partial(layer_kernel, n, m, per_group),
        out_shape=jax.ShapeDtypeStruct((length // m, n * width), bf16),
        in_specs=[pl.BlockSpec(memory_space=pl.ANY)] * len(operands),
        out_specs=pl.BlockSpec(memory_space=pl.ANY),
        scratch_shapes=[
            pltpu.VMEM((length, channels), bf16),
            pltpu.VMEM((length, channels), bf16),
            pltpu.VMEM((length, span_maps), bf16),
            pltpu.VMEM((heads, length), f32),
            pltpu.VMEM((1, heads), f32),
            pltpu.VMEM((1, heads), f32),
            pltpu.VMEM((CONV, channels), f32),
            pltpu.VMEM((1, channels), f32),
            pltpu.VMEM((CONV, span_maps), f32),
            pltpu.VMEM((1, span_maps), f32),
            pltpu.VMEM((1, channels), f32),
            pltpu.VMEM(weight.shape, bf16),
            dma((15,)),
            pltpu.VMEM((rim, channels), bf16),
            pltpu.VMEM((rim, span_maps), bf16),
            pltpu.VMEM((length, max(tile, STATE)), f32),
            pltpu.VMEM((length, channels), bf16),
            pltpu.VMEM((length, span_maps), bf16),
            pltpu.VMEM((length, channels), f32),
            pltpu.VMEM((groups_here, length, length), f32),
            pltpu.VMEM((tiles, STATE, tile), f32),
            pltpu.VMEM((tiles, STATE, tile), f32),
            pltpu.VMEM((levels, tiles, STATE, tile), bf16),
            pltpu.VMEM((tiles, STATE, tile), bf16),
            pltpu.VMEM((length, 8 * heads), bf16),
            pltpu.VMEM((8 * heads, length), bf16),
            pltpu.VMEM((groups_here, STATE, length), bf16),
            pltpu.VMEM((length, 4 * heads), bf16),
            pltpu.VMEM((length, 4 * heads), bf16),
            pltpu.VMEM((8, lanes), f32),
            pltpu.VMEM((n, 8, lanes), f32),
            pltpu.VMEM((4 * heads, channels), bf16),
            pltpu.VMEM((16, channels), f32),
            pltpu.VMEM((levels, 16, channels), f32),
            pltpu.VMEM((n, groups_here, length, channels // groups_here), bf16),
            blocks,
            blocks,
            blocks,
            dma((3,)),
            dma((3,)),
            dma((n,)),
            dma((n,)),
            dma((max(1, n // 4), tiles)),
            dma((levels, tiles)),
            dma((levels, tiles)),
            dma((n, groups_here)),
            dma((n, groups_here)),
            dma((n, m)),
            dma((n, m)),
            dma((n, m)),
            dma((n, m)),
            dma((n,)),
            dma((n,)),
            dma(()),
        ],
        compiler_params=pltpu.CompilerParams(
            collective_id=2, has_side_effects=True, vmem_limit_bytes=60 << 20
        ),
        cost_estimate=pl.CostEstimate(
            flops=2 * n * length * channels * width,
            bytes_accessed=2 * (channels * width + 3 * length * channels),
            transcendentals=0,
        ),
    )(*operands)


def shards(
    conv_values,
    gate_values,
    conv_maps,
    step_raw,
    decay_log,
    skip_gain,
    values_kernel,
    values_offset,
    maps_kernel,
    maps_offset,
    norm_weight,
    out_weight,
    residual,
):
    length = conv_values.shape[0]
    heads_dev = decay_log.shape[0]
    per_group = HEADS // GROUPS
    whole_groups = heads_dev % per_group == 0
    chips = lax.axis_size("seq") // 2
    paired = lax.axis_size("seq") == 2 * chips and chips & (chips - 1) == 0
    if whole_groups and paired and heads_dev % 32 == 0:
        summed = layer(
            conv_values, gate_values, conv_maps, step_raw, decay_log, skip_gain, values_kernel,
            values_offset, maps_kernel, maps_offset, norm_weight, out_weight,
        )
        return residual.astype(jnp.float32) + summed.astype(jnp.float32)
    step_size = jax.nn.softplus(step_raw)
    place = jnp.arange(length, dtype=jnp.int32)
    cum_log = jnp.dot(
        (place[:, None] >= place[None, :]).astype(jnp.float32),
        -jnp.exp(decay_log)[None, :] * step_size,
        precision=lax.Precision.HIGHEST,
    )
    normed = front(
        conv_values, gate_values, conv_maps, cum_log, step_size, skip_gain, values_kernel,
        values_offset, maps_kernel, maps_offset, norm_weight, whole_groups,
    )
    if not whole_groups:
        gated_out = normed.reshape(length, heads_dev, HEAD_DIM)
        head_squares = jnp.sum(gated_out * gated_out, axis=2)
        all_heads = lax.all_gather(head_squares, "tp", axis=1, tiled=True)
        group_totals = jnp.sum(all_heads.reshape(length, GROUPS, per_group), axis=2)
        heads_here = lax.axis_index("tp") * heads_dev + jnp.arange(heads_dev, dtype=jnp.int32)
        inv_rms = lax.rsqrt(
            group_totals[:, heads_here // per_group] / (per_group * HEAD_DIM) + 1e-05
        )
        normed = (
            (gated_out * inv_rms[:, :, None]).reshape(length, heads_dev * HEAD_DIM)
            * norm_weight[None, :]
        ).astype(jnp.bfloat16)
    blocks = mix(normed, out_weight)
    summed = jnp.transpose(blocks, (1, 0, 2)).reshape(residual.shape).astype(jnp.float32)
    return residual.astype(jnp.float32) + summed


def solution(mesh):
    placed = (
        P("seq", "tp"),
        P("seq", "tp"),
        P("seq", None),
        P("seq", "tp"),
        P("tp"),
        P("tp"),
        P(None, "tp"),
        P("tp"),
        P(),
        P(),
        P("tp"),
        P("tp", "seq"),
        P(("seq", "tp"), None),
    )
    return jax.shard_map(
        shards, mesh=mesh, in_specs=placed, out_specs=P(("seq", "tp"), None), check_vma=False
    )
```

```python
import functools

import jax
import jax.numpy as jnp
from jax import lax
from jax.experimental import pallas as pl
from jax.experimental.pallas import tpu as pltpu
from jax.sharding import PartitionSpec as P

HEADS = 128
HEAD_DIM = 64
STATE = 128
GROUPS = 8
CONV = 4


def ring_place(spot, size):
    if size % 4:
        return spot
    half = size // 2
    past = spot - half
    turned = half + (half - 2 - 2 * lax.div(past, 2)) + lax.rem(past, 2)
    return jnp.where(spot < half, spot, turned)


def mix_kernel(
    n, m, x_ref, w_ref, out_ref, gat, part, up, down,
    own_sem, gat_send, gat_recv, up_send, up_recv, down_send, down_recv, out_send, out_recv,
):
    mesh_ids = pl.DeviceIdType.MESH
    me, z = lax.axis_index("seq"), lax.axis_index("tp")
    spot = ring_place(me, n)
    right = ring_place(lax.rem(spot + 1, n), n)
    left = ring_place(lax.rem(spot + n - 1, n), n)
    half = gat.shape[2]
    depth = gat.shape[3]
    width = w_ref.shape[1]
    rows = part.shape[1] // m
    tile = min(width, 256)

    own = [
        pltpu.make_async_copy(x_ref.at[pl.ds(d * half, half)], gat.at[0, d], own_sem.at[d])
        for d in range(2)
    ]
    for copy in own:
        copy.start()

    barrier = pltpu.get_barrier_semaphore()

    def greet(step, carry):
        pl.semaphore_signal(
            barrier, inc=1, device_id=(lax.rem(me + step, n), z), device_id_type=mesh_ids
        )
        return carry

    lax.fori_loop(1, n, greet, 0)

    @pl.when(z > 0)
    def _():
        pl.semaphore_signal(barrier, inc=1, device_id=(me, z - 1), device_id_type=mesh_ids)

    @pl.when(z < m - 1)
    def _():
        pl.semaphore_signal(barrier, inc=1, device_id=(me, z + 1), device_id_type=mesh_ids)

    beside = (z > 0).astype(jnp.int32) + (z < m - 1).astype(jnp.int32)
    pl.semaphore_wait(barrier, n - 1 + beside)

    for copy in own:
        copy.wait()

    def gather_copy(step, d):
        return pltpu.make_async_remote_copy(
            src_ref=gat.at[step, d],
            dst_ref=gat.at[step + 1, d],
            send_sem=gat_send.at[step, d],
            recv_sem=gat_recv.at[step + 1, d],
            device_id=(right if d == 0 else left, z),
            device_id_type=mesh_ids,
        )

    def gather_arrival(step, d):
        return pltpu.make_async_remote_copy(
            src_ref=gat.at[step, d],
            dst_ref=gat.at[step, d],
            send_sem=gat_send.at[step, d],
            recv_sem=gat_recv.at[step, d],
            device_id=(right if d == 0 else left, z),
            device_id_type=mesh_ids,
        )

    def chain_copy(step, j, buffer, send, recv, to):
        return pltpu.make_async_remote_copy(
            src_ref=part.at[step, pl.ds(j * rows, rows)],
            dst_ref=buffer.at[step, pl.ds(j * rows, rows)],
            send_sem=send.at[step, j],
            recv_sem=recv.at[step, j],
            device_id=(me, to),
            device_id_type=mesh_ids,
        )

    def owner(step):
        there = jnp.where(z < m // 2, spot - step + n, spot + step)
        return ring_place(lax.rem(there, n), n)

    def out_copy(step, sender):
        return pltpu.make_async_remote_copy(
            src_ref=part.at[step, pl.ds(pl.multiple_of(z * rows, rows), rows)],
            dst_ref=out_ref.at[sender],
            send_sem=out_send.at[step],
            recv_sem=out_recv.at[sender],
            device_id=(owner(step), z),
            device_id_type=mesh_ids,
        )

    def added(step, j, buffer):
        span = pl.ds(j * rows, rows)
        part[step, span] = (
            part[step, span].astype(jnp.float32) + buffer[step, span].astype(jnp.float32)
        ).astype(jnp.bfloat16)

    up_lag, down_lag = z, m - 1 - z
    last_lag = jnp.maximum(up_lag, down_lag)

    def turn(tau, carry):
        @pl.when(tau < n)
        def _():
            @pl.when(tau > 0)
            def _():
                for d in range(2):
                    gather_arrival(tau, d).wait_recv()

            @pl.when(tau < n - 1)
            def _():
                for d in range(2):
                    gather_copy(tau, d).start()

            block = gat[tau].reshape(2 * half, depth)
            for c in range(0, width, tile):
                part[tau, :, c : c + tile] = jnp.dot(
                    block, w_ref[:, c : c + tile], preferred_element_type=jnp.float32
                ).astype(jnp.bfloat16)

        t_up = tau - up_lag

        @pl.when((t_up >= 0) & (t_up < n))
        def _():
            for j in range(m - 1, 0, -1):
                @pl.when(z < j)
                def _():
                    copy = chain_copy(t_up, j, up, up_send, up_recv, z + 1)

                    @pl.when(z > 0)
                    def _():
                        copy.wait_recv()
                        added(t_up, j, up)

                    copy.start()

        t_down = tau - down_lag

        @pl.when((t_down >= 0) & (t_down < n))
        def _():
            for j in range(m - 1):
                @pl.when(z > j)
                def _():
                    copy = chain_copy(t_down, j, down, down_send, down_recv, z - 1)

                    @pl.when(z < m - 1)
                    def _():
                        copy.wait_recv()
                        added(t_down, j, down)

                    copy.start()

        t_last = tau - last_lag

        @pl.when((t_last >= 0) & (t_last < n))
        def _():
            for j in range(m):
                @pl.when(z == j)
                def _():
                    span = pl.ds(j * rows, rows)
                    total = part[t_last, span].astype(jnp.float32)
                    if j > 0:
                        chain_copy(t_last, j, up, up_send, up_recv, z).wait_recv()
                        total = total + up[t_last, span].astype(jnp.float32)
                    if j < m - 1:
                        chain_copy(t_last, j, down, down_send, down_recv, z).wait_recv()
                        total = total + down[t_last, span].astype(jnp.float32)
                    part[t_last, span] = total.astype(jnp.bfloat16)

            @pl.when(t_last == 0)
            def _():
                out_ref[me] = part[0, pl.ds(pl.multiple_of(z * rows, rows), rows)]

            @pl.when(t_last > 0)
            def _():
                out_copy(t_last, me).start()

        return carry

    lax.fori_loop(0, n + m - 1, turn, 0)

    def finish(step, carry):
        @pl.when(step < n - 1)
        def _():
            for d in range(2):
                gather_copy(step, d).wait_send()

        for j in range(m):
            @pl.when(z < j)
            def _():
                chain_copy(step, j, up, up_send, up_recv, z).wait_send()

            @pl.when(z > j)
            def _():
                chain_copy(step, j, down, down_send, down_recv, z).wait_send()

        @pl.when(step > 0)
        def _():
            out_copy(step, me).wait_send()
            out_copy(step, lax.rem(me + step, n)).wait_recv()

        return carry

    lax.fori_loop(0, n, finish, 0)


def mix(normed, weight):
    n, m = lax.axis_size("seq"), lax.axis_size("tp")
    length, depth = normed.shape
    width = weight.shape[1]
    rows = length // m
    half = length // 2
    slots = pltpu.VMEM((n, length, width), jnp.bfloat16)
    dma = pltpu.SemaphoreType.DMA
    vmem = pl.BlockSpec(memory_space=pltpu.VMEM)
    return pl.pallas_call(
        functools.partial(mix_kernel, n, m),
        out_shape=jax.ShapeDtypeStruct((n, rows, width), jnp.bfloat16),
        in_specs=[pl.BlockSpec(memory_space=pl.ANY), vmem],
        out_specs=vmem,
        scratch_shapes=[
            pltpu.VMEM((n, 2, half, depth), jnp.bfloat16),
            slots,
            slots,
            slots,
            dma((2,)),
            dma((n, 2)),
            dma((n, 2)),
            dma((n, m)),
            dma((n, m)),
            dma((n, m)),
            dma((n, m)),
            dma((n,)),
            dma((n,)),
        ],
        compiler_params=pltpu.CompilerParams(
            collective_id=0, has_side_effects=True, vmem_limit_bytes=48 << 20
        ),
        cost_estimate=pl.CostEstimate(
            flops=2 * n * length * depth * width,
            bytes_accessed=2 * (depth * width + length * depth),
            transcendentals=0,
        ),
    )(normed, weight)


def front_kernel(
    n, per_group, whole_groups, x_ref, gate_ref, maps_ref, cum_ref, cum_t_ref, step_ref, step_t_ref,
    decay_ref, skip_ref, taps_ref, base_ref, map_taps_ref, map_base_ref, gain_ref, out_ref,
    rim_x, rim_maps, pad, values, y, b_maps, c_maps, scores, local, arrived, leaving,
    rim_send, rim_recv, chain_send, chain_recv,
):
    mesh_ids = pl.DeviceIdType.MESH
    exact = lax.Precision.HIGHEST
    me, z = lax.axis_index("seq"), lax.axis_index("tp")
    length, channels = x_ref.shape
    heads = cum_ref.shape[1]
    groups_here = scores.shape[0]
    first_group = lax.div(z * heads, per_group)
    tile = arrived.shape[2]
    tiles = channels // tile
    group_width = channels // groups_here
    rim = rim_x.shape[0]

    barrier = pltpu.get_barrier_semaphore()
    has_left, has_right = me > 0, me < n - 1

    @pl.when(has_left)
    def _():
        pl.semaphore_signal(barrier, inc=1, device_id=(me - 1, z), device_id_type=mesh_ids)

    @pl.when(has_right)
    def _():
        pl.semaphore_signal(barrier, inc=1, device_id=(me + 1, z), device_id_type=mesh_ids)

    pl.semaphore_wait(barrier, has_left.astype(jnp.int32) + has_right.astype(jnp.int32))

    def rim_copy(which):
        source, target = ((x_ref, rim_x), (maps_ref, rim_maps))[which]
        return pltpu.make_async_remote_copy(
            src_ref=source.at[pl.ds(length - rim, rim)],
            dst_ref=target,
            send_sem=rim_send.at[which],
            recv_sem=rim_recv.at[which],
            device_id=(me + 1, z),
            device_id_type=mesh_ids,
        )

    @pl.when(has_right)
    def _():
        for which in range(2):
            rim_copy(which).start()

    @pl.when(has_left)
    def _():
        for which in range(2):
            rim_copy(which).wait_recv()

    @pl.when(jnp.logical_not(has_left))
    def _():
        rim_x[...] = jnp.zeros_like(rim_x)
        rim_maps[...] = jnp.zeros_like(rim_maps)

    def conv(rows_ref, rim_ref, taps, base, start, size):
        span = pl.ds(start, size)
        pad[0:rim, 0:size] = rim_ref[:, span].astype(jnp.float32)
        pad[rim : rim + length, 0:size] = rows_ref[:, span].astype(jnp.float32)
        total = base[:, span]
        for k in range(CONV):
            at = rim - (CONV - 1) + k
            total = total + taps[k : k + 1, span] * pad[at : at + length, 0:size]
        return jax.nn.silu(total).astype(jnp.bfloat16)

    for g in range(groups_here):
        at = pl.multiple_of((first_group + g) * STATE, STATE)
        b_maps[g] = conv(maps_ref, rim_maps, map_taps_ref, map_base_ref, at, STATE)
        at = pl.multiple_of((GROUPS + first_group + g) * STATE, STATE)
        c_maps[g] = conv(maps_ref, rim_maps, map_taps_ref, map_base_ref, at, STATE)
        scores[g] = lax.dot_general(
            c_maps[g], b_maps[g], (((1,), (1,)), ((), ())), preferred_element_type=jnp.float32
        )

    def spread(per_head, start):
        head = lax.broadcasted_iota(jnp.int32, (heads, tile), 0) * HEAD_DIM
        lane = lax.broadcasted_iota(jnp.int32, (heads, tile), 1) + start
        chosen = ((lane >= head) & (lane < head + HEAD_DIM)).astype(jnp.float32)
        return jnp.dot(
            per_head, chosen, precision=exact, preferred_element_type=jnp.float32
        )

    cum = cum_ref[...]
    end_weight = jnp.exp(cum[length - 1 : length] - cum) * step_ref[...]
    grown = jnp.exp(cum)

    def states(c, carry):
        start = pl.multiple_of(c * tile, tile)
        span = pl.ds(start, tile)
        value = conv(x_ref, rim_x, taps_ref, base_ref, start, tile)
        values[:, span] = value
        weighted = (value.astype(jnp.float32) * spread(end_weight, start)).astype(jnp.bfloat16)
        g = lax.div(start, group_width)
        local[c] = lax.dot_general(
            b_maps[g], weighted, (((0,), (0,)), ((), ())), preferred_element_type=jnp.float32
        )
        return carry

    lax.fori_loop(0, tiles, states, 0)

    def chain_copy(c):
        return pltpu.make_async_remote_copy(
            src_ref=leaving.at[c],
            dst_ref=arrived.at[c],
            send_sem=chain_send.at[c],
            recv_sem=chain_recv.at[c],
            device_id=(me + 1, z),
            device_id_type=mesh_ids,
        )

    def link(c, carry):
        span = pl.ds(pl.multiple_of(c * tile, tile), tile)

        @pl.when(has_left)
        def _():
            chain_copy(c).wait_recv()

        @pl.when(jnp.logical_not(has_left))
        def _():
            arrived[c] = jnp.zeros_like(arrived[c])

        @pl.when(has_right)
        def _():
            leaving[c] = (
                decay_ref[:, span] * arrived[c].astype(jnp.float32) + local[c]
            ).astype(jnp.bfloat16)
            chain_copy(c).start()

        return carry

    pair = 2 * HEAD_DIM
    causal = lax.broadcasted_iota(jnp.int32, (length, length), 0) >= lax.broadcasted_iota(
        jnp.int32, (length, length), 1
    )

    def within(q, carry):
        span = pl.ds(pl.multiple_of(q * pair, pair), pair)
        value = values[:, span]
        g = lax.div(q * pair, group_width)
        sums = []
        for e in range(2):
            h = 2 * q + e
            lane = lax.broadcasted_iota(jnp.int32, (length, heads), 1)
            column = jnp.sum(jnp.where(lane == h, cum_ref[...], 0.0), axis=1, keepdims=True)
            gap = column - cum_t_ref[pl.ds(h, 1), :]
            kernel = jnp.where(causal, jnp.exp(jnp.where(causal, gap, 0.0)), 0.0)
            mixing = kernel * scores[g] * step_t_ref[pl.ds(h, 1), :]
            sums.append(
                jnp.dot(mixing.astype(jnp.bfloat16), value, preferred_element_type=jnp.float32)
            )
        first = lax.broadcasted_iota(jnp.int32, (length, pair), 1) < HEAD_DIM
        y[:, span] = jnp.where(first, sums[0], sums[1])
        return carry

    late = me >= n // 2

    def phase(turn, carry):
        @pl.when((turn == 0) == late)
        def _():
            lax.fori_loop(0, channels // pair, within, 0)

        @pl.when(turn == 0)
        def _():
            lax.fori_loop(0, tiles, link, 0)

        return carry

    lax.fori_loop(0, 2, phase, 0)

    for g in range(groups_here):
        per = group_width // tile

        def gated(c, squares):
            c = c + g * per
            start = pl.multiple_of(c * tile, tile)
            span = pl.ds(start, tile)
            carried = jnp.dot(
                c_maps[g], arrived[c], preferred_element_type=jnp.float32
            ) * spread(grown, start)
            total = y[:, span] + carried + skip_ref[:, span] * values[:, span].astype(jnp.float32)
            total = total * jax.nn.silu(gate_ref[:, span].astype(jnp.float32))
            y[:, span] = total
            return squares + jnp.sum(total * total, axis=1, keepdims=True)

        squares = lax.fori_loop(0, per, gated, jnp.zeros((length, 1), jnp.float32))
        scale = lax.rsqrt(squares / group_width + 1e-05)

        def scaled(c, carry):
            span = pl.ds(pl.multiple_of((c + g * per) * tile, tile), tile)
            if whole_groups:
                out_ref[:, span] = (y[:, span] * scale * gain_ref[:, span]).astype(out_ref.dtype)
            else:
                out_ref[:, span] = y[:, span]
            return carry

        lax.fori_loop(0, per, scaled, 0)

    @pl.when(has_right)
    def _():
        for which in range(2):
            rim_copy(which).wait_send()

        def sent(c, carry):
            chain_copy(c).wait_send()
            return carry

        lax.fori_loop(0, tiles, sent, 0)


def front(x, gate, maps, cum, step, skip, taps, base, map_taps, map_base, gain, whole_groups):
    n = lax.axis_size("seq")
    length, channels = x.shape
    heads = cum.shape[1]
    per_group = HEADS // GROUPS
    groups_here = max(1, heads // per_group)
    tile = max(128, channels // 8)
    tiles = channels // tile
    rim = 16
    bf16, f32 = jnp.bfloat16, jnp.float32
    dma = pltpu.SemaphoreType.DMA
    vmem = pl.BlockSpec(memory_space=pltpu.VMEM)
    decay = jnp.repeat(jnp.exp(cum[-1]), HEAD_DIM)[None]
    skips = jnp.repeat(skip, HEAD_DIM)[None]
    operands = (
        x, gate, maps, cum, cum.T, step, step.T, decay, skips,
        taps, base[None], map_taps, map_base[None], gain[None],
    )
    return pl.pallas_call(
        functools.partial(front_kernel, n, per_group, whole_groups),
        out_shape=jax.ShapeDtypeStruct((length, channels), bf16 if whole_groups else f32),
        in_specs=[vmem] * len(operands),
        out_specs=vmem,
        scratch_shapes=[
            pltpu.VMEM((rim, channels), bf16),
            pltpu.VMEM((rim, maps.shape[1]), bf16),
            pltpu.VMEM((rim + length, max(tile, STATE)), f32),
            pltpu.VMEM((length, channels), bf16),
            pltpu.VMEM((length, channels), f32),
            pltpu.VMEM((groups_here, length, STATE), bf16),
            pltpu.VMEM((groups_here, length, STATE), bf16),
            pltpu.VMEM((groups_here, length, length), f32),
            pltpu.VMEM((tiles, STATE, tile), f32),
            pltpu.VMEM((tiles, STATE, tile), bf16),
            pltpu.VMEM((tiles, STATE, tile), bf16),
            dma((2,)),
            dma((2,)),
            dma((tiles,)),
            dma((tiles,)),
        ],
        compiler_params=pltpu.CompilerParams(
            collective_id=1, has_side_effects=True, vmem_limit_bytes=48 << 20
        ),
    )(*operands)


LOG2E = 1.4426950408889634


def three(value):
    high = value.astype(jnp.bfloat16)
    rest = value - high.astype(jnp.float32)
    middle = rest.astype(jnp.bfloat16)
    low = (rest - middle.astype(jnp.float32)).astype(jnp.bfloat16)
    return high, middle, low


def layer_kernel(
    n, m, per_group, x_hbm, gate_hbm, maps_hbm, step_hbm, rate_hbm, skip_hbm, taps_hbm, base_hbm,
    map_taps_hbm, map_base_hbm, gain_hbm, w_hbm, out_ref,
    x_ref, gate_ref, maps_ref, step_ref, rate_ref, skip_ref, taps_ref, base_ref, map_taps_ref,
    map_base_ref, gain_ref, w_ref, in_sem,
    rim_x, rim_maps, pad, values, maps_conv, y, scores, local, state, arrived, leaving,
    gap_left, gap_right, turned_maps, ends, growth, own_end, all_ends, chosen, channel_rows, prefix_rows,
    gat, part, up, down,
    rim_send, rim_recv, end_send, end_recv, chain_send, chain_recv, forward_send,
    gat_send, gat_recv, up_send, up_recv, down_send, down_recv, out_send, out_recv,
    own_sem,
):
    mesh_ids = pl.DeviceIdType.MESH
    exact = lax.Precision.HIGHEST
    f32, bf16 = jnp.float32, jnp.bfloat16
    me, z = lax.axis_index("seq"), lax.axis_index("tp")
    chips = n // 2
    chip, core = lax.div(me, 2), lax.rem(me, 2)
    partner = me + 1 - 2 * core
    length, channels = x_ref.shape
    heads = step_ref.shape[0]
    levels = arrived.shape[0]
    groups_here = scores.shape[0]
    first_group = z * groups_here
    span_maps = groups_here * STATE
    tile = arrived.shape[3]
    tiles = channels // tile
    group_width = channels // groups_here
    rim = rim_x.shape[0]
    width = w_ref.shape[1]
    rows = length // m
    half = length // 2

    at_b = pl.ds(pl.multiple_of(first_group * STATE, STATE), span_maps)
    at_c = pl.ds(pl.multiple_of((GROUPS + first_group) * STATE, STATE), span_maps)
    to_b, to_c = pl.ds(0, span_maps), pl.ds(span_maps, span_maps)
    fetches = (
        (step_hbm, step_ref),
        (rate_hbm, rate_ref),
        (skip_hbm, skip_ref),
        (maps_hbm.at[:, at_b], maps_ref.at[:, to_b]),
        (maps_hbm.at[:, at_c], maps_ref.at[:, to_c]),
        (map_taps_hbm.at[:, at_b], map_taps_ref.at[:, to_b]),
        (map_taps_hbm.at[:, at_c], map_taps_ref.at[:, to_c]),
        (map_base_hbm.at[:, at_b], map_base_ref.at[:, to_b]),
        (map_base_hbm.at[:, at_c], map_base_ref.at[:, to_c]),
        (taps_hbm, taps_ref),
        (base_hbm, base_ref),
        (x_hbm, x_ref),
        (gate_hbm, gate_ref),
        (gain_hbm, gain_ref),
        (w_hbm, w_ref),
    )
    loads = [
        pltpu.make_async_copy(source, target, in_sem.at[i])
        for i, (source, target) in enumerate(fetches)
    ]

    barrier = pltpu.get_barrier_semaphore()

    def greet(step, carry):
        pl.semaphore_signal(
            barrier, inc=1, device_id=(lax.rem(me + step, n), z), device_id_type=mesh_ids
        )
        return carry

    lax.fori_loop(1, n, greet, 0)

    @pl.when(z > 0)
    def _():
        pl.semaphore_signal(barrier, inc=1, device_id=(me, z - 1), device_id_type=mesh_ids)

    @pl.when(z < m - 1)
    def _():
        pl.semaphore_signal(barrier, inc=1, device_id=(me, z + 1), device_id_type=mesh_ids)

    for load in loads[:12]:
        load.start()

    has_left, has_right = me > 0, me < n - 1
    odd = core == 1

    for load in loads[:3]:
        load.wait()

    def turned(value):
        size = value.shape[0]
        same = lax.broadcasted_iota(jnp.int32, (size, size), 0) == lax.broadcasted_iota(
            jnp.int32, (size, size), 1
        )
        return lax.dot_general(
            value, same.astype(f32), (((0,), (0,)), ((), ())), precision=exact,
            preferred_element_type=f32,
        )

    step = jax.nn.softplus(turned(step_ref[...]))
    log_decay = -jnp.exp(rate_ref[...]) * step
    row = lax.broadcasted_iota(jnp.int32, (length, length), 0)
    column = lax.broadcasted_iota(jnp.int32, (length, length), 1)
    lower = (row >= column).astype(f32)
    cum = jnp.dot(lower, log_decay, precision=exact, preferred_element_type=f32)
    final = cum[length - 1 : length]
    ones = jnp.ones((length, heads), bf16)
    blank = jnp.zeros((length, heads), bf16)
    gap_left[...] = jnp.concatenate(
        [*three(cum * LOG2E), ones, ones, ones, blank, blank], axis=1
    )
    source_log = jnp.log(step) * LOG2E - cum * LOG2E
    source_rows = turned(source_log)
    unit = jnp.ones((heads, length), bf16)
    gap_right[...] = jnp.concatenate(
        [unit, unit, unit, *three(source_rows), unit, unit], axis=0
    )
    ends[...] = jnp.concatenate([*three(jnp.exp(final - cum) * step), blank], axis=1)
    growth[...] = jnp.concatenate([*three(jnp.exp(cum)), blank], axis=1)
    lanes = own_end.shape[1]
    own_end[...] = jnp.zeros_like(own_end)
    own_end[:, 0:heads] = jnp.broadcast_to(final, (8, heads))
    all_ends[me] = jnp.zeros((8, lanes), f32)

    first_row = lax.broadcasted_iota(jnp.int32, (16, heads), 0) < 8
    two = jnp.where(first_row, jnp.exp(final), skip_ref[...])
    two = jnp.concatenate([*three(two), jnp.zeros((16, heads), bf16)], axis=1)

    def choose(c, carry):
        start = pl.multiple_of(c * tile, tile)
        slot = lax.broadcasted_iota(jnp.int32, (4 * heads, tile), 0)
        head = lax.rem(slot, heads) * HEAD_DIM
        lane = lax.broadcasted_iota(jnp.int32, (4 * heads, tile), 1) + start
        chosen[:, pl.ds(start, tile)] = (
            ((lane >= head) & (lane < head + HEAD_DIM)).astype(f32).astype(bf16)
        )
        return carry

    lax.fori_loop(0, tiles, choose, 0)

    def spread(per_head, span):
        return jnp.dot(per_head, chosen[:, span], preferred_element_type=f32)

    channel_rows[...] = spread(two, slice(None))
    for load in loads[3:9]:
        load.wait()

    def smooth(rows_ref, taps, base, out, start, size):
        span = pl.ds(start, size)
        pad[:, 0:size] = rows_ref[:, span].astype(f32)
        total = base[:, span]
        for k in range(CONV):
            at = rim - (CONV - 1) + k
            total = total + taps[k : k + 1, span] * pad[at : at + length - rim, 0:size]
        out[rim:length, span] = jax.nn.silu(total).astype(bf16)

    for c in range(0, 2 * span_maps, tile):
        smooth(maps_ref, map_taps_ref, map_base_ref, maps_conv, c, tile)

    beside = (z > 0).astype(jnp.int32) + (z < m - 1).astype(jnp.int32)
    pl.semaphore_wait(barrier, n - 1 + beside)

    last_rows = pl.ds(length - rim, rim)

    def rim_copy(which):
        source, target = (
            (x_hbm.at[last_rows], rim_x),
            (maps_hbm.at[last_rows, at_b], rim_maps.at[:, to_b]),
            (maps_hbm.at[last_rows, at_c], rim_maps.at[:, to_c]),
        )[which]
        return pltpu.make_async_remote_copy(
            src_ref=source,
            dst_ref=target,
            send_sem=rim_send.at[which],
            recv_sem=rim_recv.at[which],
            device_id=(me + 1, z),
            device_id_type=mesh_ids,
        )

    @pl.when(has_right)
    def _():
        for which in range(3):
            rim_copy(which).start()

    def end_copy(offset, sender):
        return pltpu.make_async_remote_copy(
            src_ref=own_end,
            dst_ref=all_ends.at[sender],
            send_sem=end_send.at[offset],
            recv_sem=end_recv.at[sender],
            device_id=(lax.rem(me + offset, n), z),
            device_id_type=mesh_ids,
        )

    def send_end(offset, carry):
        end_copy(offset, me).start()
        return carry

    lax.fori_loop(1, n, send_end, 0)

    for load in loads[9:12]:
        load.wait()
    for load in loads[12:]:
        load.start()

    def smooth_rim(rows_ref, rim_ref, taps, base, out, start, size):
        span = pl.ds(start, size)
        pad[0:rim, 0:size] = rim_ref[:, span].astype(f32)
        pad[rim : 2 * rim, 0:size] = rows_ref[0:rim, span].astype(f32)
        total = base[:, span]
        for k in range(CONV):
            at = rim - (CONV - 1) + k
            total = total + taps[k : k + 1, span] * pad[at : at + rim, 0:size]
        out[0:rim, span] = jax.nn.silu(total).astype(bf16)

    def smooth_tile(c, carry):
        smooth(x_ref, taps_ref, base_ref, values, pl.multiple_of(c * tile, tile), tile)
        return carry

    lax.fori_loop(0, tiles, smooth_tile, 0)

    def chain_send_copy(level, hop, c):
        return pltpu.make_async_remote_copy(
            src_ref=leaving.at[c],
            dst_ref=arrived.at[level, c],
            send_sem=chain_send.at[hop, c],
            recv_sem=chain_recv.at[level, c],
            device_id=(me + 1 if level == 0 else me + 2 * (hop + 1), z),
            device_id_type=mesh_ids,
        )

    def chain_forward(level, c):
        return pltpu.make_async_remote_copy(
            src_ref=arrived.at[level, c],
            dst_ref=arrived.at[level, c],
            send_sem=forward_send.at[level, c],
            recv_sem=chain_recv.at[level, c],
            device_id=(partner, z),
            device_id_type=mesh_ids,
        )

    def hops(level):
        return range(max(1, 2**level // 2))

    def sends(level):
        return lax.rem(me, 2 ** (level + 1)) == 2**level - 1

    def gets(level):
        return lax.rem(lax.div(me, 2**level), 2) == 1

    per = group_width // tile

    maps_conv[0:rim] = jnp.zeros((rim, 2 * span_maps), bf16)
    values[0:rim] = jnp.zeros((rim, channels), bf16)

    for g in range(groups_here):
        turned_maps[g] = turned(
            maps_conv[:, g * STATE : (g + 1) * STATE].astype(f32)
        ).astype(bf16)

    for g in range(groups_here):
        mine = range(g * per, (g + 1) * per)
        spans = [slice(c * tile, (c + 1) * tile) for c in mine]
        weighted = [
            (values[:, span].astype(f32) * spread(ends[...], span)).astype(bf16)
            for span in spans
        ]
        for c, w in zip(mine, weighted):
            local[c] = jnp.dot(turned_maps[g], w, preferred_element_type=f32)

    @pl.when(has_left)
    def _():
        for which in range(3):
            rim_copy(which).wait_recv()

    @pl.when(jnp.logical_not(has_left))
    def _():
        rim_x[...] = jnp.zeros_like(rim_x)
        rim_maps[...] = jnp.zeros_like(rim_maps)

    for c in range(0, 2 * span_maps, tile):
        smooth_rim(maps_ref, rim_maps, map_taps_ref, map_base_ref, maps_conv, c, tile)
    for c in range(0, channels, tile):
        smooth_rim(x_ref, rim_x, taps_ref, base_ref, values, c, tile)

    for g in range(groups_here):
        mine = range(g * per, (g + 1) * per)
        spans = [slice(c * tile, (c + 1) * tile) for c in mine]
        first_maps = maps_conv[0:rim, g * STATE : (g + 1) * STATE]
        weighted = [
            (values[0:rim, span].astype(f32) * spread(ends[0:rim], span)).astype(bf16)
            for span in spans
        ]
        for c, w in zip(mine, weighted):
            total = local[c] + lax.dot_general(
                first_maps, w, (((0,), (0,)), ((), ())), preferred_element_type=f32
            )
            local[c] = total
            state[c] = jnp.zeros_like(total)
            leaving[c] = total.astype(bf16)

        @pl.when(sends(0))
        def _():
            for c in mine:
                chain_send_copy(0, 0, c).start()

    def link(level, c):
        span = pl.ds(pl.multiple_of(c * tile, tile), tile)

        @pl.when(gets(level))
        def _():
            chain_forward(level, c).wait_recv()
            if level == 0:
                state[c] = arrived[level, c].astype(f32)
            else:
                @pl.when(odd)
                def _():
                    chain_forward(level, c).start()

                state[c] = state[c] + prefix_rows[level, 0:1, span] * arrived[level, c].astype(f32)

        if level + 1 < levels:
            @pl.when(sends(level + 1))
            def _():
                leaving[c] = (channel_rows[0:1, span] * state[c] + local[c]).astype(bf16)
                for hop in hops(level + 1):
                    chain_send_copy(level + 1, hop, c).start()

    def link_all(level, first, last):
        def body(c, carry):
            link(level, c)
            return carry

        lax.fori_loop(first, last, body, 0)

    link_all(0, 0, tiles)

    for g in range(groups_here):
        scores[g] = lax.dot_general(
            maps_conv[:, span_maps + g * STATE : span_maps + (g + 1) * STATE],
            maps_conv[:, g * STATE : (g + 1) * STATE],
            (((1,), (1,)), ((), ())),
            preferred_element_type=f32,
        )

    def get_end(offset, carry):
        end_copy(offset, lax.rem(me + offset, n)).wait_recv()
        return carry

    lax.fori_loop(1, n, get_end, 0)

    for level in range(1, levels):
        base = me - lax.rem(me, 2**level)
        total = jnp.zeros((8, lanes), f32)
        for i in range(n):
            total = total + jnp.where((base <= i) & (i < me), all_ends[i], 0.0)
        passed = jnp.exp(total[:, 0:heads])
        passed = jnp.concatenate([passed, passed], axis=0)
        passed = jnp.concatenate([*three(passed), jnp.zeros((16, heads), bf16)], axis=1)

        prefix_rows[level] = spread(passed, slice(None))

    pair = 2 * HEAD_DIM
    lane = lax.broadcasted_iota(jnp.int32, (half, pair), 1)
    batch = 4

    def mask_of(head):
        slot = lax.broadcasted_iota(jnp.int32, (1, 8 * heads), 1)
        return ((lax.rem(slot, heads) == head) & (slot < 6 * heads)).astype(f32).astype(bf16)

    def within(turn, carry):
        g = lax.div(turn * batch * pair, group_width)
        gaps = []
        for e in range(2 * batch):
            left = gap_left[...] * mask_of(2 * batch * turn + e)
            gaps.append((
                jnp.dot(left[0:half], gap_right[:, 0:half], preferred_element_type=f32),
                jnp.dot(left[half:length], gap_right[...], preferred_element_type=f32),
            ))
        causal = lax.broadcasted_iota(jnp.int32, (half, half), 0) >= lax.broadcasted_iota(
            jnp.int32, (half, half), 1
        )
        causal_late = lax.broadcasted_iota(jnp.int32, (half, length), 0) + half >= (
            lax.broadcasted_iota(jnp.int32, (half, length), 1)
        )
        mixing = [
            (
                (jnp.where(causal, jnp.exp2(a), 0.0) * scores[g, 0:half, 0:half]).astype(bf16),
                (jnp.where(causal_late, jnp.exp2(b), 0.0) * scores[g, half:length]).astype(bf16),
            )
            for a, b in gaps
        ]
        for q in range(batch):
            span = pl.ds(pl.multiple_of((turn * batch + q) * pair, pair), pair)
            early, late = [], []
            for a, b in mixing[2 * q : 2 * q + 2]:
                early.append(jnp.dot(a, values[0:half, span], preferred_element_type=f32))
                late.append(jnp.dot(b, values[:, span], preferred_element_type=f32))
            y[0:half, span] = jnp.where(lane < HEAD_DIM, early[0], early[1])
            y[half:length, span] = jnp.where(lane < HEAD_DIM, late[0], late[1])
        return carry

    batches = channels // (pair * batch)
    share = tiles // batches

    def within_level(turn, carry):
        for c in range(share):
            if levels > 2:
                link(1, turn * share + c)
        return within(turn, carry)

    lax.fori_loop(0, batches, within_level, 0)

    for level in range(2, levels - 1):
        link_all(level, 0, tiles)

    for load in loads[12:14]:
        load.wait()

    def partner_copy(slot, g):
        return pltpu.make_async_remote_copy(
            src_ref=gat.at[slot - 1, g],
            dst_ref=gat.at[slot, g],
            send_sem=gat_send.at[slot, g],
            recv_sem=gat_recv.at[slot, g],
            device_id=(partner, z),
            device_id_type=mesh_ids,
        )

    def source_mask(i, who):
        swap = (who == 1) & (chips >= 4)
        return i + jnp.where(swap & (i == 1), 1, 0) - jnp.where(swap & (i == 2), 1, 0)

    def chip_at(mask):
        there, bit = chip, 1
        while bit < chips:
            on = lax.rem(lax.div(mask, bit), 2)
            there = there + on * (bit - 2 * bit * lax.rem(lax.div(chip, bit), 2))
            bit *= 2
        return there

    def across_copy(i, g):
        return pltpu.make_async_remote_copy(
            src_ref=gat.at[0, g],
            dst_ref=gat.at[2 * i, g],
            send_sem=gat_send.at[2 * i, g],
            recv_sem=gat_recv.at[2 * i, g],
            device_id=(2 * chip_at(source_mask(i, core)) + core, z),
            device_id_type=mesh_ids,
        )

    relayed = chips == 4

    def relay_copy(slot, g):
        mask = source_mask(lax.div(slot, 2), core)
        return pltpu.make_async_remote_copy(
            src_ref=gat.at[slot, g],
            dst_ref=gat.at[6, g],
            send_sem=gat_send.at[6, g],
            recv_sem=gat_recv.at[6, g],
            device_id=(2 * chip_at(3 - mask) + core, z),
            device_id_type=mesh_ids,
        )

    def arrival(slot, g):
        return pltpu.make_async_remote_copy(
            src_ref=gat.at[slot, g],
            dst_ref=gat.at[slot, g],
            send_sem=gat_send.at[slot, g],
            recv_sem=gat_recv.at[slot, g],
            device_id=(partner, z),
            device_id_type=mesh_ids,
        )

    for g in range(groups_here):
        mine = range(g * per, (g + 1) * per)
        spans = [slice(c * tile, (c + 1) * tile) for c in mine]
        output_map = maps_conv[:, span_maps + g * STATE : span_maps + (g + 1) * STATE]
        squares = jnp.zeros((length, 128), f32)
        for first in range(0, per, 2):
            link_all(levels - 1, g * per + first, g * per + first + 2)
            carried = [
                jnp.dot(output_map, state[c].astype(bf16), preferred_element_type=f32)
                for c in mine[first : first + 2]
            ]
            grown = [spread(growth[...], span) for span in spans[first : first + 2]]
            for span, more, scale in zip(spans[first : first + 2], carried, grown):
                total = y[:, span] + more * scale
                total = total + channel_rows[8:9, span] * values[:, span].astype(f32)
                total = total * jax.nn.silu(gate_ref[:, span].astype(f32))
                y[:, span] = total
                for d in range(0, tile, 128):
                    squares = squares + total[:, d : d + 128] * total[:, d : d + 128]
        scale = lax.rsqrt(jnp.sum(squares, axis=1, keepdims=True) / group_width + 1e-05)
        for c, span in enumerate(spans):
            gat[0, g, :, c * tile : (c + 1) * tile] = (
                y[:, span] * scale * gain_ref[:, span]
            ).astype(bf16)
        partner_copy(1, g).start()
        if chips > 1:
            across_copy(1, g).start()

    def chain_z(step, j, buffer, send, recv, to):
        return pltpu.make_async_remote_copy(
            src_ref=part.at[step, pl.ds(j * rows, rows)],
            dst_ref=buffer.at[step, pl.ds(j * rows, rows)],
            send_sem=send.at[step, j],
            recv_sem=recv.at[step, j],
            device_id=(me, to),
            device_id_type=mesh_ids,
        )

    def slot_of(step):
        return jnp.where(step == n - 1, n - 3, jnp.where(step >= n - 3, step + 1, step))

    def owner(step):
        slot = slot_of(step)
        who = core + lax.rem(slot, 2) * (1 - 2 * core)
        return 2 * chip_at(source_mask(lax.div(slot, 2), who)) + who

    def columns(sender):
        return pl.ds(pl.multiple_of(sender * width, width), width)

    def own_rows():
        return pl.ds(pl.multiple_of(z * rows, rows), rows)

    def out_copy(step, sender):
        return pltpu.make_async_remote_copy(
            src_ref=part.at[step, own_rows()],
            dst_ref=out_ref.at[:, columns(sender)],
            send_sem=out_send.at[step],
            recv_sem=out_recv.at[sender],
            device_id=(owner(step), z),
            device_id_type=mesh_ids,
        )

    pieces = 2 if rows % 32 == 0 else 1
    size = rows // pieces

    def piece_z(j, h, buffer, send, recv, to):
        span = pl.ds(j * rows + h * size, size)
        return pltpu.make_async_remote_copy(
            src_ref=part.at[n - 1, span],
            dst_ref=buffer.at[n - 1, span],
            send_sem=send.at[n - 1 + h, j],
            recv_sem=recv.at[n - 1 + h, j],
            device_id=(me, to),
            device_id_type=mesh_ids,
        )

    def piece_out(h, sender):
        mine = pl.ds(pl.multiple_of(z * rows + h * size, size), size)
        return pltpu.make_async_remote_copy(
            src_ref=part.at[n - 1, mine],
            dst_ref=out_ref.at[pl.ds(h * size, size), columns(sender)],
            send_sem=out_send.at[n - 1 + h],
            recv_sem=out_recv.at[sender if h == 0 else n],
            device_id=(owner(n - 1), z),
            device_id_type=mesh_ids,
        )

    def own_copy():
        return pltpu.make_async_copy(part.at[0, own_rows()], out_ref.at[:, columns(me)], own_sem)

    def added(step, j, buffer):
        span = pl.ds(j * rows, rows)
        part[step, span] = (
            part[step, span].astype(f32) + buffer[step, span].astype(f32)
        ).astype(bf16)

    up_lag, down_lag = z, m - 1 - z
    held = min(3, n - 1)
    last_lag = m - 1 + max(held - 2, 0)
    wide = min(width, 256)

    loads[14].wait()

    def turn(tau, carry):
        @pl.when(tau < n)
        def _():
            slot = slot_of(tau)
            direct = (slot > 0) & (lax.rem(slot, 2) == 0)

            @pl.when(direct)
            def _():
                for g in range(groups_here):
                    arrival(slot, g).wait_send()

            @pl.when(direct & (slot < (4 if relayed else n - 2)))
            def _():
                for g in range(groups_here):
                    across_copy(lax.div(slot, 2) + 1, g).start()

            @pl.when(tau > 0)
            def _():
                for g in range(groups_here):
                    arrival(slot, g).wait_recv()

            @pl.when(direct)
            def _():
                for g in range(groups_here):
                    partner_copy(slot + 1, g).start()

            if relayed:
                @pl.when((slot == 3) | (slot == 4))
                def _():
                    source = jnp.where(slot == 3, 2, 4)
                    along = source_mask(lax.div(source, 2), core) == 1
                    for g in range(groups_here):
                        @pl.when(along == (g < (groups_here + 1) // 2))
                        def _():
                            relay_copy(source, g).start()

            for c in range(0, width, wide):
                total = jnp.zeros((length, wide), f32)
                for g in range(groups_here):
                    total = total + jnp.dot(
                        gat[slot, g],
                        w_ref[g * group_width : (g + 1) * group_width, c : c + wide],
                        preferred_element_type=f32,
                    )
                part[tau, :, c : c + wide] = total.astype(bf16)

        t_up = tau - up_lag

        @pl.when((t_up >= 0) & (t_up < n))
        def _():
            for j in range(m - 1, 0, -1):
                @pl.when(z < j)
                def _():
                    copy = chain_z(t_up, j, up, up_send, up_recv, z + 1)

                    @pl.when(z > 0)
                    def _():
                        copy.wait_recv()
                        added(t_up, j, up)

                    if j == 1:
                        @pl.when(t_up == n - 1)
                        def _():
                            for before in range(held, 0, -1):
                                chain_z(n - 1 - before, j, up, up_send, up_recv, z + 1).start()
                            for h in range(pieces):
                                piece_z(j, h, up, up_send, up_recv, z + 1).start()

                        @pl.when(t_up < n - 1 - held)
                        def _():
                            copy.start()
                    else:
                        copy.start()

        t_down = tau - down_lag

        @pl.when((t_down >= 0) & (t_down < n))
        def _():
            for j in range(m - 1):
                @pl.when(z > j)
                def _():
                    copy = chain_z(t_down, j, down, down_send, down_recv, z - 1)

                    @pl.when(z < m - 1)
                    def _():
                        copy.wait_recv()
                        added(t_down, j, down)

                    if j == m - 2:
                        @pl.when(t_down == n - 1)
                        def _():
                            for before in range(held, 0, -1):
                                chain_z(n - 1 - before, j, down, down_send, down_recv, z - 1).start()
                            for h in range(pieces):
                                piece_z(j, h, down, down_send, down_recv, z - 1).start()

                        @pl.when(t_down < n - 1 - held)
                        def _():
                            copy.start()
                    else:
                        copy.start()

        t_last = tau - last_lag

        @pl.when((t_last >= 0) & (t_last < n - 1))
        def _():
            for j in range(m):
                @pl.when(z == j)
                def _():
                    span = pl.ds(j * rows, rows)
                    total = part[t_last, span].astype(f32)
                    if j > 0:
                        chain_z(t_last, j, up, up_send, up_recv, z).wait_recv()
                        total = total + up[t_last, span].astype(f32)
                    if j < m - 1:
                        chain_z(t_last, j, down, down_send, down_recv, z).wait_recv()
                        total = total + down[t_last, span].astype(f32)
                    part[t_last, span] = total.astype(bf16)

            @pl.when(t_last == 0)
            def _():
                own_copy().start()

            @pl.when(t_last > 0)
            def _():
                out_copy(t_last, me).start()

        @pl.when(t_last == n - 1)
        def _():
            for j in range(m):
                @pl.when(z == j)
                def _():
                    for h in range(pieces):
                        span = pl.ds(j * rows + h * size, size)
                        total = part[n - 1, span].astype(f32)
                        if j > 0:
                            if j == 1:
                                piece_z(j, h, up, up_send, up_recv, z).wait_recv()
                            elif h == 0:
                                chain_z(n - 1, j, up, up_send, up_recv, z).wait_recv()
                            total = total + up[n - 1, span].astype(f32)
                        if j < m - 1:
                            if j == m - 2:
                                piece_z(j, h, down, down_send, down_recv, z).wait_recv()
                            elif h == 0:
                                chain_z(n - 1, j, down, down_send, down_recv, z).wait_recv()
                            total = total + down[n - 1, span].astype(f32)
                        part[n - 1, span] = total.astype(bf16)
                        piece_out(h, me).start()

        return carry

    lax.fori_loop(0, n + last_lag, turn, 0)

    def finish(step, carry):
        @pl.when(lax.rem(step, 2) == 1)
        def _():
            for g in range(groups_here):
                arrival(step, g).wait_send()

        @pl.when(step > 0)
        def _():
            end_copy(step, me).wait_send()

        for j in range(m):
            @pl.when((z < j) & ((step < n - 1) | (j != 1)))
            def _():
                chain_z(step, j, up, up_send, up_recv, z).wait_send()

            @pl.when((z > j) & ((step < n - 1) | (j != m - 2)))
            def _():
                chain_z(step, j, down, down_send, down_recv, z).wait_send()

        @pl.when((step > 0) & (step < n - 1))
        def _():
            out_copy(step, me).wait_send()

        sender = lax.rem(me + step, n)

        @pl.when((step > 0) & (sender != ending))
        def _():
            out_copy(step, sender).wait_recv()

        return carry

    ending_slot = slot_of(n - 1)
    ending = 2 * chip_at(source_mask(lax.div(ending_slot, 2), core)) + core
    ending = ending + lax.rem(ending_slot, 2) * (1 - 2 * core)
    lax.fori_loop(0, n, finish, 0)
    for h in range(pieces):
        @pl.when(z == 0)
        def _():
            piece_z(1, h, up, up_send, up_recv, z).wait_send()

        @pl.when(z == m - 1)
        def _():
            piece_z(m - 2, h, down, down_send, down_recv, z).wait_send()

        piece_out(h, me).wait_send()
        piece_out(h, ending).wait_recv()
    own_copy().wait()

    @pl.when(has_right)
    def _():
        for which in range(3):
            rim_copy(which).wait_send()

    def sent(c, carry):
        for level in range(levels):
            @pl.when(sends(level))
            def _():
                for hop in hops(level):
                    chain_send_copy(level, hop, c).wait_send()

            if level > 0:
                @pl.when(gets(level) & odd)
                def _():
                    chain_forward(level, c).wait_send()

        return carry

    lax.fori_loop(0, tiles, sent, 0)


def layer(x, gate, maps, step_raw, rate, skip, taps, base, map_taps, map_base, gain, weight):
    n, m = lax.axis_size("seq"), lax.axis_size("tp")
    length, channels = x.shape
    heads = rate.shape[0]
    per_group = HEADS // GROUPS
    groups_here = heads // per_group
    tile = max(128, channels // 8)
    tiles = channels // tile
    width = weight.shape[1]
    span_maps = 2 * groups_here * STATE
    rim = 16
    levels = n.bit_length() - 1
    lanes = -(-heads // 128) * 128
    bf16, f32 = jnp.bfloat16, jnp.float32
    dma = pltpu.SemaphoreType.DMA
    operands = (
        x, gate, maps, step_raw.T, rate[None], skip[None], taps, base[None],
        map_taps, map_base[None], gain[None], weight,
    )
    blocks = pltpu.VMEM((n, length, width), bf16)
    return pl.pallas_call(
        functools.partial(layer_kernel, n, m, per_group),
        out_shape=jax.ShapeDtypeStruct((length // m, n * width), bf16),
        in_specs=[pl.BlockSpec(memory_space=pl.ANY)] * len(operands),
        out_specs=pl.BlockSpec(memory_space=pl.ANY),
        scratch_shapes=[
            pltpu.VMEM((length, channels), bf16),
            pltpu.VMEM((length, channels), bf16),
            pltpu.VMEM((length, span_maps), bf16),
            pltpu.VMEM((heads, length), f32),
            pltpu.VMEM((1, heads), f32),
            pltpu.VMEM((1, heads), f32),
            pltpu.VMEM((CONV, channels), f32),
            pltpu.VMEM((1, channels), f32),
            pltpu.VMEM((CONV, span_maps), f32),
            pltpu.VMEM((1, span_maps), f32),
            pltpu.VMEM((1, channels), f32),
            pltpu.VMEM(weight.shape, bf16),
            dma((15,)),
            pltpu.VMEM((rim, channels), bf16),
            pltpu.VMEM((rim, span_maps), bf16),
            pltpu.VMEM((length, max(tile, STATE)), f32),
            pltpu.VMEM((length, channels), bf16),
            pltpu.VMEM((length, span_maps), bf16),
            pltpu.VMEM((length, channels), f32),
            pltpu.VMEM((groups_here, length, length), f32),
            pltpu.VMEM((tiles, STATE, tile), f32),
            pltpu.VMEM((tiles, STATE, tile), f32),
            pltpu.VMEM((levels, tiles, STATE, tile), bf16),
            pltpu.VMEM((tiles, STATE, tile), bf16),
            pltpu.VMEM((length, 8 * heads), bf16),
            pltpu.VMEM((8 * heads, length), bf16),
            pltpu.VMEM((groups_here, STATE, length), bf16),
            pltpu.VMEM((length, 4 * heads), bf16),
            pltpu.VMEM((length, 4 * heads), bf16),
            pltpu.VMEM((8, lanes), f32),
            pltpu.VMEM((n, 8, lanes), f32),
            pltpu.VMEM((4 * heads, channels), bf16),
            pltpu.VMEM((16, channels), f32),
            pltpu.VMEM((levels, 16, channels), f32),
            pltpu.VMEM((n, groups_here, length, channels // groups_here), bf16),
            blocks,
            blocks,
            blocks,
            dma((3,)),
            dma((3,)),
            dma((n,)),
            dma((n,)),
            dma((max(1, n // 4), tiles)),
            dma((levels, tiles)),
            dma((levels, tiles)),
            dma((n, groups_here)),
            dma((n, groups_here)),
            dma((n + 1, m)),
            dma((n + 1, m)),
            dma((n + 1, m)),
            dma((n + 1, m)),
            dma((n + 1,)),
            dma((n + 1,)),
            dma(()),
        ],
        compiler_params=pltpu.CompilerParams(
            collective_id=2, has_side_effects=True, vmem_limit_bytes=60 << 20
        ),
        cost_estimate=pl.CostEstimate(
            flops=2 * n * length * channels * width,
            bytes_accessed=2 * (channels * width + 3 * length * channels),
            transcendentals=0,
        ),
    )(*operands)


def shards(
    conv_values,
    gate_values,
    conv_maps,
    step_raw,
    decay_log,
    skip_gain,
    values_kernel,
    values_offset,
    maps_kernel,
    maps_offset,
    norm_weight,
    out_weight,
    residual,
):
    length = conv_values.shape[0]
    heads_dev = decay_log.shape[0]
    per_group = HEADS // GROUPS
    whole_groups = heads_dev % per_group == 0
    chips = lax.axis_size("seq") // 2
    paired = lax.axis_size("seq") == 2 * chips and chips & (chips - 1) == 0
    if whole_groups and paired and heads_dev % 32 == 0:
        summed = layer(
            conv_values, gate_values, conv_maps, step_raw, decay_log, skip_gain, values_kernel,
            values_offset, maps_kernel, maps_offset, norm_weight, out_weight,
        )
        return residual.astype(jnp.float32) + summed.astype(jnp.float32)
    step_size = jax.nn.softplus(step_raw)
    place = jnp.arange(length, dtype=jnp.int32)
    cum_log = jnp.dot(
        (place[:, None] >= place[None, :]).astype(jnp.float32),
        -jnp.exp(decay_log)[None, :] * step_size,
        precision=lax.Precision.HIGHEST,
    )
    normed = front(
        conv_values, gate_values, conv_maps, cum_log, step_size, skip_gain, values_kernel,
        values_offset, maps_kernel, maps_offset, norm_weight, whole_groups,
    )
    if not whole_groups:
        gated_out = normed.reshape(length, heads_dev, HEAD_DIM)
        head_squares = jnp.sum(gated_out * gated_out, axis=2)
        all_heads = lax.all_gather(head_squares, "tp", axis=1, tiled=True)
        group_totals = jnp.sum(all_heads.reshape(length, GROUPS, per_group), axis=2)
        heads_here = lax.axis_index("tp") * heads_dev + jnp.arange(heads_dev, dtype=jnp.int32)
        inv_rms = lax.rsqrt(
            group_totals[:, heads_here // per_group] / (per_group * HEAD_DIM) + 1e-05
        )
        normed = (
            (gated_out * inv_rms[:, :, None]).reshape(length, heads_dev * HEAD_DIM)
            * norm_weight[None, :]
        ).astype(jnp.bfloat16)
    blocks = mix(normed, out_weight)
    summed = jnp.transpose(blocks, (1, 0, 2)).reshape(residual.shape).astype(jnp.float32)
    return residual.astype(jnp.float32) + summed


def solution(mesh):
    placed = (
        P("seq", "tp"),
        P("seq", "tp"),
        P("seq", None),
        P("seq", "tp"),
        P("tp"),
        P("tp"),
        P(None, "tp"),
        P("tp"),
        P(),
        P(),
        P("tp"),
        P("tp", "seq"),
        P(("seq", "tp"), None),
    )
    return jax.shard_map(
        shards, mesh=mesh, in_specs=placed, out_specs=P(("seq", "tp"), None), check_vma=False
    )
```

```python
import functools

import jax
import jax.numpy as jnp
from jax import lax
from jax.experimental import pallas as pl
from jax.experimental.pallas import tpu as pltpu
from jax.sharding import PartitionSpec as P

HEADS = 128
HEAD_DIM = 64
STATE = 128
GROUPS = 8
CONV = 4


def ring_place(spot, size):
    if size % 4:
        return spot
    half = size // 2
    past = spot - half
    turned = half + (half - 2 - 2 * lax.div(past, 2)) + lax.rem(past, 2)
    return jnp.where(spot < half, spot, turned)


def mix_kernel(
    n, m, x_ref, w_ref, out_ref, gat, part, up, down,
    own_sem, gat_send, gat_recv, up_send, up_recv, down_send, down_recv, out_send, out_recv,
):
    mesh_ids = pl.DeviceIdType.MESH
    me, z = lax.axis_index("seq"), lax.axis_index("tp")
    spot = ring_place(me, n)
    right = ring_place(lax.rem(spot + 1, n), n)
    left = ring_place(lax.rem(spot + n - 1, n), n)
    half = gat.shape[2]
    depth = gat.shape[3]
    width = w_ref.shape[1]
    rows = part.shape[1] // m
    tile = min(width, 256)

    own = [
        pltpu.make_async_copy(x_ref.at[pl.ds(d * half, half)], gat.at[0, d], own_sem.at[d])
        for d in range(2)
    ]
    for copy in own:
        copy.start()

    barrier = pltpu.get_barrier_semaphore()

    def greet(step, carry):
        pl.semaphore_signal(
            barrier, inc=1, device_id=(lax.rem(me + step, n), z), device_id_type=mesh_ids
        )
        return carry

    lax.fori_loop(1, n, greet, 0)

    @pl.when(z > 0)
    def _():
        pl.semaphore_signal(barrier, inc=1, device_id=(me, z - 1), device_id_type=mesh_ids)

    @pl.when(z < m - 1)
    def _():
        pl.semaphore_signal(barrier, inc=1, device_id=(me, z + 1), device_id_type=mesh_ids)

    beside = (z > 0).astype(jnp.int32) + (z < m - 1).astype(jnp.int32)
    pl.semaphore_wait(barrier, n - 1 + beside)

    for copy in own:
        copy.wait()

    def gather_copy(step, d):
        return pltpu.make_async_remote_copy(
            src_ref=gat.at[step, d],
            dst_ref=gat.at[step + 1, d],
            send_sem=gat_send.at[step, d],
            recv_sem=gat_recv.at[step + 1, d],
            device_id=(right if d == 0 else left, z),
            device_id_type=mesh_ids,
        )

    def gather_arrival(step, d):
        return pltpu.make_async_remote_copy(
            src_ref=gat.at[step, d],
            dst_ref=gat.at[step, d],
            send_sem=gat_send.at[step, d],
            recv_sem=gat_recv.at[step, d],
            device_id=(right if d == 0 else left, z),
            device_id_type=mesh_ids,
        )

    def chain_copy(step, j, buffer, send, recv, to):
        return pltpu.make_async_remote_copy(
            src_ref=part.at[step, pl.ds(j * rows, rows)],
            dst_ref=buffer.at[step, pl.ds(j * rows, rows)],
            send_sem=send.at[step, j],
            recv_sem=recv.at[step, j],
            device_id=(me, to),
            device_id_type=mesh_ids,
        )

    def owner(step):
        there = jnp.where(z < m // 2, spot - step + n, spot + step)
        return ring_place(lax.rem(there, n), n)

    def out_copy(step, sender):
        return pltpu.make_async_remote_copy(
            src_ref=part.at[step, pl.ds(pl.multiple_of(z * rows, rows), rows)],
            dst_ref=out_ref.at[sender],
            send_sem=out_send.at[step],
            recv_sem=out_recv.at[sender],
            device_id=(owner(step), z),
            device_id_type=mesh_ids,
        )

    def added(step, j, buffer):
        span = pl.ds(j * rows, rows)
        part[step, span] = (
            part[step, span].astype(jnp.float32) + buffer[step, span].astype(jnp.float32)
        ).astype(jnp.bfloat16)

    up_lag, down_lag = z, m - 1 - z
    last_lag = jnp.maximum(up_lag, down_lag)

    def turn(tau, carry):
        @pl.when(tau < n)
        def _():
            @pl.when(tau > 0)
            def _():
                for d in range(2):
                    gather_arrival(tau, d).wait_recv()

            @pl.when(tau < n - 1)
            def _():
                for d in range(2):
                    gather_copy(tau, d).start()

            block = gat[tau].reshape(2 * half, depth)
            for c in range(0, width, tile):
                part[tau, :, c : c + tile] = jnp.dot(
                    block, w_ref[:, c : c + tile], preferred_element_type=jnp.float32
                ).astype(jnp.bfloat16)

        t_up = tau - up_lag

        @pl.when((t_up >= 0) & (t_up < n))
        def _():
            for j in range(m - 1, 0, -1):
                @pl.when(z < j)
                def _():
                    copy = chain_copy(t_up, j, up, up_send, up_recv, z + 1)

                    @pl.when(z > 0)
                    def _():
                        copy.wait_recv()
                        added(t_up, j, up)

                    copy.start()

        t_down = tau - down_lag

        @pl.when((t_down >= 0) & (t_down < n))
        def _():
            for j in range(m - 1):
                @pl.when(z > j)
                def _():
                    copy = chain_copy(t_down, j, down, down_send, down_recv, z - 1)

                    @pl.when(z < m - 1)
                    def _():
                        copy.wait_recv()
                        added(t_down, j, down)

                    copy.start()

        t_last = tau - last_lag

        @pl.when((t_last >= 0) & (t_last < n))
        def _():
            for j in range(m):
                @pl.when(z == j)
                def _():
                    span = pl.ds(j * rows, rows)
                    total = part[t_last, span].astype(jnp.float32)
                    if j > 0:
                        chain_copy(t_last, j, up, up_send, up_recv, z).wait_recv()
                        total = total + up[t_last, span].astype(jnp.float32)
                    if j < m - 1:
                        chain_copy(t_last, j, down, down_send, down_recv, z).wait_recv()
                        total = total + down[t_last, span].astype(jnp.float32)
                    part[t_last, span] = total.astype(jnp.bfloat16)

            @pl.when(t_last == 0)
            def _():
                out_ref[me] = part[0, pl.ds(pl.multiple_of(z * rows, rows), rows)]

            @pl.when(t_last > 0)
            def _():
                out_copy(t_last, me).start()

        return carry

    lax.fori_loop(0, n + m - 1, turn, 0)

    def finish(step, carry):
        @pl.when(step < n - 1)
        def _():
            for d in range(2):
                gather_copy(step, d).wait_send()

        for j in range(m):
            @pl.when(z < j)
            def _():
                chain_copy(step, j, up, up_send, up_recv, z).wait_send()

            @pl.when(z > j)
            def _():
                chain_copy(step, j, down, down_send, down_recv, z).wait_send()

        @pl.when(step > 0)
        def _():
            out_copy(step, me).wait_send()
            out_copy(step, lax.rem(me + step, n)).wait_recv()

        return carry

    lax.fori_loop(0, n, finish, 0)


def mix(normed, weight):
    n, m = lax.axis_size("seq"), lax.axis_size("tp")
    length, depth = normed.shape
    width = weight.shape[1]
    rows = length // m
    half = length // 2
    slots = pltpu.VMEM((n, length, width), jnp.bfloat16)
    dma = pltpu.SemaphoreType.DMA
    vmem = pl.BlockSpec(memory_space=pltpu.VMEM)
    return pl.pallas_call(
        functools.partial(mix_kernel, n, m),
        out_shape=jax.ShapeDtypeStruct((n, rows, width), jnp.bfloat16),
        in_specs=[pl.BlockSpec(memory_space=pl.ANY), vmem],
        out_specs=vmem,
        scratch_shapes=[
            pltpu.VMEM((n, 2, half, depth), jnp.bfloat16),
            slots,
            slots,
            slots,
            dma((2,)),
            dma((n, 2)),
            dma((n, 2)),
            dma((n, m)),
            dma((n, m)),
            dma((n, m)),
            dma((n, m)),
            dma((n,)),
            dma((n,)),
        ],
        compiler_params=pltpu.CompilerParams(
            collective_id=0, has_side_effects=True, vmem_limit_bytes=48 << 20
        ),
        cost_estimate=pl.CostEstimate(
            flops=2 * n * length * depth * width,
            bytes_accessed=2 * (depth * width + length * depth),
            transcendentals=0,
        ),
    )(normed, weight)


def front_kernel(
    n, per_group, whole_groups, x_ref, gate_ref, maps_ref, cum_ref, cum_t_ref, step_ref, step_t_ref,
    decay_ref, skip_ref, taps_ref, base_ref, map_taps_ref, map_base_ref, gain_ref, out_ref,
    rim_x, rim_maps, pad, values, y, b_maps, c_maps, scores, local, arrived, leaving,
    rim_send, rim_recv, chain_send, chain_recv,
):
    mesh_ids = pl.DeviceIdType.MESH
    exact = lax.Precision.HIGHEST
    me, z = lax.axis_index("seq"), lax.axis_index("tp")
    length, channels = x_ref.shape
    heads = cum_ref.shape[1]
    groups_here = scores.shape[0]
    first_group = lax.div(z * heads, per_group)
    tile = arrived.shape[2]
    tiles = channels // tile
    group_width = channels // groups_here
    rim = rim_x.shape[0]

    barrier = pltpu.get_barrier_semaphore()
    has_left, has_right = me > 0, me < n - 1

    @pl.when(has_left)
    def _():
        pl.semaphore_signal(barrier, inc=1, device_id=(me - 1, z), device_id_type=mesh_ids)

    @pl.when(has_right)
    def _():
        pl.semaphore_signal(barrier, inc=1, device_id=(me + 1, z), device_id_type=mesh_ids)

    pl.semaphore_wait(barrier, has_left.astype(jnp.int32) + has_right.astype(jnp.int32))

    def rim_copy(which):
        source, target = ((x_ref, rim_x), (maps_ref, rim_maps))[which]
        return pltpu.make_async_remote_copy(
            src_ref=source.at[pl.ds(length - rim, rim)],
            dst_ref=target,
            send_sem=rim_send.at[which],
            recv_sem=rim_recv.at[which],
            device_id=(me + 1, z),
            device_id_type=mesh_ids,
        )

    @pl.when(has_right)
    def _():
        for which in range(2):
            rim_copy(which).start()

    @pl.when(has_left)
    def _():
        for which in range(2):
            rim_copy(which).wait_recv()

    @pl.when(jnp.logical_not(has_left))
    def _():
        rim_x[...] = jnp.zeros_like(rim_x)
        rim_maps[...] = jnp.zeros_like(rim_maps)

    def conv(rows_ref, rim_ref, taps, base, start, size):
        span = pl.ds(start, size)
        pad[0:rim, 0:size] = rim_ref[:, span].astype(jnp.float32)
        pad[rim : rim + length, 0:size] = rows_ref[:, span].astype(jnp.float32)
        total = base[:, span]
        for k in range(CONV):
            at = rim - (CONV - 1) + k
            total = total + taps[k : k + 1, span] * pad[at : at + length, 0:size]
        return jax.nn.silu(total).astype(jnp.bfloat16)

    for g in range(groups_here):
        at = pl.multiple_of((first_group + g) * STATE, STATE)
        b_maps[g] = conv(maps_ref, rim_maps, map_taps_ref, map_base_ref, at, STATE)
        at = pl.multiple_of((GROUPS + first_group + g) * STATE, STATE)
        c_maps[g] = conv(maps_ref, rim_maps, map_taps_ref, map_base_ref, at, STATE)
        scores[g] = lax.dot_general(
            c_maps[g], b_maps[g], (((1,), (1,)), ((), ())), preferred_element_type=jnp.float32
        )

    def spread(per_head, start):
        head = lax.broadcasted_iota(jnp.int32, (heads, tile), 0) * HEAD_DIM
        lane = lax.broadcasted_iota(jnp.int32, (heads, tile), 1) + start
        chosen = ((lane >= head) & (lane < head + HEAD_DIM)).astype(jnp.float32)
        return jnp.dot(
            per_head, chosen, precision=exact, preferred_element_type=jnp.float32
        )

    cum = cum_ref[...]
    end_weight = jnp.exp(cum[length - 1 : length] - cum) * step_ref[...]
    grown = jnp.exp(cum)

    def states(c, carry):
        start = pl.multiple_of(c * tile, tile)
        span = pl.ds(start, tile)
        value = conv(x_ref, rim_x, taps_ref, base_ref, start, tile)
        values[:, span] = value
        weighted = (value.astype(jnp.float32) * spread(end_weight, start)).astype(jnp.bfloat16)
        g = lax.div(start, group_width)
        local[c] = lax.dot_general(
            b_maps[g], weighted, (((0,), (0,)), ((), ())), preferred_element_type=jnp.float32
        )
        return carry

    lax.fori_loop(0, tiles, states, 0)

    def chain_copy(c):
        return pltpu.make_async_remote_copy(
            src_ref=leaving.at[c],
            dst_ref=arrived.at[c],
            send_sem=chain_send.at[c],
            recv_sem=chain_recv.at[c],
            device_id=(me + 1, z),
            device_id_type=mesh_ids,
        )

    def link(c, carry):
        span = pl.ds(pl.multiple_of(c * tile, tile), tile)

        @pl.when(has_left)
        def _():
            chain_copy(c).wait_recv()

        @pl.when(jnp.logical_not(has_left))
        def _():
            arrived[c] = jnp.zeros_like(arrived[c])

        @pl.when(has_right)
        def _():
            leaving[c] = (
                decay_ref[:, span] * arrived[c].astype(jnp.float32) + local[c]
            ).astype(jnp.bfloat16)
            chain_copy(c).start()

        return carry

    pair = 2 * HEAD_DIM
    causal = lax.broadcasted_iota(jnp.int32, (length, length), 0) >= lax.broadcasted_iota(
        jnp.int32, (length, length), 1
    )

    def within(q, carry):
        span = pl.ds(pl.multiple_of(q * pair, pair), pair)
        value = values[:, span]
        g = lax.div(q * pair, group_width)
        sums = []
        for e in range(2):
            h = 2 * q + e
            lane = lax.broadcasted_iota(jnp.int32, (length, heads), 1)
            column = jnp.sum(jnp.where(lane == h, cum_ref[...], 0.0), axis=1, keepdims=True)
            gap = column - cum_t_ref[pl.ds(h, 1), :]
            kernel = jnp.where(causal, jnp.exp(jnp.where(causal, gap, 0.0)), 0.0)
            mixing = kernel * scores[g] * step_t_ref[pl.ds(h, 1), :]
            sums.append(
                jnp.dot(mixing.astype(jnp.bfloat16), value, preferred_element_type=jnp.float32)
            )
        first = lax.broadcasted_iota(jnp.int32, (length, pair), 1) < HEAD_DIM
        y[:, span] = jnp.where(first, sums[0], sums[1])
        return carry

    late = me >= n // 2

    def phase(turn, carry):
        @pl.when((turn == 0) == late)
        def _():
            lax.fori_loop(0, channels // pair, within, 0)

        @pl.when(turn == 0)
        def _():
            lax.fori_loop(0, tiles, link, 0)

        return carry

    lax.fori_loop(0, 2, phase, 0)

    for g in range(groups_here):
        per = group_width // tile

        def gated(c, squares):
            c = c + g * per
            start = pl.multiple_of(c * tile, tile)
            span = pl.ds(start, tile)
            carried = jnp.dot(
                c_maps[g], arrived[c], preferred_element_type=jnp.float32
            ) * spread(grown, start)
            total = y[:, span] + carried + skip_ref[:, span] * values[:, span].astype(jnp.float32)
            total = total * jax.nn.silu(gate_ref[:, span].astype(jnp.float32))
            y[:, span] = total
            return squares + jnp.sum(total * total, axis=1, keepdims=True)

        squares = lax.fori_loop(0, per, gated, jnp.zeros((length, 1), jnp.float32))
        scale = lax.rsqrt(squares / group_width + 1e-05)

        def scaled(c, carry):
            span = pl.ds(pl.multiple_of((c + g * per) * tile, tile), tile)
            if whole_groups:
                out_ref[:, span] = (y[:, span] * scale * gain_ref[:, span]).astype(out_ref.dtype)
            else:
                out_ref[:, span] = y[:, span]
            return carry

        lax.fori_loop(0, per, scaled, 0)

    @pl.when(has_right)
    def _():
        for which in range(2):
            rim_copy(which).wait_send()

        def sent(c, carry):
            chain_copy(c).wait_send()
            return carry

        lax.fori_loop(0, tiles, sent, 0)


def front(x, gate, maps, cum, step, skip, taps, base, map_taps, map_base, gain, whole_groups):
    n = lax.axis_size("seq")
    length, channels = x.shape
    heads = cum.shape[1]
    per_group = HEADS // GROUPS
    groups_here = max(1, heads // per_group)
    tile = max(128, channels // 8)
    tiles = channels // tile
    rim = 16
    bf16, f32 = jnp.bfloat16, jnp.float32
    dma = pltpu.SemaphoreType.DMA
    vmem = pl.BlockSpec(memory_space=pltpu.VMEM)
    decay = jnp.repeat(jnp.exp(cum[-1]), HEAD_DIM)[None]
    skips = jnp.repeat(skip, HEAD_DIM)[None]
    operands = (
        x, gate, maps, cum, cum.T, step, step.T, decay, skips,
        taps, base[None], map_taps, map_base[None], gain[None],
    )
    return pl.pallas_call(
        functools.partial(front_kernel, n, per_group, whole_groups),
        out_shape=jax.ShapeDtypeStruct((length, channels), bf16 if whole_groups else f32),
        in_specs=[vmem] * len(operands),
        out_specs=vmem,
        scratch_shapes=[
            pltpu.VMEM((rim, channels), bf16),
            pltpu.VMEM((rim, maps.shape[1]), bf16),
            pltpu.VMEM((rim + length, max(tile, STATE)), f32),
            pltpu.VMEM((length, channels), bf16),
            pltpu.VMEM((length, channels), f32),
            pltpu.VMEM((groups_here, length, STATE), bf16),
            pltpu.VMEM((groups_here, length, STATE), bf16),
            pltpu.VMEM((groups_here, length, length), f32),
            pltpu.VMEM((tiles, STATE, tile), f32),
            pltpu.VMEM((tiles, STATE, tile), bf16),
            pltpu.VMEM((tiles, STATE, tile), bf16),
            dma((2,)),
            dma((2,)),
            dma((tiles,)),
            dma((tiles,)),
        ],
        compiler_params=pltpu.CompilerParams(
            collective_id=1, has_side_effects=True, vmem_limit_bytes=48 << 20
        ),
    )(*operands)


LOG2E = 1.4426950408889634


def three(value):
    high = value.astype(jnp.bfloat16)
    rest = value - high.astype(jnp.float32)
    middle = rest.astype(jnp.bfloat16)
    low = (rest - middle.astype(jnp.float32)).astype(jnp.bfloat16)
    return high, middle, low


def layer_kernel(
    n, m, per_group, x_hbm, gate_hbm, maps_hbm, step_hbm, rate_hbm, skip_hbm, taps_hbm, base_hbm,
    map_taps_hbm, map_base_hbm, gain_hbm, w_hbm, out_ref,
    x_ref, gate_ref, maps_ref, step_ref, rate_ref, skip_ref, taps_ref, base_ref, map_taps_ref,
    map_base_ref, gain_ref, w_ref, in_sem,
    rim_x, rim_maps, pad, values, maps_conv, y, scores, local, state, arrived, leaving,
    gap_left, gap_right, turned_maps, ends, growth, own_end, all_ends, chosen, channel_rows, prefix_rows,
    gat, part, up, down,
    rim_send, rim_recv, end_send, end_recv, chain_send, chain_recv, forward_send,
    gat_send, gat_recv, up_send, up_recv, down_send, down_recv, out_send, out_recv,
    own_sem,
):
    mesh_ids = pl.DeviceIdType.MESH
    exact = lax.Precision.HIGHEST
    f32, bf16 = jnp.float32, jnp.bfloat16
    me, z = lax.axis_index("seq"), lax.axis_index("tp")
    chips = n // 2
    chip, core = lax.div(me, 2), lax.rem(me, 2)
    partner = me + 1 - 2 * core
    length, channels = x_ref.shape
    heads = step_ref.shape[0]
    levels = arrived.shape[0]
    groups_here = scores.shape[0]
    first_group = z * groups_here
    span_maps = groups_here * STATE
    tile = arrived.shape[3]
    tiles = channels // tile
    group_width = channels // groups_here
    rim = rim_x.shape[0]
    width = w_ref.shape[1]
    rows = length // m
    half = length // 2

    at_b = pl.ds(pl.multiple_of(first_group * STATE, STATE), span_maps)
    at_c = pl.ds(pl.multiple_of((GROUPS + first_group) * STATE, STATE), span_maps)
    to_b, to_c = pl.ds(0, span_maps), pl.ds(span_maps, span_maps)
    fetches = (
        (step_hbm, step_ref),
        (rate_hbm, rate_ref),
        (skip_hbm, skip_ref),
        (maps_hbm.at[:, at_b], maps_ref.at[:, to_b]),
        (maps_hbm.at[:, at_c], maps_ref.at[:, to_c]),
        (map_taps_hbm.at[:, at_b], map_taps_ref.at[:, to_b]),
        (map_taps_hbm.at[:, at_c], map_taps_ref.at[:, to_c]),
        (map_base_hbm.at[:, at_b], map_base_ref.at[:, to_b]),
        (map_base_hbm.at[:, at_c], map_base_ref.at[:, to_c]),
        (taps_hbm, taps_ref),
        (base_hbm, base_ref),
        (x_hbm, x_ref),
        (gate_hbm, gate_ref),
        (gain_hbm, gain_ref),
        (w_hbm, w_ref),
    )
    loads = [
        pltpu.make_async_copy(source, target, in_sem.at[i])
        for i, (source, target) in enumerate(fetches)
    ]

    barrier = pltpu.get_barrier_semaphore()

    def greet(step, carry):
        pl.semaphore_signal(
            barrier, inc=1, device_id=(lax.rem(me + step, n), z), device_id_type=mesh_ids
        )
        return carry

    lax.fori_loop(1, n, greet, 0)

    @pl.when(z > 0)
    def _():
        pl.semaphore_signal(barrier, inc=1, device_id=(me, z - 1), device_id_type=mesh_ids)

    @pl.when(z < m - 1)
    def _():
        pl.semaphore_signal(barrier, inc=1, device_id=(me, z + 1), device_id_type=mesh_ids)

    for load in loads[:12]:
        load.start()

    has_left, has_right = me > 0, me < n - 1
    odd = core == 1

    for load in loads[:3]:
        load.wait()

    def turned(value):
        size = value.shape[0]
        same = lax.broadcasted_iota(jnp.int32, (size, size), 0) == lax.broadcasted_iota(
            jnp.int32, (size, size), 1
        )
        return lax.dot_general(
            value, same.astype(f32), (((0,), (0,)), ((), ())), precision=exact,
            preferred_element_type=f32,
        )

    step = jax.nn.softplus(turned(step_ref[...]))
    log_decay = -jnp.exp(rate_ref[...]) * step
    row = lax.broadcasted_iota(jnp.int32, (length, length), 0)
    column = lax.broadcasted_iota(jnp.int32, (length, length), 1)
    lower = (row >= column).astype(f32)
    cum = jnp.dot(lower, log_decay, precision=exact, preferred_element_type=f32)
    final = cum[length - 1 : length]
    ones = jnp.ones((length, heads), bf16)
    blank = jnp.zeros((length, heads), bf16)
    gap_left[...] = jnp.concatenate(
        [*three(cum * LOG2E), ones, ones, ones, blank, blank], axis=1
    )
    source_log = jnp.log(step) * LOG2E - cum * LOG2E
    source_rows = turned(source_log)
    unit = jnp.ones((heads, length), bf16)
    gap_right[...] = jnp.concatenate(
        [unit, unit, unit, *three(source_rows), unit, unit], axis=0
    )
    ends[...] = jnp.concatenate([*three(jnp.exp(final - cum) * step), blank], axis=1)
    growth[...] = jnp.concatenate([*three(jnp.exp(cum)), blank], axis=1)
    lanes = own_end.shape[1]
    own_end[...] = jnp.zeros_like(own_end)
    own_end[:, 0:heads] = jnp.broadcast_to(final, (8, heads))
    all_ends[me] = jnp.zeros((8, lanes), f32)

    first_row = lax.broadcasted_iota(jnp.int32, (16, heads), 0) < 8
    two = jnp.where(first_row, jnp.exp(final), skip_ref[...])
    two = jnp.concatenate([*three(two), jnp.zeros((16, heads), bf16)], axis=1)

    def choose(c, carry):
        start = pl.multiple_of(c * tile, tile)
        slot = lax.broadcasted_iota(jnp.int32, (4 * heads, tile), 0)
        head = lax.rem(slot, heads) * HEAD_DIM
        lane = lax.broadcasted_iota(jnp.int32, (4 * heads, tile), 1) + start
        chosen[:, pl.ds(start, tile)] = (
            ((lane >= head) & (lane < head + HEAD_DIM)).astype(f32).astype(bf16)
        )
        return carry

    lax.fori_loop(0, tiles, choose, 0)

    def spread(per_head, span):
        return jnp.dot(per_head, chosen[:, span], preferred_element_type=f32)

    channel_rows[...] = spread(two, slice(None))
    for load in loads[3:9]:
        load.wait()

    def smooth(rows_ref, taps, base, out, start, size):
        span = pl.ds(start, size)
        pad[:, 0:size] = rows_ref[:, span].astype(f32)
        total = base[:, span]
        for k in range(CONV):
            at = rim - (CONV - 1) + k
            total = total + taps[k : k + 1, span] * pad[at : at + length - rim, 0:size]
        out[rim:length, span] = jax.nn.silu(total).astype(bf16)

    for c in range(0, 2 * span_maps, tile):
        smooth(maps_ref, map_taps_ref, map_base_ref, maps_conv, c, tile)

    beside = (z > 0).astype(jnp.int32) + (z < m - 1).astype(jnp.int32)
    pl.semaphore_wait(barrier, n - 1 + beside)

    last_rows = pl.ds(length - rim, rim)

    def rim_copy(which):
        source, target = (
            (x_hbm.at[last_rows], rim_x),
            (maps_hbm.at[last_rows, at_b], rim_maps.at[:, to_b]),
            (maps_hbm.at[last_rows, at_c], rim_maps.at[:, to_c]),
        )[which]
        return pltpu.make_async_remote_copy(
            src_ref=source,
            dst_ref=target,
            send_sem=rim_send.at[which],
            recv_sem=rim_recv.at[which],
            device_id=(me + 1, z),
            device_id_type=mesh_ids,
        )

    @pl.when(has_right)
    def _():
        for which in range(3):
            rim_copy(which).start()

    def end_copy(offset, sender):
        return pltpu.make_async_remote_copy(
            src_ref=own_end,
            dst_ref=all_ends.at[sender],
            send_sem=end_send.at[offset],
            recv_sem=end_recv.at[sender],
            device_id=(lax.rem(me + offset, n), z),
            device_id_type=mesh_ids,
        )

    def send_end(offset, carry):
        end_copy(offset, me).start()
        return carry

    lax.fori_loop(1, n, send_end, 0)

    for load in loads[9:12]:
        load.wait()
    for load in loads[12:]:
        load.start()

    def smooth_rim(rows_ref, rim_ref, taps, base, out, start, size):
        span = pl.ds(start, size)
        pad[0:rim, 0:size] = rim_ref[:, span].astype(f32)
        pad[rim : 2 * rim, 0:size] = rows_ref[0:rim, span].astype(f32)
        total = base[:, span]
        for k in range(CONV):
            at = rim - (CONV - 1) + k
            total = total + taps[k : k + 1, span] * pad[at : at + rim, 0:size]
        out[0:rim, span] = jax.nn.silu(total).astype(bf16)

    def smooth_tile(c, carry):
        smooth(x_ref, taps_ref, base_ref, values, pl.multiple_of(c * tile, tile), tile)
        return carry

    lax.fori_loop(0, tiles, smooth_tile, 0)

    def chain_send_copy(level, hop, c):
        return pltpu.make_async_remote_copy(
            src_ref=leaving.at[c],
            dst_ref=arrived.at[level, c],
            send_sem=chain_send.at[hop, c],
            recv_sem=chain_recv.at[level, c],
            device_id=(me + 1 if level == 0 else me + 2 * (hop + 1), z),
            device_id_type=mesh_ids,
        )

    def chain_forward(level, c):
        return pltpu.make_async_remote_copy(
            src_ref=arrived.at[level, c],
            dst_ref=arrived.at[level, c],
            send_sem=forward_send.at[level, c],
            recv_sem=chain_recv.at[level, c],
            device_id=(partner, z),
            device_id_type=mesh_ids,
        )

    def hops(level):
        return range(max(1, 2**level // 2))

    def sends(level):
        return lax.rem(me, 2 ** (level + 1)) == 2**level - 1

    def gets(level):
        return lax.rem(lax.div(me, 2**level), 2) == 1

    per = group_width // tile

    maps_conv[0:rim] = jnp.zeros((rim, 2 * span_maps), bf16)
    values[0:rim] = jnp.zeros((rim, channels), bf16)

    for g in range(groups_here):
        turned_maps[g] = turned(
            maps_conv[:, g * STATE : (g + 1) * STATE].astype(f32)
        ).astype(bf16)

    for g in range(groups_here):
        mine = range(g * per, (g + 1) * per)
        spans = [slice(c * tile, (c + 1) * tile) for c in mine]
        weighted = [
            (values[:, span].astype(f32) * spread(ends[...], span)).astype(bf16)
            for span in spans
        ]
        for c, w in zip(mine, weighted):
            local[c] = jnp.dot(turned_maps[g], w, preferred_element_type=f32)

    @pl.when(has_left)
    def _():
        for which in range(3):
            rim_copy(which).wait_recv()

    @pl.when(jnp.logical_not(has_left))
    def _():
        rim_x[...] = jnp.zeros_like(rim_x)
        rim_maps[...] = jnp.zeros_like(rim_maps)

    for c in range(0, 2 * span_maps, tile):
        smooth_rim(maps_ref, rim_maps, map_taps_ref, map_base_ref, maps_conv, c, tile)
    for c in range(0, channels, tile):
        smooth_rim(x_ref, rim_x, taps_ref, base_ref, values, c, tile)

    for g in range(groups_here):
        mine = range(g * per, (g + 1) * per)
        spans = [slice(c * tile, (c + 1) * tile) for c in mine]
        first_maps = maps_conv[0:rim, g * STATE : (g + 1) * STATE]
        weighted = [
            (values[0:rim, span].astype(f32) * spread(ends[0:rim], span)).astype(bf16)
            for span in spans
        ]
        for c, w in zip(mine, weighted):
            total = local[c] + lax.dot_general(
                first_maps, w, (((0,), (0,)), ((), ())), preferred_element_type=f32
            )
            local[c] = total
            state[c] = jnp.zeros_like(total)
            leaving[c] = total.astype(bf16)

        @pl.when(sends(0))
        def _():
            for c in mine:
                chain_send_copy(0, 0, c).start()

    def link(level, c):
        span = pl.ds(pl.multiple_of(c * tile, tile), tile)

        @pl.when(gets(level))
        def _():
            chain_forward(level, c).wait_recv()
            if level == 0:
                state[c] = arrived[level, c].astype(f32)
            else:
                @pl.when(odd)
                def _():
                    chain_forward(level, c).start()

                state[c] = state[c] + prefix_rows[level, 0:1, span] * arrived[level, c].astype(f32)

        if level + 1 < levels:
            @pl.when(sends(level + 1))
            def _():
                leaving[c] = (channel_rows[0:1, span] * state[c] + local[c]).astype(bf16)
                for hop in hops(level + 1):
                    chain_send_copy(level + 1, hop, c).start()

    def link_all(level, first, last):
        def body(c, carry):
            link(level, c)
            return carry

        lax.fori_loop(first, last, body, 0)

    link_all(0, 0, tiles)

    for g in range(groups_here):
        scores[g] = lax.dot_general(
            maps_conv[:, span_maps + g * STATE : span_maps + (g + 1) * STATE],
            maps_conv[:, g * STATE : (g + 1) * STATE],
            (((1,), (1,)), ((), ())),
            preferred_element_type=f32,
        )

    def get_end(offset, carry):
        end_copy(offset, lax.rem(me + offset, n)).wait_recv()
        return carry

    lax.fori_loop(1, n, get_end, 0)

    for level in range(1, levels):
        base = me - lax.rem(me, 2**level)
        total = jnp.zeros((8, lanes), f32)
        for i in range(n):
            total = total + jnp.where((base <= i) & (i < me), all_ends[i], 0.0)
        passed = jnp.exp(total[:, 0:heads])
        passed = jnp.concatenate([passed, passed], axis=0)
        passed = jnp.concatenate([*three(passed), jnp.zeros((16, heads), bf16)], axis=1)

        prefix_rows[level] = spread(passed, slice(None))

    pair = 2 * HEAD_DIM
    lane = lax.broadcasted_iota(jnp.int32, (half, pair), 1)
    batch = 4

    def mask_of(head):
        slot = lax.broadcasted_iota(jnp.int32, (1, 8 * heads), 1)
        return ((lax.rem(slot, heads) == head) & (slot < 6 * heads)).astype(f32).astype(bf16)

    def within(turn, carry):
        g = lax.div(turn * batch * pair, group_width)
        gaps = []
        for e in range(2 * batch):
            left = gap_left[...] * mask_of(2 * batch * turn + e)
            gaps.append((
                jnp.dot(left[0:half], gap_right[:, 0:half], preferred_element_type=f32),
                jnp.dot(left[half:length], gap_right[...], preferred_element_type=f32),
            ))
        causal = lax.broadcasted_iota(jnp.int32, (half, half), 0) >= lax.broadcasted_iota(
            jnp.int32, (half, half), 1
        )
        causal_late = lax.broadcasted_iota(jnp.int32, (half, length), 0) + half >= (
            lax.broadcasted_iota(jnp.int32, (half, length), 1)
        )
        mixing = [
            (
                (jnp.where(causal, jnp.exp2(a), 0.0) * scores[g, 0:half, 0:half]).astype(bf16),
                (jnp.where(causal_late, jnp.exp2(b), 0.0) * scores[g, half:length]).astype(bf16),
            )
            for a, b in gaps
        ]
        for q in range(batch):
            span = pl.ds(pl.multiple_of((turn * batch + q) * pair, pair), pair)
            early, late = [], []
            for a, b in mixing[2 * q : 2 * q + 2]:
                early.append(jnp.dot(a, values[0:half, span], preferred_element_type=f32))
                late.append(jnp.dot(b, values[:, span], preferred_element_type=f32))
            y[0:half, span] = jnp.where(lane < HEAD_DIM, early[0], early[1])
            y[half:length, span] = jnp.where(lane < HEAD_DIM, late[0], late[1])
        return carry

    batches = channels // (pair * batch)
    share = tiles // batches

    def within_level(turn, carry):
        for c in range(share):
            if levels > 2:
                link(1, turn * share + c)
        return within(turn, carry)

    lax.fori_loop(0, batches, within_level, 0)

    for level in range(2, levels - 1):
        link_all(level, 0, tiles)

    for load in loads[12:14]:
        load.wait()

    def partner_copy(slot, g):
        return pltpu.make_async_remote_copy(
            src_ref=gat.at[slot - 1, g],
            dst_ref=gat.at[slot, g],
            send_sem=gat_send.at[slot, g],
            recv_sem=gat_recv.at[slot, g],
            device_id=(partner, z),
            device_id_type=mesh_ids,
        )

    def source_mask(i, who):
        swap = (who == 1) & (chips >= 4)
        return i + jnp.where(swap & (i == 1), 1, 0) - jnp.where(swap & (i == 2), 1, 0)

    def chip_at(mask):
        there, bit = chip, 1
        while bit < chips:
            on = lax.rem(lax.div(mask, bit), 2)
            there = there + on * (bit - 2 * bit * lax.rem(lax.div(chip, bit), 2))
            bit *= 2
        return there

    def across_copy(i, g):
        return pltpu.make_async_remote_copy(
            src_ref=gat.at[0, g],
            dst_ref=gat.at[2 * i, g],
            send_sem=gat_send.at[2 * i, g],
            recv_sem=gat_recv.at[2 * i, g],
            device_id=(2 * chip_at(source_mask(i, core)) + core, z),
            device_id_type=mesh_ids,
        )

    relayed = chips == 4

    def relay_copy(slot, g):
        mask = source_mask(lax.div(slot, 2), core)
        return pltpu.make_async_remote_copy(
            src_ref=gat.at[slot, g],
            dst_ref=gat.at[6, g],
            send_sem=gat_send.at[6, g],
            recv_sem=gat_recv.at[6, g],
            device_id=(2 * chip_at(3 - mask) + core, z),
            device_id_type=mesh_ids,
        )

    def arrival(slot, g):
        return pltpu.make_async_remote_copy(
            src_ref=gat.at[slot, g],
            dst_ref=gat.at[slot, g],
            send_sem=gat_send.at[slot, g],
            recv_sem=gat_recv.at[slot, g],
            device_id=(partner, z),
            device_id_type=mesh_ids,
        )

    for g in range(groups_here):
        mine = range(g * per, (g + 1) * per)
        spans = [slice(c * tile, (c + 1) * tile) for c in mine]
        output_map = maps_conv[:, span_maps + g * STATE : span_maps + (g + 1) * STATE]
        squares = jnp.zeros((length, 128), f32)
        for first in range(0, per, 2):
            link_all(levels - 1, g * per + first, g * per + first + 2)
            carried = [
                jnp.dot(output_map, state[c].astype(bf16), preferred_element_type=f32)
                for c in mine[first : first + 2]
            ]
            grown = [spread(growth[...], span) for span in spans[first : first + 2]]
            for span, more, scale in zip(spans[first : first + 2], carried, grown):
                total = y[:, span] + more * scale
                total = total + channel_rows[8:9, span] * values[:, span].astype(f32)
                total = total * jax.nn.silu(gate_ref[:, span].astype(f32))
                y[:, span] = total
                for d in range(0, tile, 128):
                    squares = squares + total[:, d : d + 128] * total[:, d : d + 128]
        scale = lax.rsqrt(jnp.sum(squares, axis=1, keepdims=True) / group_width + 1e-05)
        for c, span in enumerate(spans):
            gat[0, g, :, c * tile : (c + 1) * tile] = (
                y[:, span] * scale * gain_ref[:, span]
            ).astype(bf16)
        partner_copy(1, g).start()
        if chips > 1:
            across_copy(1, g).start()

    def chain_z(step, j, buffer, send, recv, to):
        return pltpu.make_async_remote_copy(
            src_ref=part.at[step, pl.ds(j * rows, rows)],
            dst_ref=buffer.at[step, pl.ds(j * rows, rows)],
            send_sem=send.at[step, j],
            recv_sem=recv.at[step, j],
            device_id=(me, to),
            device_id_type=mesh_ids,
        )

    def slot_of(step):
        return jnp.where(step == n - 1, n - 3, jnp.where(step >= n - 3, step + 1, step))

    def owner(step):
        slot = slot_of(step)
        who = core + lax.rem(slot, 2) * (1 - 2 * core)
        return 2 * chip_at(source_mask(lax.div(slot, 2), who)) + who

    def columns(sender):
        return pl.ds(pl.multiple_of(sender * width, width), width)

    def own_rows():
        return pl.ds(pl.multiple_of(z * rows, rows), rows)

    def out_copy(step, sender):
        return pltpu.make_async_remote_copy(
            src_ref=part.at[step, own_rows()],
            dst_ref=out_ref.at[:, columns(sender)],
            send_sem=out_send.at[step],
            recv_sem=out_recv.at[sender],
            device_id=(owner(step), z),
            device_id_type=mesh_ids,
        )

    pieces = 2 if rows % 32 == 0 else 1
    size = rows // pieces

    def piece_z(j, h, buffer, send, recv, to):
        span = pl.ds(j * rows + h * size, size)
        return pltpu.make_async_remote_copy(
            src_ref=part.at[n - 1, span],
            dst_ref=buffer.at[n - 1, span],
            send_sem=send.at[n - 1 + h, j],
            recv_sem=recv.at[n - 1 + h, j],
            device_id=(me, to),
            device_id_type=mesh_ids,
        )

    def piece_out(h, sender):
        mine = pl.ds(pl.multiple_of(z * rows + h * size, size), size)
        return pltpu.make_async_remote_copy(
            src_ref=part.at[n - 1, mine],
            dst_ref=out_ref.at[pl.ds(h * size, size), columns(sender)],
            send_sem=out_send.at[n - 1 + h],
            recv_sem=out_recv.at[sender if h == 0 else n],
            device_id=(owner(n - 1), z),
            device_id_type=mesh_ids,
        )

    def own_copy():
        return pltpu.make_async_copy(part.at[0, own_rows()], out_ref.at[:, columns(me)], own_sem)

    def added(step, j, buffer):
        span = pl.ds(j * rows, rows)
        part[step, span] = (
            part[step, span].astype(f32) + buffer[step, span].astype(f32)
        ).astype(bf16)

    up_lag, down_lag = z, m - 1 - z
    held = min(2, n - 1)
    kept = (1, 0) if n - 1 - held >= 2 else ()
    last_lag = m - 1 + max(held - 2, 0) + len(kept)
    wide = min(width, 256)

    loads[14].wait()

    def last_step(place):
        if not kept:
            return place
        skipped = place
        for early in sorted(kept):
            skipped = skipped + (skipped >= early).astype(jnp.int32)
        for i, early in enumerate(kept):
            skipped = jnp.where(place == n - len(kept) + i, early, skipped)
        return jnp.where((place < 0) | (place >= n), -1, skipped)

    def turn(tau, carry):
        @pl.when(tau < n)
        def _():
            slot = slot_of(tau)
            direct = (slot > 0) & (lax.rem(slot, 2) == 0)

            @pl.when(direct)
            def _():
                for g in range(groups_here):
                    arrival(slot, g).wait_send()

            @pl.when(direct & (slot < (4 if relayed else n - 2)))
            def _():
                for g in range(groups_here):
                    across_copy(lax.div(slot, 2) + 1, g).start()

            @pl.when(tau > 0)
            def _():
                for g in range(groups_here):
                    arrival(slot, g).wait_recv()

            @pl.when(direct)
            def _():
                for g in range(groups_here):
                    partner_copy(slot + 1, g).start()

            if relayed:
                @pl.when((slot == 3) | (slot == 4))
                def _():
                    source = jnp.where(slot == 3, 2, 4)
                    along = source_mask(lax.div(source, 2), core) == 1
                    for g in range(groups_here):
                        @pl.when(along == (g < (groups_here + 1) // 2))
                        def _():
                            relay_copy(source, g).start()

            for c in range(0, width, wide):
                total = jnp.zeros((length, wide), f32)
                for g in range(groups_here):
                    total = total + jnp.dot(
                        gat[slot, g],
                        w_ref[g * group_width : (g + 1) * group_width, c : c + wide],
                        preferred_element_type=f32,
                    )
                part[tau, :, c : c + wide] = total.astype(bf16)

        t_up = tau - up_lag

        @pl.when((t_up >= 0) & (t_up < n))
        def _():
            for j in range(m - 1, 0, -1):
                @pl.when(z < j)
                def _():
                    copy = chain_z(t_up, j, up, up_send, up_recv, z + 1)

                    @pl.when(z > 0)
                    def _():
                        copy.wait_recv()
                        added(t_up, j, up)

                    if j == 1:
                        @pl.when(t_up == n - 1)
                        def _():
                            for before in range(held, 0, -1):
                                chain_z(n - 1 - before, j, up, up_send, up_recv, z + 1).start()
                            for h in range(pieces):
                                piece_z(j, h, up, up_send, up_recv, z + 1).start()
                            for early in kept:
                                chain_z(early, j, up, up_send, up_recv, z + 1).start()

                        now = t_up < n - 1 - held
                        for early in kept:
                            now = now & (t_up != early)

                        @pl.when(now)
                        def _():
                            copy.start()
                    else:
                        copy.start()

        t_down = tau - down_lag

        @pl.when((t_down >= 0) & (t_down < n))
        def _():
            for j in range(m - 1):
                @pl.when(z > j)
                def _():
                    copy = chain_z(t_down, j, down, down_send, down_recv, z - 1)

                    @pl.when(z < m - 1)
                    def _():
                        copy.wait_recv()
                        added(t_down, j, down)

                    if j == m - 2:
                        @pl.when(t_down == n - 1)
                        def _():
                            for before in range(held, 0, -1):
                                chain_z(n - 1 - before, j, down, down_send, down_recv, z - 1).start()
                            for h in range(pieces):
                                piece_z(j, h, down, down_send, down_recv, z - 1).start()
                            for early in kept:
                                chain_z(early, j, down, down_send, down_recv, z - 1).start()

                        now = t_down < n - 1 - held
                        for early in kept:
                            now = now & (t_down != early)

                        @pl.when(now)
                        def _():
                            copy.start()
                    else:
                        copy.start()

        t_last = last_step(tau - last_lag)

        @pl.when((t_last >= 0) & (t_last < n - 1))
        def _():
            for j in range(m):
                @pl.when(z == j)
                def _():
                    span = pl.ds(j * rows, rows)
                    total = part[t_last, span].astype(f32)
                    if j > 0:
                        chain_z(t_last, j, up, up_send, up_recv, z).wait_recv()
                        total = total + up[t_last, span].astype(f32)
                    if j < m - 1:
                        chain_z(t_last, j, down, down_send, down_recv, z).wait_recv()
                        total = total + down[t_last, span].astype(f32)
                    part[t_last, span] = total.astype(bf16)

            @pl.when(t_last == 0)
            def _():
                own_copy().start()

            @pl.when(t_last > 0)
            def _():
                out_copy(t_last, me).start()

        @pl.when(t_last == n - 1)
        def _():
            for j in range(m):
                @pl.when(z == j)
                def _():
                    for h in range(pieces):
                        span = pl.ds(j * rows + h * size, size)
                        total = part[n - 1, span].astype(f32)
                        if j > 0:
                            if j == 1:
                                piece_z(j, h, up, up_send, up_recv, z).wait_recv()
                            elif h == 0:
                                chain_z(n - 1, j, up, up_send, up_recv, z).wait_recv()
                            total = total + up[n - 1, span].astype(f32)
                        if j < m - 1:
                            if j == m - 2:
                                piece_z(j, h, down, down_send, down_recv, z).wait_recv()
                            elif h == 0:
                                chain_z(n - 1, j, down, down_send, down_recv, z).wait_recv()
                            total = total + down[n - 1, span].astype(f32)
                        part[n - 1, span] = total.astype(bf16)
                        piece_out(h, me).start()

        return carry

    lax.fori_loop(0, n + last_lag, turn, 0)

    def finish(step, carry):
        @pl.when(lax.rem(step, 2) == 1)
        def _():
            for g in range(groups_here):
                arrival(step, g).wait_send()

        @pl.when(step > 0)
        def _():
            end_copy(step, me).wait_send()

        for j in range(m):
            @pl.when((z < j) & ((step < n - 1) | (j != 1)))
            def _():
                chain_z(step, j, up, up_send, up_recv, z).wait_send()

            @pl.when((z > j) & ((step < n - 1) | (j != m - 2)))
            def _():
                chain_z(step, j, down, down_send, down_recv, z).wait_send()

        @pl.when((step > 0) & (step < n - 1))
        def _():
            out_copy(step, me).wait_send()

        sender = lax.rem(me + step, n)

        @pl.when((step > 0) & (sender != ending))
        def _():
            out_copy(step, sender).wait_recv()

        return carry

    ending_slot = slot_of(n - 1)
    ending = 2 * chip_at(source_mask(lax.div(ending_slot, 2), core)) + core
    ending = ending + lax.rem(ending_slot, 2) * (1 - 2 * core)
    lax.fori_loop(0, n, finish, 0)
    for h in range(pieces):
        @pl.when(z == 0)
        def _():
            piece_z(1, h, up, up_send, up_recv, z).wait_send()

        @pl.when(z == m - 1)
        def _():
            piece_z(m - 2, h, down, down_send, down_recv, z).wait_send()

        piece_out(h, me).wait_send()
        piece_out(h, ending).wait_recv()
    own_copy().wait()

    @pl.when(has_right)
    def _():
        for which in range(3):
            rim_copy(which).wait_send()

    def sent(c, carry):
        for level in range(levels):
            @pl.when(sends(level))
            def _():
                for hop in hops(level):
                    chain_send_copy(level, hop, c).wait_send()

            if level > 0:
                @pl.when(gets(level) & odd)
                def _():
                    chain_forward(level, c).wait_send()

        return carry

    lax.fori_loop(0, tiles, sent, 0)


def layer(x, gate, maps, step_raw, rate, skip, taps, base, map_taps, map_base, gain, weight):
    n, m = lax.axis_size("seq"), lax.axis_size("tp")
    length, channels = x.shape
    heads = rate.shape[0]
    per_group = HEADS // GROUPS
    groups_here = heads // per_group
    tile = max(128, channels // 8)
    tiles = channels // tile
    width = weight.shape[1]
    span_maps = 2 * groups_here * STATE
    rim = 16
    levels = n.bit_length() - 1
    lanes = -(-heads // 128) * 128
    bf16, f32 = jnp.bfloat16, jnp.float32
    dma = pltpu.SemaphoreType.DMA
    operands = (
        x, gate, maps, step_raw.T, rate[None], skip[None], taps, base[None],
        map_taps, map_base[None], gain[None], weight,
    )
    blocks = pltpu.VMEM((n, length, width), bf16)
    return pl.pallas_call(
        functools.partial(layer_kernel, n, m, per_group),
        out_shape=jax.ShapeDtypeStruct((length // m, n * width), bf16),
        in_specs=[pl.BlockSpec(memory_space=pl.ANY)] * len(operands),
        out_specs=pl.BlockSpec(memory_space=pl.ANY),
        scratch_shapes=[
            pltpu.VMEM((length, channels), bf16),
            pltpu.VMEM((length, channels), bf16),
            pltpu.VMEM((length, span_maps), bf16),
            pltpu.VMEM((heads, length), f32),
            pltpu.VMEM((1, heads), f32),
            pltpu.VMEM((1, heads), f32),
            pltpu.VMEM((CONV, channels), f32),
            pltpu.VMEM((1, channels), f32),
            pltpu.VMEM((CONV, span_maps), f32),
            pltpu.VMEM((1, span_maps), f32),
            pltpu.VMEM((1, channels), f32),
            pltpu.VMEM(weight.shape, bf16),
            dma((15,)),
            pltpu.VMEM((rim, channels), bf16),
            pltpu.VMEM((rim, span_maps), bf16),
            pltpu.VMEM((length, max(tile, STATE)), f32),
            pltpu.VMEM((length, channels), bf16),
            pltpu.VMEM((length, span_maps), bf16),
            pltpu.VMEM((length, channels), f32),
            pltpu.VMEM((groups_here, length, length), f32),
            pltpu.VMEM((tiles, STATE, tile), f32),
            pltpu.VMEM((tiles, STATE, tile), f32),
            pltpu.VMEM((levels, tiles, STATE, tile), bf16),
            pltpu.VMEM((tiles, STATE, tile), bf16),
            pltpu.VMEM((length, 8 * heads), bf16),
            pltpu.VMEM((8 * heads, length), bf16),
            pltpu.VMEM((groups_here, STATE, length), bf16),
            pltpu.VMEM((length, 4 * heads), bf16),
            pltpu.VMEM((length, 4 * heads), bf16),
            pltpu.VMEM((8, lanes), f32),
            pltpu.VMEM((n, 8, lanes), f32),
            pltpu.VMEM((4 * heads, channels), bf16),
            pltpu.VMEM((16, channels), f32),
            pltpu.VMEM((levels, 16, channels), f32),
            pltpu.VMEM((n, groups_here, length, channels // groups_here), bf16),
            blocks,
            blocks,
            blocks,
            dma((3,)),
            dma((3,)),
            dma((n,)),
            dma((n,)),
            dma((max(1, n // 4), tiles)),
            dma((levels, tiles)),
            dma((levels, tiles)),
            dma((n, groups_here)),
            dma((n, groups_here)),
            dma((n + 1, m)),
            dma((n + 1, m)),
            dma((n + 1, m)),
            dma((n + 1, m)),
            dma((n + 1,)),
            dma((n + 1,)),
            dma(()),
        ],
        compiler_params=pltpu.CompilerParams(
            collective_id=2, has_side_effects=True, vmem_limit_bytes=60 << 20
        ),
        cost_estimate=pl.CostEstimate(
            flops=2 * n * length * channels * width,
            bytes_accessed=2 * (channels * width + 3 * length * channels),
            transcendentals=0,
        ),
    )(*operands)


def shards(
    conv_values,
    gate_values,
    conv_maps,
    step_raw,
    decay_log,
    skip_gain,
    values_kernel,
    values_offset,
    maps_kernel,
    maps_offset,
    norm_weight,
    out_weight,
    residual,
):
    length = conv_values.shape[0]
    heads_dev = decay_log.shape[0]
    per_group = HEADS // GROUPS
    whole_groups = heads_dev % per_group == 0
    chips = lax.axis_size("seq") // 2
    paired = lax.axis_size("seq") == 2 * chips and chips & (chips - 1) == 0
    if whole_groups and paired and heads_dev % 32 == 0:
        summed = layer(
            conv_values, gate_values, conv_maps, step_raw, decay_log, skip_gain, values_kernel,
            values_offset, maps_kernel, maps_offset, norm_weight, out_weight,
        )
        return residual.astype(jnp.float32) + summed.astype(jnp.float32)
    step_size = jax.nn.softplus(step_raw)
    place = jnp.arange(length, dtype=jnp.int32)
    cum_log = jnp.dot(
        (place[:, None] >= place[None, :]).astype(jnp.float32),
        -jnp.exp(decay_log)[None, :] * step_size,
        precision=lax.Precision.HIGHEST,
    )
    normed = front(
        conv_values, gate_values, conv_maps, cum_log, step_size, skip_gain, values_kernel,
        values_offset, maps_kernel, maps_offset, norm_weight, whole_groups,
    )
    if not whole_groups:
        gated_out = normed.reshape(length, heads_dev, HEAD_DIM)
        head_squares = jnp.sum(gated_out * gated_out, axis=2)
        all_heads = lax.all_gather(head_squares, "tp", axis=1, tiled=True)
        group_totals = jnp.sum(all_heads.reshape(length, GROUPS, per_group), axis=2)
        heads_here = lax.axis_index("tp") * heads_dev + jnp.arange(heads_dev, dtype=jnp.int32)
        inv_rms = lax.rsqrt(
            group_totals[:, heads_here // per_group] / (per_group * HEAD_DIM) + 1e-05
        )
        normed = (
            (gated_out * inv_rms[:, :, None]).reshape(length, heads_dev * HEAD_DIM)
            * norm_weight[None, :]
        ).astype(jnp.bfloat16)
    blocks = mix(normed, out_weight)
    summed = jnp.transpose(blocks, (1, 0, 2)).reshape(residual.shape).astype(jnp.float32)
    return residual.astype(jnp.float32) + summed


def solution(mesh):
    placed = (
        P("seq", "tp"),
        P("seq", "tp"),
        P("seq", None),
        P("seq", "tp"),
        P("tp"),
        P("tp"),
        P(None, "tp"),
        P("tp"),
        P(),
        P(),
        P("tp"),
        P("tp", "seq"),
        P(("seq", "tp"), None),
    )
    return jax.shard_map(
        shards, mesh=mesh, in_specs=placed, out_specs=P(("seq", "tp"), None), check_vma=False
    )
```

```python
import functools

import jax
import jax.numpy as jnp
from jax import lax
from jax.experimental import pallas as pl
from jax.experimental.pallas import tpu as pltpu
from jax.sharding import PartitionSpec as P

HEADS = 128
HEAD_DIM = 64
STATE = 128
GROUPS = 8
CONV = 4


def ring_place(spot, size):
    if size % 4:
        return spot
    half = size // 2
    past = spot - half
    turned = half + (half - 2 - 2 * lax.div(past, 2)) + lax.rem(past, 2)
    return jnp.where(spot < half, spot, turned)


def mix_kernel(
    n, m, x_ref, w_ref, out_ref, gat, part, up, down,
    own_sem, gat_send, gat_recv, up_send, up_recv, down_send, down_recv, out_send, out_recv,
):
    mesh_ids = pl.DeviceIdType.MESH
    me, z = lax.axis_index("seq"), lax.axis_index("tp")
    spot = ring_place(me, n)
    right = ring_place(lax.rem(spot + 1, n), n)
    left = ring_place(lax.rem(spot + n - 1, n), n)
    half = gat.shape[2]
    depth = gat.shape[3]
    width = w_ref.shape[1]
    rows = part.shape[1] // m
    tile = min(width, 256)

    own = [
        pltpu.make_async_copy(x_ref.at[pl.ds(d * half, half)], gat.at[0, d], own_sem.at[d])
        for d in range(2)
    ]
    for copy in own:
        copy.start()

    barrier = pltpu.get_barrier_semaphore()

    def greet(step, carry):
        pl.semaphore_signal(
            barrier, inc=1, device_id=(lax.rem(me + step, n), z), device_id_type=mesh_ids
        )
        return carry

    lax.fori_loop(1, n, greet, 0)

    @pl.when(z > 0)
    def _():
        pl.semaphore_signal(barrier, inc=1, device_id=(me, z - 1), device_id_type=mesh_ids)

    @pl.when(z < m - 1)
    def _():
        pl.semaphore_signal(barrier, inc=1, device_id=(me, z + 1), device_id_type=mesh_ids)

    beside = (z > 0).astype(jnp.int32) + (z < m - 1).astype(jnp.int32)
    pl.semaphore_wait(barrier, n - 1 + beside)

    for copy in own:
        copy.wait()

    def gather_copy(step, d):
        return pltpu.make_async_remote_copy(
            src_ref=gat.at[step, d],
            dst_ref=gat.at[step + 1, d],
            send_sem=gat_send.at[step, d],
            recv_sem=gat_recv.at[step + 1, d],
            device_id=(right if d == 0 else left, z),
            device_id_type=mesh_ids,
        )

    def gather_arrival(step, d):
        return pltpu.make_async_remote_copy(
            src_ref=gat.at[step, d],
            dst_ref=gat.at[step, d],
            send_sem=gat_send.at[step, d],
            recv_sem=gat_recv.at[step, d],
            device_id=(right if d == 0 else left, z),
            device_id_type=mesh_ids,
        )

    def chain_copy(step, j, buffer, send, recv, to):
        return pltpu.make_async_remote_copy(
            src_ref=part.at[step, pl.ds(j * rows, rows)],
            dst_ref=buffer.at[step, pl.ds(j * rows, rows)],
            send_sem=send.at[step, j],
            recv_sem=recv.at[step, j],
            device_id=(me, to),
            device_id_type=mesh_ids,
        )

    def owner(step):
        there = jnp.where(z < m // 2, spot - step + n, spot + step)
        return ring_place(lax.rem(there, n), n)

    def out_copy(step, sender):
        return pltpu.make_async_remote_copy(
            src_ref=part.at[step, pl.ds(pl.multiple_of(z * rows, rows), rows)],
            dst_ref=out_ref.at[sender],
            send_sem=out_send.at[step],
            recv_sem=out_recv.at[sender],
            device_id=(owner(step), z),
            device_id_type=mesh_ids,
        )

    def added(step, j, buffer):
        span = pl.ds(j * rows, rows)
        part[step, span] = (
            part[step, span].astype(jnp.float32) + buffer[step, span].astype(jnp.float32)
        ).astype(jnp.bfloat16)

    up_lag, down_lag = z, m - 1 - z
    last_lag = jnp.maximum(up_lag, down_lag)

    def turn(tau, carry):
        @pl.when(tau < n)
        def _():
            @pl.when(tau > 0)
            def _():
                for d in range(2):
                    gather_arrival(tau, d).wait_recv()

            @pl.when(tau < n - 1)
            def _():
                for d in range(2):
                    gather_copy(tau, d).start()

            block = gat[tau].reshape(2 * half, depth)
            for c in range(0, width, tile):
                part[tau, :, c : c + tile] = jnp.dot(
                    block, w_ref[:, c : c + tile], preferred_element_type=jnp.float32
                ).astype(jnp.bfloat16)

        t_up = tau - up_lag

        @pl.when((t_up >= 0) & (t_up < n))
        def _():
            for j in range(m - 1, 0, -1):
                @pl.when(z < j)
                def _():
                    copy = chain_copy(t_up, j, up, up_send, up_recv, z + 1)

                    @pl.when(z > 0)
                    def _():
                        copy.wait_recv()
                        added(t_up, j, up)

                    copy.start()

        t_down = tau - down_lag

        @pl.when((t_down >= 0) & (t_down < n))
        def _():
            for j in range(m - 1):
                @pl.when(z > j)
                def _():
                    copy = chain_copy(t_down, j, down, down_send, down_recv, z - 1)

                    @pl.when(z < m - 1)
                    def _():
                        copy.wait_recv()
                        added(t_down, j, down)

                    copy.start()

        t_last = tau - last_lag

        @pl.when((t_last >= 0) & (t_last < n))
        def _():
            for j in range(m):
                @pl.when(z == j)
                def _():
                    span = pl.ds(j * rows, rows)
                    total = part[t_last, span].astype(jnp.float32)
                    if j > 0:
                        chain_copy(t_last, j, up, up_send, up_recv, z).wait_recv()
                        total = total + up[t_last, span].astype(jnp.float32)
                    if j < m - 1:
                        chain_copy(t_last, j, down, down_send, down_recv, z).wait_recv()
                        total = total + down[t_last, span].astype(jnp.float32)
                    part[t_last, span] = total.astype(jnp.bfloat16)

            @pl.when(t_last == 0)
            def _():
                out_ref[me] = part[0, pl.ds(pl.multiple_of(z * rows, rows), rows)]

            @pl.when(t_last > 0)
            def _():
                out_copy(t_last, me).start()

        return carry

    lax.fori_loop(0, n + m - 1, turn, 0)

    def finish(step, carry):
        @pl.when(step < n - 1)
        def _():
            for d in range(2):
                gather_copy(step, d).wait_send()

        for j in range(m):
            @pl.when(z < j)
            def _():
                chain_copy(step, j, up, up_send, up_recv, z).wait_send()

            @pl.when(z > j)
            def _():
                chain_copy(step, j, down, down_send, down_recv, z).wait_send()

        @pl.when(step > 0)
        def _():
            out_copy(step, me).wait_send()
            out_copy(step, lax.rem(me + step, n)).wait_recv()

        return carry

    lax.fori_loop(0, n, finish, 0)


def mix(normed, weight):
    n, m = lax.axis_size("seq"), lax.axis_size("tp")
    length, depth = normed.shape
    width = weight.shape[1]
    rows = length // m
    half = length // 2
    slots = pltpu.VMEM((n, length, width), jnp.bfloat16)
    dma = pltpu.SemaphoreType.DMA
    vmem = pl.BlockSpec(memory_space=pltpu.VMEM)
    return pl.pallas_call(
        functools.partial(mix_kernel, n, m),
        out_shape=jax.ShapeDtypeStruct((n, rows, width), jnp.bfloat16),
        in_specs=[pl.BlockSpec(memory_space=pl.ANY), vmem],
        out_specs=vmem,
        scratch_shapes=[
            pltpu.VMEM((n, 2, half, depth), jnp.bfloat16),
            slots,
            slots,
            slots,
            dma((2,)),
            dma((n, 2)),
            dma((n, 2)),
            dma((n, m)),
            dma((n, m)),
            dma((n, m)),
            dma((n, m)),
            dma((n,)),
            dma((n,)),
        ],
        compiler_params=pltpu.CompilerParams(
            collective_id=0, has_side_effects=True, vmem_limit_bytes=48 << 20
        ),
        cost_estimate=pl.CostEstimate(
            flops=2 * n * length * depth * width,
            bytes_accessed=2 * (depth * width + length * depth),
            transcendentals=0,
        ),
    )(normed, weight)


def front_kernel(
    n, per_group, whole_groups, x_ref, gate_ref, maps_ref, cum_ref, cum_t_ref, step_ref, step_t_ref,
    decay_ref, skip_ref, taps_ref, base_ref, map_taps_ref, map_base_ref, gain_ref, out_ref,
    rim_x, rim_maps, pad, values, y, b_maps, c_maps, scores, local, arrived, leaving,
    rim_send, rim_recv, chain_send, chain_recv,
):
    mesh_ids = pl.DeviceIdType.MESH
    exact = lax.Precision.HIGHEST
    me, z = lax.axis_index("seq"), lax.axis_index("tp")
    length, channels = x_ref.shape
    heads = cum_ref.shape[1]
    groups_here = scores.shape[0]
    first_group = lax.div(z * heads, per_group)
    tile = arrived.shape[2]
    tiles = channels // tile
    group_width = channels // groups_here
    rim = rim_x.shape[0]

    barrier = pltpu.get_barrier_semaphore()
    has_left, has_right = me > 0, me < n - 1

    @pl.when(has_left)
    def _():
        pl.semaphore_signal(barrier, inc=1, device_id=(me - 1, z), device_id_type=mesh_ids)

    @pl.when(has_right)
    def _():
        pl.semaphore_signal(barrier, inc=1, device_id=(me + 1, z), device_id_type=mesh_ids)

    pl.semaphore_wait(barrier, has_left.astype(jnp.int32) + has_right.astype(jnp.int32))

    def rim_copy(which):
        source, target = ((x_ref, rim_x), (maps_ref, rim_maps))[which]
        return pltpu.make_async_remote_copy(
            src_ref=source.at[pl.ds(length - rim, rim)],
            dst_ref=target,
            send_sem=rim_send.at[which],
            recv_sem=rim_recv.at[which],
            device_id=(me + 1, z),
            device_id_type=mesh_ids,
        )

    @pl.when(has_right)
    def _():
        for which in range(2):
            rim_copy(which).start()

    @pl.when(has_left)
    def _():
        for which in range(2):
            rim_copy(which).wait_recv()

    @pl.when(jnp.logical_not(has_left))
    def _():
        rim_x[...] = jnp.zeros_like(rim_x)
        rim_maps[...] = jnp.zeros_like(rim_maps)

    def conv(rows_ref, rim_ref, taps, base, start, size):
        span = pl.ds(start, size)
        pad[0:rim, 0:size] = rim_ref[:, span].astype(jnp.float32)
        pad[rim : rim + length, 0:size] = rows_ref[:, span].astype(jnp.float32)
        total = base[:, span]
        for k in range(CONV):
            at = rim - (CONV - 1) + k
            total = total + taps[k : k + 1, span] * pad[at : at + length, 0:size]
        return jax.nn.silu(total).astype(jnp.bfloat16)

    for g in range(groups_here):
        at = pl.multiple_of((first_group + g) * STATE, STATE)
        b_maps[g] = conv(maps_ref, rim_maps, map_taps_ref, map_base_ref, at, STATE)
        at = pl.multiple_of((GROUPS + first_group + g) * STATE, STATE)
        c_maps[g] = conv(maps_ref, rim_maps, map_taps_ref, map_base_ref, at, STATE)
        scores[g] = lax.dot_general(
            c_maps[g], b_maps[g], (((1,), (1,)), ((), ())), preferred_element_type=jnp.float32
        )

    def spread(per_head, start):
        head = lax.broadcasted_iota(jnp.int32, (heads, tile), 0) * HEAD_DIM
        lane = lax.broadcasted_iota(jnp.int32, (heads, tile), 1) + start
        chosen = ((lane >= head) & (lane < head + HEAD_DIM)).astype(jnp.float32)
        return jnp.dot(
            per_head, chosen, precision=exact, preferred_element_type=jnp.float32
        )

    cum = cum_ref[...]
    end_weight = jnp.exp(cum[length - 1 : length] - cum) * step_ref[...]
    grown = jnp.exp(cum)

    def states(c, carry):
        start = pl.multiple_of(c * tile, tile)
        span = pl.ds(start, tile)
        value = conv(x_ref, rim_x, taps_ref, base_ref, start, tile)
        values[:, span] = value
        weighted = (value.astype(jnp.float32) * spread(end_weight, start)).astype(jnp.bfloat16)
        g = lax.div(start, group_width)
        local[c] = lax.dot_general(
            b_maps[g], weighted, (((0,), (0,)), ((), ())), preferred_element_type=jnp.float32
        )
        return carry

    lax.fori_loop(0, tiles, states, 0)

    def chain_copy(c):
        return pltpu.make_async_remote_copy(
            src_ref=leaving.at[c],
            dst_ref=arrived.at[c],
            send_sem=chain_send.at[c],
            recv_sem=chain_recv.at[c],
            device_id=(me + 1, z),
            device_id_type=mesh_ids,
        )

    def link(c, carry):
        span = pl.ds(pl.multiple_of(c * tile, tile), tile)

        @pl.when(has_left)
        def _():
            chain_copy(c).wait_recv()

        @pl.when(jnp.logical_not(has_left))
        def _():
            arrived[c] = jnp.zeros_like(arrived[c])

        @pl.when(has_right)
        def _():
            leaving[c] = (
                decay_ref[:, span] * arrived[c].astype(jnp.float32) + local[c]
            ).astype(jnp.bfloat16)
            chain_copy(c).start()

        return carry

    pair = 2 * HEAD_DIM
    causal = lax.broadcasted_iota(jnp.int32, (length, length), 0) >= lax.broadcasted_iota(
        jnp.int32, (length, length), 1
    )

    def within(q, carry):
        span = pl.ds(pl.multiple_of(q * pair, pair), pair)
        value = values[:, span]
        g = lax.div(q * pair, group_width)
        sums = []
        for e in range(2):
            h = 2 * q + e
            lane = lax.broadcasted_iota(jnp.int32, (length, heads), 1)
            column = jnp.sum(jnp.where(lane == h, cum_ref[...], 0.0), axis=1, keepdims=True)
            gap = column - cum_t_ref[pl.ds(h, 1), :]
            kernel = jnp.where(causal, jnp.exp(jnp.where(causal, gap, 0.0)), 0.0)
            mixing = kernel * scores[g] * step_t_ref[pl.ds(h, 1), :]
            sums.append(
                jnp.dot(mixing.astype(jnp.bfloat16), value, preferred_element_type=jnp.float32)
            )
        first = lax.broadcasted_iota(jnp.int32, (length, pair), 1) < HEAD_DIM
        y[:, span] = jnp.where(first, sums[0], sums[1])
        return carry

    late = me >= n // 2

    def phase(turn, carry):
        @pl.when((turn == 0) == late)
        def _():
            lax.fori_loop(0, channels // pair, within, 0)

        @pl.when(turn == 0)
        def _():
            lax.fori_loop(0, tiles, link, 0)

        return carry

    lax.fori_loop(0, 2, phase, 0)

    for g in range(groups_here):
        per = group_width // tile

        def gated(c, squares):
            c = c + g * per
            start = pl.multiple_of(c * tile, tile)
            span = pl.ds(start, tile)
            carried = jnp.dot(
                c_maps[g], arrived[c], preferred_element_type=jnp.float32
            ) * spread(grown, start)
            total = y[:, span] + carried + skip_ref[:, span] * values[:, span].astype(jnp.float32)
            total = total * jax.nn.silu(gate_ref[:, span].astype(jnp.float32))
            y[:, span] = total
            return squares + jnp.sum(total * total, axis=1, keepdims=True)

        squares = lax.fori_loop(0, per, gated, jnp.zeros((length, 1), jnp.float32))
        scale = lax.rsqrt(squares / group_width + 1e-05)

        def scaled(c, carry):
            span = pl.ds(pl.multiple_of((c + g * per) * tile, tile), tile)
            if whole_groups:
                out_ref[:, span] = (y[:, span] * scale * gain_ref[:, span]).astype(out_ref.dtype)
            else:
                out_ref[:, span] = y[:, span]
            return carry

        lax.fori_loop(0, per, scaled, 0)

    @pl.when(has_right)
    def _():
        for which in range(2):
            rim_copy(which).wait_send()

        def sent(c, carry):
            chain_copy(c).wait_send()
            return carry

        lax.fori_loop(0, tiles, sent, 0)


def front(x, gate, maps, cum, step, skip, taps, base, map_taps, map_base, gain, whole_groups):
    n = lax.axis_size("seq")
    length, channels = x.shape
    heads = cum.shape[1]
    per_group = HEADS // GROUPS
    groups_here = max(1, heads // per_group)
    tile = max(128, channels // 8)
    tiles = channels // tile
    rim = 16
    bf16, f32 = jnp.bfloat16, jnp.float32
    dma = pltpu.SemaphoreType.DMA
    vmem = pl.BlockSpec(memory_space=pltpu.VMEM)
    decay = jnp.repeat(jnp.exp(cum[-1]), HEAD_DIM)[None]
    skips = jnp.repeat(skip, HEAD_DIM)[None]
    operands = (
        x, gate, maps, cum, cum.T, step, step.T, decay, skips,
        taps, base[None], map_taps, map_base[None], gain[None],
    )
    return pl.pallas_call(
        functools.partial(front_kernel, n, per_group, whole_groups),
        out_shape=jax.ShapeDtypeStruct((length, channels), bf16 if whole_groups else f32),
        in_specs=[vmem] * len(operands),
        out_specs=vmem,
        scratch_shapes=[
            pltpu.VMEM((rim, channels), bf16),
            pltpu.VMEM((rim, maps.shape[1]), bf16),
            pltpu.VMEM((rim + length, max(tile, STATE)), f32),
            pltpu.VMEM((length, channels), bf16),
            pltpu.VMEM((length, channels), f32),
            pltpu.VMEM((groups_here, length, STATE), bf16),
            pltpu.VMEM((groups_here, length, STATE), bf16),
            pltpu.VMEM((groups_here, length, length), f32),
            pltpu.VMEM((tiles, STATE, tile), f32),
            pltpu.VMEM((tiles, STATE, tile), bf16),
            pltpu.VMEM((tiles, STATE, tile), bf16),
            dma((2,)),
            dma((2,)),
            dma((tiles,)),
            dma((tiles,)),
        ],
        compiler_params=pltpu.CompilerParams(
            collective_id=1, has_side_effects=True, vmem_limit_bytes=48 << 20
        ),
    )(*operands)


LOG2E = 1.4426950408889634


def three(value):
    high = value.astype(jnp.bfloat16)
    rest = value - high.astype(jnp.float32)
    middle = rest.astype(jnp.bfloat16)
    low = (rest - middle.astype(jnp.float32)).astype(jnp.bfloat16)
    return high, middle, low


def layer_kernel(
    n, m, per_group, x_hbm, gate_hbm, maps_hbm, step_hbm, rate_hbm, skip_hbm, taps_hbm, base_hbm,
    map_taps_hbm, map_base_hbm, gain_hbm, w_hbm, out_ref,
    x_ref, gate_ref, maps_ref, step_ref, rate_ref, skip_ref, taps_ref, base_ref, map_taps_ref,
    map_base_ref, gain_ref, w_ref, in_sem,
    rim_x, rim_maps, pad, values, maps_conv, y, scores, local, state, arrived, leaving,
    gap_left, gap_right, turned_maps, ends, growth, own_end, all_ends, chosen, channel_rows, prefix_rows,
    gat, part, up, down,
    rim_send, rim_recv, end_send, end_recv, chain_send, chain_recv, forward_send,
    gat_send, gat_recv, up_send, up_recv, down_send, down_recv, out_send, out_recv,
    own_sem,
):
    mesh_ids = pl.DeviceIdType.MESH
    exact = lax.Precision.HIGHEST
    f32, bf16 = jnp.float32, jnp.bfloat16
    me, z = lax.axis_index("seq"), lax.axis_index("tp")
    chips = n // 2
    chip, core = lax.div(me, 2), lax.rem(me, 2)
    partner = me + 1 - 2 * core
    length, channels = x_ref.shape
    heads = step_ref.shape[0]
    levels = arrived.shape[0]
    groups_here = scores.shape[0]
    first_group = z * groups_here
    span_maps = groups_here * STATE
    tile = arrived.shape[3]
    tiles = channels // tile
    group_width = channels // groups_here
    rim = rim_x.shape[0]
    width = w_ref.shape[1]
    rows = length // m
    half = length // 2

    at_b = pl.ds(pl.multiple_of(first_group * STATE, STATE), span_maps)
    at_c = pl.ds(pl.multiple_of((GROUPS + first_group) * STATE, STATE), span_maps)
    to_b, to_c = pl.ds(0, span_maps), pl.ds(span_maps, span_maps)
    fetches = (
        (step_hbm, step_ref),
        (rate_hbm, rate_ref),
        (skip_hbm, skip_ref),
        (maps_hbm.at[:, at_b], maps_ref.at[:, to_b]),
        (maps_hbm.at[:, at_c], maps_ref.at[:, to_c]),
        (map_taps_hbm.at[:, at_b], map_taps_ref.at[:, to_b]),
        (map_taps_hbm.at[:, at_c], map_taps_ref.at[:, to_c]),
        (map_base_hbm.at[:, at_b], map_base_ref.at[:, to_b]),
        (map_base_hbm.at[:, at_c], map_base_ref.at[:, to_c]),
        (taps_hbm, taps_ref),
        (base_hbm, base_ref),
        (x_hbm, x_ref),
        (gate_hbm, gate_ref),
        (gain_hbm, gain_ref),
        (w_hbm, w_ref),
    )
    loads = [
        pltpu.make_async_copy(source, target, in_sem.at[i])
        for i, (source, target) in enumerate(fetches)
    ]

    barrier = pltpu.get_barrier_semaphore()

    def greet(step, carry):
        pl.semaphore_signal(
            barrier, inc=1, device_id=(lax.rem(me + step, n), z), device_id_type=mesh_ids
        )
        return carry

    lax.fori_loop(1, n, greet, 0)

    @pl.when(z > 0)
    def _():
        pl.semaphore_signal(barrier, inc=1, device_id=(me, z - 1), device_id_type=mesh_ids)

    @pl.when(z < m - 1)
    def _():
        pl.semaphore_signal(barrier, inc=1, device_id=(me, z + 1), device_id_type=mesh_ids)

    for load in loads[:12]:
        load.start()

    has_left, has_right = me > 0, me < n - 1
    odd = core == 1

    for load in loads[:3]:
        load.wait()

    def turned(value):
        size = value.shape[0]
        same = lax.broadcasted_iota(jnp.int32, (size, size), 0) == lax.broadcasted_iota(
            jnp.int32, (size, size), 1
        )
        return lax.dot_general(
            value, same.astype(f32), (((0,), (0,)), ((), ())), precision=exact,
            preferred_element_type=f32,
        )

    step = jax.nn.softplus(turned(step_ref[...]))
    log_decay = -jnp.exp(rate_ref[...]) * step
    row = lax.broadcasted_iota(jnp.int32, (length, length), 0)
    column = lax.broadcasted_iota(jnp.int32, (length, length), 1)
    lower = (row >= column).astype(f32)
    cum = jnp.dot(lower, log_decay, precision=exact, preferred_element_type=f32)
    final = cum[length - 1 : length]
    ones = jnp.ones((length, heads), bf16)
    blank = jnp.zeros((length, heads), bf16)
    gap_left[...] = jnp.concatenate(
        [*three(cum * LOG2E), ones, ones, ones, blank, blank], axis=1
    )
    source_log = jnp.log(step) * LOG2E - cum * LOG2E
    source_rows = turned(source_log)
    unit = jnp.ones((heads, length), bf16)
    gap_right[...] = jnp.concatenate(
        [unit, unit, unit, *three(source_rows), unit, unit], axis=0
    )
    ends[...] = jnp.concatenate([*three(jnp.exp(final - cum) * step), blank], axis=1)
    growth[...] = jnp.concatenate([*three(jnp.exp(cum)), blank], axis=1)
    lanes = own_end.shape[1]
    own_end[...] = jnp.zeros_like(own_end)
    own_end[:, 0:heads] = jnp.broadcast_to(final, (8, heads))
    all_ends[me] = jnp.zeros((8, lanes), f32)

    beside = (z > 0).astype(jnp.int32) + (z < m - 1).astype(jnp.int32)
    pl.semaphore_wait(barrier, n - 1 + beside)

    last_rows = pl.ds(length - rim, rim)

    def rim_copy(which):
        source, target = (
            (x_hbm.at[last_rows], rim_x),
            (maps_hbm.at[last_rows, at_b], rim_maps.at[:, to_b]),
            (maps_hbm.at[last_rows, at_c], rim_maps.at[:, to_c]),
        )[which]
        return pltpu.make_async_remote_copy(
            src_ref=source,
            dst_ref=target,
            send_sem=rim_send.at[which],
            recv_sem=rim_recv.at[which],
            device_id=(me + 1, z),
            device_id_type=mesh_ids,
        )

    @pl.when(has_right)
    def _():
        for which in range(3):
            rim_copy(which).start()

    def end_copy(offset, sender):
        return pltpu.make_async_remote_copy(
            src_ref=own_end,
            dst_ref=all_ends.at[sender],
            send_sem=end_send.at[offset],
            recv_sem=end_recv.at[sender],
            device_id=(lax.rem(me + offset, n), z),
            device_id_type=mesh_ids,
        )

    def send_end(offset, carry):
        end_copy(offset, me).start()
        return carry

    lax.fori_loop(1, n, send_end, 0)

    first_row = lax.broadcasted_iota(jnp.int32, (16, heads), 0) < 8
    two = jnp.where(first_row, jnp.exp(final), skip_ref[...])
    two = jnp.concatenate([*three(two), jnp.zeros((16, heads), bf16)], axis=1)

    def choose(c, carry):
        start = pl.multiple_of(c * tile, tile)
        slot = lax.broadcasted_iota(jnp.int32, (4 * heads, tile), 0)
        head = lax.rem(slot, heads) * HEAD_DIM
        lane = lax.broadcasted_iota(jnp.int32, (4 * heads, tile), 1) + start
        chosen[:, pl.ds(start, tile)] = (
            ((lane >= head) & (lane < head + HEAD_DIM)).astype(f32).astype(bf16)
        )
        return carry

    lax.fori_loop(0, tiles, choose, 0)

    def spread(per_head, span):
        return jnp.dot(per_head, chosen[:, span], preferred_element_type=f32)

    channel_rows[...] = spread(two, slice(None))
    for load in loads[3:9]:
        load.wait()

    def smooth(rows_ref, taps, base, out, start, size):
        span = pl.ds(start, size)
        pad[:, 0:size] = rows_ref[:, span].astype(f32)
        total = base[:, span]
        for k in range(CONV):
            at = rim - (CONV - 1) + k
            total = total + taps[k : k + 1, span] * pad[at : at + length - rim, 0:size]
        out[rim:length, span] = jax.nn.silu(total).astype(bf16)

    for c in range(0, 2 * span_maps, tile):
        smooth(maps_ref, map_taps_ref, map_base_ref, maps_conv, c, tile)

    for load in loads[9:12]:
        load.wait()
    for load in loads[12:]:
        load.start()

    def smooth_rim(rows_ref, rim_ref, taps, base, out, start, size):
        span = pl.ds(start, size)
        pad[0:rim, 0:size] = rim_ref[:, span].astype(f32)
        pad[rim : 2 * rim, 0:size] = rows_ref[0:rim, span].astype(f32)
        total = base[:, span]
        for k in range(CONV):
            at = rim - (CONV - 1) + k
            total = total + taps[k : k + 1, span] * pad[at : at + rim, 0:size]
        out[0:rim, span] = jax.nn.silu(total).astype(bf16)

    def smooth_tile(c, carry):
        smooth(x_ref, taps_ref, base_ref, values, pl.multiple_of(c * tile, tile), tile)
        return carry

    lax.fori_loop(0, tiles, smooth_tile, 0)

    def chain_send_copy(level, hop, c):
        return pltpu.make_async_remote_copy(
            src_ref=leaving.at[c],
            dst_ref=arrived.at[level, c],
            send_sem=chain_send.at[hop, c],
            recv_sem=chain_recv.at[level, c],
            device_id=(me + 1 if level == 0 else me + 2 * (hop + 1), z),
            device_id_type=mesh_ids,
        )

    def chain_forward(level, c):
        return pltpu.make_async_remote_copy(
            src_ref=arrived.at[level, c],
            dst_ref=arrived.at[level, c],
            send_sem=forward_send.at[level, c],
            recv_sem=chain_recv.at[level, c],
            device_id=(partner, z),
            device_id_type=mesh_ids,
        )

    def hops(level):
        return range(max(1, 2**level // 2))

    def sends(level):
        return lax.rem(me, 2 ** (level + 1)) == 2**level - 1

    def gets(level):
        return lax.rem(lax.div(me, 2**level), 2) == 1

    per = group_width // tile

    maps_conv[0:rim] = jnp.zeros((rim, 2 * span_maps), bf16)
    values[0:rim] = jnp.zeros((rim, channels), bf16)

    for g in range(groups_here):
        turned_maps[g] = turned(
            maps_conv[:, g * STATE : (g + 1) * STATE].astype(f32)
        ).astype(bf16)

    for g in range(groups_here):
        mine = range(g * per, (g + 1) * per)
        spans = [slice(c * tile, (c + 1) * tile) for c in mine]
        weighted = [
            (values[:, span].astype(f32) * spread(ends[...], span)).astype(bf16)
            for span in spans
        ]
        for c, w in zip(mine, weighted):
            local[c] = jnp.dot(turned_maps[g], w, preferred_element_type=f32)

    @pl.when(has_left)
    def _():
        for which in range(3):
            rim_copy(which).wait_recv()

    @pl.when(jnp.logical_not(has_left))
    def _():
        rim_x[...] = jnp.zeros_like(rim_x)
        rim_maps[...] = jnp.zeros_like(rim_maps)

    for c in range(0, 2 * span_maps, tile):
        smooth_rim(maps_ref, rim_maps, map_taps_ref, map_base_ref, maps_conv, c, tile)
    for c in range(0, channels, tile):
        smooth_rim(x_ref, rim_x, taps_ref, base_ref, values, c, tile)

    for g in range(groups_here):
        mine = range(g * per, (g + 1) * per)
        spans = [slice(c * tile, (c + 1) * tile) for c in mine]
        first_maps = maps_conv[0:rim, g * STATE : (g + 1) * STATE]
        weighted = [
            (values[0:rim, span].astype(f32) * spread(ends[0:rim], span)).astype(bf16)
            for span in spans
        ]
        for c, w in zip(mine, weighted):
            total = local[c] + lax.dot_general(
                first_maps, w, (((0,), (0,)), ((), ())), preferred_element_type=f32
            )
            local[c] = total
            state[c] = jnp.zeros_like(total)
            leaving[c] = total.astype(bf16)

        @pl.when(sends(0))
        def _():
            for c in mine:
                chain_send_copy(0, 0, c).start()

    def link(level, c):
        span = pl.ds(pl.multiple_of(c * tile, tile), tile)

        @pl.when(gets(level))
        def _():
            chain_forward(level, c).wait_recv()
            if level == 0:
                state[c] = arrived[level, c].astype(f32)
            else:
                @pl.when(odd)
                def _():
                    chain_forward(level, c).start()

                state[c] = state[c] + prefix_rows[level, 0:1, span] * arrived[level, c].astype(f32)

        if level + 1 < levels:
            @pl.when(sends(level + 1))
            def _():
                leaving[c] = (channel_rows[0:1, span] * state[c] + local[c]).astype(bf16)
                for hop in hops(level + 1):
                    chain_send_copy(level + 1, hop, c).start()

    def link_all(level, first, last):
        def body(c, carry):
            link(level, c)
            return carry

        lax.fori_loop(first, last, body, 0)

    link_all(0, 0, tiles)

    for g in range(groups_here):
        scores[g] = lax.dot_general(
            maps_conv[:, span_maps + g * STATE : span_maps + (g + 1) * STATE],
            maps_conv[:, g * STATE : (g + 1) * STATE],
            (((1,), (1,)), ((), ())),
            preferred_element_type=f32,
        )

    def get_end(offset, carry):
        end_copy(offset, lax.rem(me + offset, n)).wait_recv()
        return carry

    lax.fori_loop(1, n, get_end, 0)

    for level in range(1, levels):
        base = me - lax.rem(me, 2**level)
        total = jnp.zeros((8, lanes), f32)
        for i in range(n):
            total = total + jnp.where((base <= i) & (i < me), all_ends[i], 0.0)
        passed = jnp.exp(total[:, 0:heads])
        passed = jnp.concatenate([passed, passed], axis=0)
        passed = jnp.concatenate([*three(passed), jnp.zeros((16, heads), bf16)], axis=1)

        prefix_rows[level] = spread(passed, slice(None))

    pair = 2 * HEAD_DIM
    lane = lax.broadcasted_iota(jnp.int32, (half, pair), 1)
    batch = 4

    def mask_of(head):
        slot = lax.broadcasted_iota(jnp.int32, (1, 8 * heads), 1)
        return ((lax.rem(slot, heads) == head) & (slot < 6 * heads)).astype(f32).astype(bf16)

    def within(turn, carry):
        g = lax.div(turn * batch * pair, group_width)
        gaps = []
        for e in range(2 * batch):
            left = gap_left[...] * mask_of(2 * batch * turn + e)
            gaps.append((
                jnp.dot(left[0:half], gap_right[:, 0:half], preferred_element_type=f32),
                jnp.dot(left[half:length], gap_right[...], preferred_element_type=f32),
            ))
        causal = lax.broadcasted_iota(jnp.int32, (half, half), 0) >= lax.broadcasted_iota(
            jnp.int32, (half, half), 1
        )
        causal_late = lax.broadcasted_iota(jnp.int32, (half, length), 0) + half >= (
            lax.broadcasted_iota(jnp.int32, (half, length), 1)
        )
        mixing = [
            (
                (jnp.where(causal, jnp.exp2(a), 0.0) * scores[g, 0:half, 0:half]).astype(bf16),
                (jnp.where(causal_late, jnp.exp2(b), 0.0) * scores[g, half:length]).astype(bf16),
            )
            for a, b in gaps
        ]
        for q in range(batch):
            span = pl.ds(pl.multiple_of((turn * batch + q) * pair, pair), pair)
            early, late = [], []
            for a, b in mixing[2 * q : 2 * q + 2]:
                early.append(jnp.dot(a, values[0:half, span], preferred_element_type=f32))
                late.append(jnp.dot(b, values[:, span], preferred_element_type=f32))
            y[0:half, span] = jnp.where(lane < HEAD_DIM, early[0], early[1])
            y[half:length, span] = jnp.where(lane < HEAD_DIM, late[0], late[1])
        return carry

    batches = channels // (pair * batch)
    share = tiles // batches

    def within_level(turn, carry):
        for c in range(share):
            if levels > 2:
                link(1, turn * share + c)
        return within(turn, carry)

    lax.fori_loop(0, batches, within_level, 0)

    for level in range(2, levels - 1):
        link_all(level, 0, tiles)

    for load in loads[12:14]:
        load.wait()

    def partner_copy(slot, g):
        return pltpu.make_async_remote_copy(
            src_ref=gat.at[slot - 1, g],
            dst_ref=gat.at[slot, g],
            send_sem=gat_send.at[slot, g],
            recv_sem=gat_recv.at[slot, g],
            device_id=(partner, z),
            device_id_type=mesh_ids,
        )

    def source_mask(i, who):
        swap = (who == 1) & (chips >= 4)
        return i + jnp.where(swap & (i == 1), 1, 0) - jnp.where(swap & (i == 2), 1, 0)

    def chip_at(mask):
        there, bit = chip, 1
        while bit < chips:
            on = lax.rem(lax.div(mask, bit), 2)
            there = there + on * (bit - 2 * bit * lax.rem(lax.div(chip, bit), 2))
            bit *= 2
        return there

    def across_copy(i, g):
        return pltpu.make_async_remote_copy(
            src_ref=gat.at[0, g],
            dst_ref=gat.at[2 * i, g],
            send_sem=gat_send.at[2 * i, g],
            recv_sem=gat_recv.at[2 * i, g],
            device_id=(2 * chip_at(source_mask(i, core)) + core, z),
            device_id_type=mesh_ids,
        )

    relayed = chips == 4

    def relay_copy(slot, g):
        mask = source_mask(lax.div(slot, 2), core)
        return pltpu.make_async_remote_copy(
            src_ref=gat.at[slot, g],
            dst_ref=gat.at[6, g],
            send_sem=gat_send.at[6, g],
            recv_sem=gat_recv.at[6, g],
            device_id=(2 * chip_at(3 - mask) + core, z),
            device_id_type=mesh_ids,
        )

    def arrival(slot, g):
        return pltpu.make_async_remote_copy(
            src_ref=gat.at[slot, g],
            dst_ref=gat.at[slot, g],
            send_sem=gat_send.at[slot, g],
            recv_sem=gat_recv.at[slot, g],
            device_id=(partner, z),
            device_id_type=mesh_ids,
        )

    for g in range(groups_here):
        mine = range(g * per, (g + 1) * per)
        spans = [slice(c * tile, (c + 1) * tile) for c in mine]
        output_map = maps_conv[:, span_maps + g * STATE : span_maps + (g + 1) * STATE]
        squares = jnp.zeros((length, 128), f32)
        for first in range(0, per, 2):
            link_all(levels - 1, g * per + first, g * per + first + 2)
            carried = [
                jnp.dot(output_map, state[c].astype(bf16), preferred_element_type=f32)
                for c in mine[first : first + 2]
            ]
            grown = [spread(growth[...], span) for span in spans[first : first + 2]]
            for span, more, scale in zip(spans[first : first + 2], carried, grown):
                total = y[:, span] + more * scale
                total = total + channel_rows[8:9, span] * values[:, span].astype(f32)
                total = total * jax.nn.silu(gate_ref[:, span].astype(f32))
                y[:, span] = total
                for d in range(0, tile, 128):
                    squares = squares + total[:, d : d + 128] * total[:, d : d + 128]
        scale = lax.rsqrt(jnp.sum(squares, axis=1, keepdims=True) / group_width + 1e-05)
        for c, span in enumerate(spans):
            gat[0, g, :, c * tile : (c + 1) * tile] = (
                y[:, span] * scale * gain_ref[:, span]
            ).astype(bf16)
        partner_copy(1, g).start()
        if chips > 1:
            across_copy(1, g).start()

    def chain_z(step, j, buffer, send, recv, to):
        return pltpu.make_async_remote_copy(
            src_ref=part.at[step, pl.ds(j * rows, rows)],
            dst_ref=buffer.at[step, pl.ds(j * rows, rows)],
            send_sem=send.at[step, j],
            recv_sem=recv.at[step, j],
            device_id=(me, to),
            device_id_type=mesh_ids,
        )

    def slot_of(step):
        return jnp.where(step == n - 1, n - 3, jnp.where(step >= n - 3, step + 1, step))

    def owner(step):
        slot = slot_of(step)
        who = core + lax.rem(slot, 2) * (1 - 2 * core)
        return 2 * chip_at(source_mask(lax.div(slot, 2), who)) + who

    def columns(sender):
        return pl.ds(pl.multiple_of(sender * width, width), width)

    def own_rows():
        return pl.ds(pl.multiple_of(z * rows, rows), rows)

    def out_copy(step, sender):
        return pltpu.make_async_remote_copy(
            src_ref=part.at[step, own_rows()],
            dst_ref=out_ref.at[:, columns(sender)],
            send_sem=out_send.at[step],
            recv_sem=out_recv.at[sender],
            device_id=(owner(step), z),
            device_id_type=mesh_ids,
        )

    pieces = 2 if rows % 32 == 0 else 1
    size = rows // pieces

    def piece_z(j, h, buffer, send, recv, to):
        span = pl.ds(j * rows + h * size, size)
        return pltpu.make_async_remote_copy(
            src_ref=part.at[n - 1, span],
            dst_ref=buffer.at[n - 1, span],
            send_sem=send.at[n - 1 + h, j],
            recv_sem=recv.at[n - 1 + h, j],
            device_id=(me, to),
            device_id_type=mesh_ids,
        )

    def piece_out(h, sender):
        mine = pl.ds(pl.multiple_of(z * rows + h * size, size), size)
        return pltpu.make_async_remote_copy(
            src_ref=part.at[n - 1, mine],
            dst_ref=out_ref.at[pl.ds(h * size, size), columns(sender)],
            send_sem=out_send.at[n - 1 + h],
            recv_sem=out_recv.at[sender if h == 0 else n],
            device_id=(owner(n - 1), z),
            device_id_type=mesh_ids,
        )

    def own_copy():
        return pltpu.make_async_copy(part.at[0, own_rows()], out_ref.at[:, columns(me)], own_sem)

    def added(step, j, buffer):
        span = pl.ds(j * rows, rows)
        part[step, span] = (
            part[step, span].astype(f32) + buffer[step, span].astype(f32)
        ).astype(bf16)

    up_lag, down_lag = z, m - 1 - z
    held = min(2, n - 1)
    kept = (1, 0) if n - 1 - held >= 2 else ()
    last_lag = m - 1 + max(held - 2, 0) + len(kept)
    wide = min(width, 256)

    loads[14].wait()

    def last_step(place):
        if not kept:
            return place
        skipped = place
        for early in sorted(kept):
            skipped = skipped + (skipped >= early).astype(jnp.int32)
        for i, early in enumerate(kept):
            skipped = jnp.where(place == n - len(kept) + i, early, skipped)
        return jnp.where((place < 0) | (place >= n), -1, skipped)

    def turn(tau, carry):
        @pl.when(tau < n)
        def _():
            slot = slot_of(tau)
            direct = (slot > 0) & (lax.rem(slot, 2) == 0)

            @pl.when(direct)
            def _():
                for g in range(groups_here):
                    arrival(slot, g).wait_send()

            @pl.when(direct & (slot < (4 if relayed else n - 2)))
            def _():
                for g in range(groups_here):
                    across_copy(lax.div(slot, 2) + 1, g).start()

            @pl.when(tau > 0)
            def _():
                for g in range(groups_here):
                    arrival(slot, g).wait_recv()

            @pl.when(direct)
            def _():
                for g in range(groups_here):
                    partner_copy(slot + 1, g).start()

            if relayed:
                @pl.when((slot == 3) | (slot == 4))
                def _():
                    source = jnp.where(slot == 3, 2, 4)
                    along = source_mask(lax.div(source, 2), core) == 1
                    for g in range(groups_here):
                        @pl.when(along == (g < (groups_here + 1) // 2))
                        def _():
                            relay_copy(source, g).start()

            for c in range(0, width, wide):
                total = jnp.zeros((length, wide), f32)
                for g in range(groups_here):
                    total = total + jnp.dot(
                        gat[slot, g],
                        w_ref[g * group_width : (g + 1) * group_width, c : c + wide],
                        preferred_element_type=f32,
                    )
                part[tau, :, c : c + wide] = total.astype(bf16)

        t_up = tau - up_lag

        @pl.when((t_up >= 0) & (t_up < n))
        def _():
            for j in range(m - 1, 0, -1):
                @pl.when(z < j)
                def _():
                    copy = chain_z(t_up, j, up, up_send, up_recv, z + 1)

                    @pl.when(z > 0)
                    def _():
                        copy.wait_recv()
                        added(t_up, j, up)

                    if j == 1:
                        @pl.when(t_up == n - 1)
                        def _():
                            for before in range(held, 0, -1):
                                chain_z(n - 1 - before, j, up, up_send, up_recv, z + 1).start()
                            for h in range(pieces):
                                piece_z(j, h, up, up_send, up_recv, z + 1).start()
                            for early in kept:
                                chain_z(early, j, up, up_send, up_recv, z + 1).start()

                        now = t_up < n - 1 - held
                        for early in kept:
                            now = now & (t_up != early)

                        @pl.when(now)
                        def _():
                            copy.start()
                    else:
                        copy.start()

        t_down = tau - down_lag

        @pl.when((t_down >= 0) & (t_down < n))
        def _():
            for j in range(m - 1):
                @pl.when(z > j)
                def _():
                    copy = chain_z(t_down, j, down, down_send, down_recv, z - 1)

                    @pl.when(z < m - 1)
                    def _():
                        copy.wait_recv()
                        added(t_down, j, down)

                    if j == m - 2:
                        @pl.when(t_down == n - 1)
                        def _():
                            for before in range(held, 0, -1):
                                chain_z(n - 1 - before, j, down, down_send, down_recv, z - 1).start()
                            for h in range(pieces):
                                piece_z(j, h, down, down_send, down_recv, z - 1).start()
                            for early in kept:
                                chain_z(early, j, down, down_send, down_recv, z - 1).start()

                        now = t_down < n - 1 - held
                        for early in kept:
                            now = now & (t_down != early)

                        @pl.when(now)
                        def _():
                            copy.start()
                    else:
                        copy.start()

        t_last = last_step(tau - last_lag)

        @pl.when((t_last >= 0) & (t_last < n - 1))
        def _():
            for j in range(m):
                @pl.when(z == j)
                def _():
                    span = pl.ds(j * rows, rows)
                    total = part[t_last, span].astype(f32)
                    if j > 0:
                        chain_z(t_last, j, up, up_send, up_recv, z).wait_recv()
                        total = total + up[t_last, span].astype(f32)
                    if j < m - 1:
                        chain_z(t_last, j, down, down_send, down_recv, z).wait_recv()
                        total = total + down[t_last, span].astype(f32)
                    part[t_last, span] = total.astype(bf16)

            @pl.when(t_last == 0)
            def _():
                own_copy().start()

            @pl.when(t_last > 0)
            def _():
                out_copy(t_last, me).start()

        @pl.when(t_last == n - 1)
        def _():
            for j in range(m):
                @pl.when(z == j)
                def _():
                    for h in range(pieces):
                        span = pl.ds(j * rows + h * size, size)
                        total = part[n - 1, span].astype(f32)
                        if j > 0:
                            if j == 1:
                                piece_z(j, h, up, up_send, up_recv, z).wait_recv()
                            elif h == 0:
                                chain_z(n - 1, j, up, up_send, up_recv, z).wait_recv()
                            total = total + up[n - 1, span].astype(f32)
                        if j < m - 1:
                            if j == m - 2:
                                piece_z(j, h, down, down_send, down_recv, z).wait_recv()
                            elif h == 0:
                                chain_z(n - 1, j, down, down_send, down_recv, z).wait_recv()
                            total = total + down[n - 1, span].astype(f32)
                        part[n - 1, span] = total.astype(bf16)
                        piece_out(h, me).start()

        return carry

    lax.fori_loop(0, n + last_lag, turn, 0)

    def finish(step, carry):
        @pl.when(lax.rem(step, 2) == 1)
        def _():
            for g in range(groups_here):
                arrival(step, g).wait_send()

        @pl.when(step > 0)
        def _():
            end_copy(step, me).wait_send()

        for j in range(m):
            @pl.when((z < j) & ((step < n - 1) | (j != 1)))
            def _():
                chain_z(step, j, up, up_send, up_recv, z).wait_send()

            @pl.when((z > j) & ((step < n - 1) | (j != m - 2)))
            def _():
                chain_z(step, j, down, down_send, down_recv, z).wait_send()

        @pl.when((step > 0) & (step < n - 1))
        def _():
            out_copy(step, me).wait_send()

        sender = lax.rem(me + step, n)

        @pl.when((step > 0) & (sender != ending))
        def _():
            out_copy(step, sender).wait_recv()

        return carry

    ending_slot = slot_of(n - 1)
    ending = 2 * chip_at(source_mask(lax.div(ending_slot, 2), core)) + core
    ending = ending + lax.rem(ending_slot, 2) * (1 - 2 * core)
    lax.fori_loop(0, n, finish, 0)
    for h in range(pieces):
        @pl.when(z == 0)
        def _():
            piece_z(1, h, up, up_send, up_recv, z).wait_send()

        @pl.when(z == m - 1)
        def _():
            piece_z(m - 2, h, down, down_send, down_recv, z).wait_send()

        piece_out(h, me).wait_send()
        piece_out(h, ending).wait_recv()
    own_copy().wait()

    @pl.when(has_right)
    def _():
        for which in range(3):
            rim_copy(which).wait_send()

    def sent(c, carry):
        for level in range(levels):
            @pl.when(sends(level))
            def _():
                for hop in hops(level):
                    chain_send_copy(level, hop, c).wait_send()

            if level > 0:
                @pl.when(gets(level) & odd)
                def _():
                    chain_forward(level, c).wait_send()

        return carry

    lax.fori_loop(0, tiles, sent, 0)


def layer(x, gate, maps, step_raw, rate, skip, taps, base, map_taps, map_base, gain, weight):
    n, m = lax.axis_size("seq"), lax.axis_size("tp")
    length, channels = x.shape
    heads = rate.shape[0]
    per_group = HEADS // GROUPS
    groups_here = heads // per_group
    tile = max(128, channels // 8)
    tiles = channels // tile
    width = weight.shape[1]
    span_maps = 2 * groups_here * STATE
    rim = 16
    levels = n.bit_length() - 1
    lanes = -(-heads // 128) * 128
    bf16, f32 = jnp.bfloat16, jnp.float32
    dma = pltpu.SemaphoreType.DMA
    operands = (
        x, gate, maps, step_raw.T, rate[None], skip[None], taps, base[None],
        map_taps, map_base[None], gain[None], weight,
    )
    blocks = pltpu.VMEM((n, length, width), bf16)
    return pl.pallas_call(
        functools.partial(layer_kernel, n, m, per_group),
        out_shape=jax.ShapeDtypeStruct((length // m, n * width), bf16),
        in_specs=[pl.BlockSpec(memory_space=pl.ANY)] * len(operands),
        out_specs=pl.BlockSpec(memory_space=pl.ANY),
        scratch_shapes=[
            pltpu.VMEM((length, channels), bf16),
            pltpu.VMEM((length, channels), bf16),
            pltpu.VMEM((length, span_maps), bf16),
            pltpu.VMEM((heads, length), f32),
            pltpu.VMEM((1, heads), f32),
            pltpu.VMEM((1, heads), f32),
            pltpu.VMEM((CONV, channels), f32),
            pltpu.VMEM((1, channels), f32),
            pltpu.VMEM((CONV, span_maps), f32),
            pltpu.VMEM((1, span_maps), f32),
            pltpu.VMEM((1, channels), f32),
            pltpu.VMEM(weight.shape, bf16),
            dma((15,)),
            pltpu.VMEM((rim, channels), bf16),
            pltpu.VMEM((rim, span_maps), bf16),
            pltpu.VMEM((length, max(tile, STATE)), f32),
            pltpu.VMEM((length, channels), bf16),
            pltpu.VMEM((length, span_maps), bf16),
            pltpu.VMEM((length, channels), f32),
            pltpu.VMEM((groups_here, length, length), f32),
            pltpu.VMEM((tiles, STATE, tile), f32),
            pltpu.VMEM((tiles, STATE, tile), f32),
            pltpu.VMEM((levels, tiles, STATE, tile), bf16),
            pltpu.VMEM((tiles, STATE, tile), bf16),
            pltpu.VMEM((length, 8 * heads), bf16),
            pltpu.VMEM((8 * heads, length), bf16),
            pltpu.VMEM((groups_here, STATE, length), bf16),
            pltpu.VMEM((length, 4 * heads), bf16),
            pltpu.VMEM((length, 4 * heads), bf16),
            pltpu.VMEM((8, lanes), f32),
            pltpu.VMEM((n, 8, lanes), f32),
            pltpu.VMEM((4 * heads, channels), bf16),
            pltpu.VMEM((16, channels), f32),
            pltpu.VMEM((levels, 16, channels), f32),
            pltpu.VMEM((n, groups_here, length, channels // groups_here), bf16),
            blocks,
            blocks,
            blocks,
            dma((3,)),
            dma((3,)),
            dma((n,)),
            dma((n,)),
            dma((max(1, n // 4), tiles)),
            dma((levels, tiles)),
            dma((levels, tiles)),
            dma((n, groups_here)),
            dma((n, groups_here)),
            dma((n + 1, m)),
            dma((n + 1, m)),
            dma((n + 1, m)),
            dma((n + 1, m)),
            dma((n + 1,)),
            dma((n + 1,)),
            dma(()),
        ],
        compiler_params=pltpu.CompilerParams(
            collective_id=2, has_side_effects=True, vmem_limit_bytes=60 << 20
        ),
        cost_estimate=pl.CostEstimate(
            flops=2 * n * length * channels * width,
            bytes_accessed=2 * (channels * width + 3 * length * channels),
            transcendentals=0,
        ),
    )(*operands)


def shards(
    conv_values,
    gate_values,
    conv_maps,
    step_raw,
    decay_log,
    skip_gain,
    values_kernel,
    values_offset,
    maps_kernel,
    maps_offset,
    norm_weight,
    out_weight,
    residual,
):
    length = conv_values.shape[0]
    heads_dev = decay_log.shape[0]
    per_group = HEADS // GROUPS
    whole_groups = heads_dev % per_group == 0
    chips = lax.axis_size("seq") // 2
    paired = lax.axis_size("seq") == 2 * chips and chips & (chips - 1) == 0
    if whole_groups and paired and heads_dev % 32 == 0:
        summed = layer(
            conv_values, gate_values, conv_maps, step_raw, decay_log, skip_gain, values_kernel,
            values_offset, maps_kernel, maps_offset, norm_weight, out_weight,
        )
        return residual.astype(jnp.float32) + summed.astype(jnp.float32)
    step_size = jax.nn.softplus(step_raw)
    place = jnp.arange(length, dtype=jnp.int32)
    cum_log = jnp.dot(
        (place[:, None] >= place[None, :]).astype(jnp.float32),
        -jnp.exp(decay_log)[None, :] * step_size,
        precision=lax.Precision.HIGHEST,
    )
    normed = front(
        conv_values, gate_values, conv_maps, cum_log, step_size, skip_gain, values_kernel,
        values_offset, maps_kernel, maps_offset, norm_weight, whole_groups,
    )
    if not whole_groups:
        gated_out = normed.reshape(length, heads_dev, HEAD_DIM)
        head_squares = jnp.sum(gated_out * gated_out, axis=2)
        all_heads = lax.all_gather(head_squares, "tp", axis=1, tiled=True)
        group_totals = jnp.sum(all_heads.reshape(length, GROUPS, per_group), axis=2)
        heads_here = lax.axis_index("tp") * heads_dev + jnp.arange(heads_dev, dtype=jnp.int32)
        inv_rms = lax.rsqrt(
            group_totals[:, heads_here // per_group] / (per_group * HEAD_DIM) + 1e-05
        )
        normed = (
            (gated_out * inv_rms[:, :, None]).reshape(length, heads_dev * HEAD_DIM)
            * norm_weight[None, :]
        ).astype(jnp.bfloat16)
    blocks = mix(normed, out_weight)
    summed = jnp.transpose(blocks, (1, 0, 2)).reshape(residual.shape).astype(jnp.float32)
    return residual.astype(jnp.float32) + summed


def solution(mesh):
    placed = (
        P("seq", "tp"),
        P("seq", "tp"),
        P("seq", None),
        P("seq", "tp"),
        P("tp"),
        P("tp"),
        P(None, "tp"),
        P("tp"),
        P(),
        P(),
        P("tp"),
        P("tp", "seq"),
        P(("seq", "tp"), None),
    )
    return jax.shard_map(
        shards, mesh=mesh, in_specs=placed, out_specs=P(("seq", "tp"), None), check_vma=False
    )
```
